32 devices in a mesh: dp: 8 (over y, x, core), tensor: 4 (over z).
Axes of the slice: x: 2, y: 2, z: 4, core: 2. Of those that a mesh axis runs over, the one named last changes fastest.
Arguments:
- image_rows: bfloat16 [8, 1024, 1536], P('dp', 'tensor'), may hold values from -6 to 6
- text_rows: bfloat16 [8, 160, 1536], P('dp', 'tensor'), may hold values from -6 to 6
- conditioning: bfloat16 [8, 1536], P('dp'), may hold values from -6 to 6
- modulator: bfloat16 [1, 2, 1536, 6, 1536], P(None, None, 'dp', None, 'tensor'), may hold values from -0.15625 to 0.15625
- attention_in: bfloat16 [1, 2, 1536, 3, 1536], P(None, None, 'dp', None, 'tensor'), may hold values from -0.15625 to 0.15625
- attention_out: bfloat16 [1, 2, 1536, 1536], P(None, None, ('tensor', 'dp')), may hold values from -1 to 1
- up_weight: bfloat16 [1, 2, 1536, 6144], P(None, None, 'dp', 'tensor'), may hold values from -0.15625 to 0.15625
- down_weight: bfloat16 [1, 2, 6144, 1536], P(None, None, ('tensor', 'dp')), may hold values from -0.078125 to 0.078125
- image_cotangent: bfloat16 [8, 1024, 1536], P('dp', 'tensor'), may hold values from -6 to 6
- text_cotangent: bfloat16 [8, 160, 1536], P('dp', 'tensor'), may hold values from -6 to 6
Outputs:
- image_out: bfloat16 [8, 1024, 1536], P('dp', 'tensor')
- text_out: bfloat16 [8, 160, 1536], P('dp', 'tensor')
- image_grad: float32 [8, 1024, 1536], P('dp', 'tensor')
- text_grad: float32 [8, 160, 1536], P('dp', 'tensor')
- conditioning_grad: float32 [8, 1536], P('dp', 'tensor')
- modulator_grad: float32 [1, 2, 1536, 6, 1536], P(None, None, 'dp', None, 'tensor')
- attention_in_grad: float32 [1, 2, 1536, 3, 1536], P(None, None, 'dp', None, 'tensor')
- attention_out_grad: float32 [1, 2, 1536, 1536], P(None, None, ('tensor', 'dp'))
- up_grad: float32 [1, 2, 1536, 6144], P(None, None, 'dp', 'tensor')
- down_grad: float32 [1, 2, 6144, 1536], P(None, None, ('tensor', 'dp'))
The draws below stay inside these ranges and needn't reach their ends.
All inputs are finite; a program needn't handle non-finite values.
Results may differ from the reference program's by a relative error of at most 0.014.
The reference program's roundings to bfloat16 on the way count: a program that leaves them out, or rounds other values in their place, can miss the bound.
Values may be sent and summed in bfloat16 or wider, within the bound.
No kernel may reach another device: no remote copies, remote signals or barrier semaphores. Data moves between devices by JAX's collectives and lax.ppermute only.
A program may use at most 256 MiB of HBM per device.

```python
import jax
import jax.numpy as jnp
from jax import lax

D = 1536
HEADS = 24
HD = 64
FF = 6144
IMG = 1024
TXT = 160
LAYERS = 1
SEQS = 8


def block_levels(own_key, extent, cuts, low, top_value):
    level = 1.0
    for position, shards_of in cuts:
        heights = jax.random.uniform(jax.random.fold_in(jax.random.fold_in(own_key, 6), position), (shards_of,), jnp.float32, low / len(cuts), top_value / len(cuts))
        level = level * jnp.repeat(jnp.exp(heights), extent[position] // shards_of).reshape((-1,) + (1,) * (len(extent) - 1 - position))
    return level


def noise(stream_key, extent, scale, most, shards=(), kind=jnp.bfloat16):
    level = block_levels(stream_key, extent, shards, -0.22, 0.18) if shards else 1.0
    values = jax.random.normal(stream_key, extent, jnp.float32) * scale * level
    return jnp.minimum(jnp.maximum(values, -most), most).astype(kind)


def setup_inputs(seed: int = 0) -> dict:
    streams_of = jax.random.split(jax.random.key(seed), 11)
    image_rows = noise(streams_of[0], (SEQS, IMG, D), 1.0, 6.0, ((0, 8), (1, 4)))
    text_rows = noise(streams_of[1], (SEQS, TXT, D), 1.0, 6.0, ((0, 8), (1, 4)))
    conditioning = noise(streams_of[2], (SEQS, D), 1.0, 6.0, ((0, 8),))
    modulator = noise(streams_of[3], (LAYERS, 2, D, 6, D), D ** -0.5, 0.15625, ((2, 8), (4, 4)))
    attention_in = noise(streams_of[4], (LAYERS, 2, D, 3, D), D ** -0.5, 0.15625, ((2, 8), (4, 4)))
    attention_out = noise(streams_of[5], (LAYERS, 2, D, D), (HD // 2) ** -0.5, 1.0, ((2, 32),))
    up_weight = noise(streams_of[6], (LAYERS, 2, D, FF), D ** -0.5, 0.15625, ((2, 8), (3, 4)))
    down_weight = noise(streams_of[7], (LAYERS, 2, FF, D), FF ** -0.5, 0.078125, ((2, 32),))
    image_cotangent = noise(streams_of[8], (SEQS, IMG, D), 1.0, 6.0, ((0, 8), (1, 4)))
    text_cotangent = noise(streams_of[9], (SEQS, TXT, D), 1.0, 6.0, ((0, 8), (1, 4)))
    return dict(image_rows=image_rows, text_rows=text_rows, conditioning=conditioning, modulator=modulator, attention_in=attention_in, attention_out=attention_out, up_weight=up_weight, down_weight=down_weight, image_cotangent=image_cotangent, text_cotangent=text_cotangent)


@jax.custom_vjp
def low(v):
    return lax.optimization_barrier(v.astype(jnp.bfloat16)).astype(jnp.float32)

@jax.custom_vjp
def low_back(v):
    return v

def low_keep(v):
    return (low(v), None)

def low_pass(kept, grad):
    return (grad,)

def back_keep(v):
    return (v, None)

def back_low(kept, grad):
    return (low(grad),)
low.defvjp(low_keep, low_pass)
low_back.defvjp(back_keep, back_low)
highest = lax.Precision.HIGHEST
norm_eps = 1e-06

def layer_norm(rows):
    middle = lax.optimization_barrier(jnp.mean(rows, axis=-1, keepdims=True))
    centered = rows - middle
    spread = lax.optimization_barrier(jnp.mean(centered * centered, axis=-1, keepdims=True))
    return centered * lax.rsqrt(spread + norm_eps)

def one_sequence(weights, image_seq, text_seq, cond_seq):
    modulator, attention_in, attention_out, up_weight, down_weight = weights
    lifted = low(jax.nn.silu(cond_seq))
    carried = [image_seq, text_seq]
    image_count = image_seq.shape[0]
    for layer in range(LAYERS):
        factors = [jnp.einsum('d,dke->ke', lifted, modulator[layer, modality], precision=highest) for modality in range(2)]
        projected = []
        for modality in range(2):
            entry = low(layer_norm(carried[modality]) * (1.0 + factors[modality][1]) + factors[modality][0])
            projected.append(low(low_back(jnp.einsum('td,dke->tke', entry, attention_in[layer, modality], precision=highest))))
        joint = jnp.concatenate(projected, axis=0)
        length = joint.shape[0]
        split_heads = joint.reshape(length, 3, HEADS, HD)
        query = split_heads[:, 0]
        keys = split_heads[:, 1]
        values = split_heads[:, 2]
        scores = low_back(jnp.einsum('qhe,khe->hqk', query, keys, precision=highest) * HD ** (-0.5))
        probs = jax.nn.softmax(scores, axis=-1)
        mixed = low(low_back(jnp.einsum('hqk,khe->qhe', low(probs), values, precision=highest))).reshape(length, D)
        pieces = [mixed[:image_count], mixed[image_count:]]
        for modality in range(2):
            branch = low_back(jnp.dot(pieces[modality], attention_out[layer, modality], precision=highest))
            carried[modality] = carried[modality] + factors[modality][2] * branch
        for modality in range(2):
            entry = low(layer_norm(carried[modality]) * (1.0 + factors[modality][4]) + factors[modality][3])
            hidden = low_back(jnp.dot(entry, up_weight[layer, modality], precision=highest))
            active = low(jax.nn.gelu(hidden, approximate=True))
            branch = low_back(jnp.dot(active, down_weight[layer, modality], precision=highest))
            carried[modality] = carried[modality] + factors[modality][5] * branch
    return (carried[0], carried[1])

def reference(image_rows, text_rows, conditioning, modulator, attention_in, attention_out, up_weight, down_weight, image_cotangent, text_cotangent):
    weights = tuple((entry.astype(jnp.float32) for entry in (modulator, attention_in, attention_out, up_weight, down_weight)))

    def per_sequence(totals, items):
        image_seq, text_seq, cond_seq, image_back, text_back = items
        outputs, pullback = jax.vjp(one_sequence, weights, image_seq.astype(jnp.float32), text_seq.astype(jnp.float32), cond_seq.astype(jnp.float32))
        weight_grads, image_in_grad, text_in_grad, cond_in_grad = pullback((image_back.astype(jnp.float32), text_back.astype(jnp.float32)))
        totals = jax.tree.map(jnp.add, totals, weight_grads)
        return (totals, (outputs[0].astype(jnp.bfloat16), outputs[1].astype(jnp.bfloat16), image_in_grad, text_in_grad, cond_in_grad))
    start = tuple((jnp.zeros_like(entry) for entry in weights))
    totals, stacked = lax.scan(per_sequence, start, (image_rows, text_rows, conditioning, image_cotangent, text_cotangent))
    return (stacked[0], stacked[1], stacked[2], stacked[3], stacked[4], totals[0], totals[1], totals[2], totals[3], totals[4])
```

```python
from functools import partial

import jax
import jax.numpy as jnp
from jax import lax
from jax.sharding import PartitionSpec as P

HD = 64

norm_eps = 1e-06
highest = lax.Precision.HIGHEST
bf16 = jnp.bfloat16
f32 = jnp.float32


def layer_norm(rows):
    middle = jnp.mean(rows, axis=-1, keepdims=True)
    centered = rows - middle
    spread = jnp.mean(centered * centered, axis=-1, keepdims=True)
    return centered * lax.rsqrt(spread + norm_eps)


def modulate(rows, shift, scale):
    return layer_norm(rows) * (1.0 + scale[:, None, :]) + shift[:, None, :]


def modulate_back(rows, scale, grad):
    middle = jnp.mean(rows, axis=-1, keepdims=True)
    centered = rows - middle
    spread = jnp.mean(centered * centered, axis=-1, keepdims=True)
    inverse = lax.rsqrt(spread + norm_eps)
    normal = centered * inverse
    wide = grad * (1.0 + scale[:, None, :])
    first = jnp.mean(wide, axis=-1, keepdims=True)
    second = jnp.mean(wide * normal, axis=-1, keepdims=True)
    return inverse * (wide - first - normal * second), normal


def gelu_parts(hidden):
    slope = 0.7978845608028654
    square = hidden * hidden
    tail = jnp.tanh(slope * hidden * (1.0 + 0.044715 * square))
    active = 0.5 * hidden * (1.0 + tail)
    back = 0.5 * (1.0 + tail) + 0.5 * hidden * (1.0 - tail * tail) * (
        slope * (1.0 + 3.0 * 0.044715 * square)
    )
    return active, back


def query_blocks(length):
    count = max(1, length // 512)
    while length % count:
        count -= 1
    return count


def attend_forward(packed, scale):
    query = packed[:, 0]
    keys = packed[:, 1]
    values = packed[:, 2]
    length = packed.shape[0]
    blocks = query_blocks(length)
    rows = length // blocks
    mixed_parts = []
    total_parts = []
    for block in range(blocks):
        lower = block * rows
        block_query = query[lower : lower + rows]
        scores = jnp.einsum("qhe,khe->hqk", block_query, keys, preferred_element_type=f32) * scale
        largest = jnp.max(scores, axis=-1, keepdims=True)
        raised = jnp.exp(scores - largest)
        denominator = jnp.sum(raised, axis=-1, keepdims=True)
        probs = (raised / denominator).astype(bf16)
        mixed_parts.append(
            jnp.einsum("hqk,khe->qhe", probs, values, preferred_element_type=f32).astype(bf16)
        )
        total_parts.append(largest[..., 0] + jnp.log(denominator[..., 0]))
    return (jnp.concatenate(mixed_parts, axis=0), jnp.concatenate(total_parts, axis=1))


def attend_backward(items, scale):
    packed, grad_mixed, log_totals = items
    query = packed[:, 0]
    keys = packed[:, 1]
    values = packed[:, 2]
    length = packed.shape[0]
    blocks = query_blocks(length)
    rows = length // blocks
    grad_keys = jnp.zeros(keys.shape, f32)
    grad_values = jnp.zeros(values.shape, f32)
    query_parts = []
    for block in range(blocks):
        lower = block * rows
        block_query = query[lower : lower + rows]
        block_grad = grad_mixed[lower : lower + rows]
        scores = jnp.einsum("qhe,khe->hqk", block_query, keys, preferred_element_type=f32) * scale
        probs = jnp.exp(scores - log_totals[:, lower : lower + rows, None])
        grad_probs = jnp.einsum("qhe,khe->hqk", block_grad, values, preferred_element_type=f32)
        inner = jnp.sum(probs * grad_probs, axis=-1, keepdims=True)
        grad_scores = (probs * (grad_probs - inner)).astype(bf16)
        query_parts.append(
            jnp.einsum("hqk,khe->qhe", grad_scores, keys, preferred_element_type=f32) * scale
        )
        grad_keys = (
            grad_keys
            + jnp.einsum("hqk,qhe->khe", grad_scores, block_query, preferred_element_type=f32)
            * scale
        )
        grad_values = grad_values + jnp.einsum(
            "hqk,qhe->khe", probs.astype(bf16), block_grad, preferred_element_type=f32
        )
    grad_query = jnp.concatenate(query_parts, axis=0)
    return jnp.stack([grad_query, grad_keys, grad_values], axis=1).astype(bf16)


def ring_pairs(size):
    order = list(range(0, size, 2)) + list(range(size - 1, 0, -2)) if size != 4 else [0, 1, 3, 2]
    if size == 1:
        order = [0]
    return [(order[place], order[(place + 1) % size]) for place in range(size)]


def ring_gather(block, size):
    pairs = ring_pairs(size)
    blocks = [block]
    for step in range(size - 1):
        blocks.append(lax.ppermute(blocks[-1], "tensor", pairs))
    return blocks


def ring_scatter(parts, size):
    pairs = ring_pairs(size)
    if size == 1:
        return parts[0].astype(f32)
    total = parts[1].astype(bf16)
    for slot in list(range(2, size)) + [0]:
        total = lax.ppermute(total, "tensor", pairs).astype(f32) + parts[slot].astype(f32)
        if slot:
            total = total.astype(bf16)
    return total


def split_rows(blocks, count):
    return [
        jnp.concatenate([block[:, :count] for block in blocks], axis=1),
        jnp.concatenate([block[:, count:] for block in blocks], axis=1),
    ]


def join_slots(image, text, size):
    image_rows = image.shape[1] // size
    text_rows = text.shape[1] // size
    return [
        jnp.concatenate(
            [
                image[:, slot * image_rows : (slot + 1) * image_rows],
                text[:, slot * text_rows : (slot + 1) * text_rows],
            ],
            axis=1,
        )
        for slot in range(size)
    ]


def gather_weight(weight):
    return lax.all_gather(weight, "dp", axis=1, tiled=True)


def scatter_weight(grad):
    return lax.psum_scatter(grad.astype(bf16), "dp", scatter_dimension=1, tiled=True).astype(f32)


def sum_to_columns(value, axis_name, size, axis):
    shape = value.shape
    cut = value.reshape(shape[:axis] + (size, shape[axis] // size) + shape[axis + 1 :])
    cut = jnp.moveaxis(cut, axis, 0)
    return jnp.sum(lax.all_to_all(cut, axis_name, 0, 0, tiled=True), axis=0)


def shards(
    image_rows,
    text_rows,
    conditioning,
    modulator,
    attention_in,
    attention_out,
    up_weight,
    down_weight,
    image_cotangent,
    text_cotangent,
    dp_size,
    size,
):
    scale = HD ** (-0.5)
    modalities = range(2)
    modulator = modulator[0]
    seq_count, image_own = image_rows.shape[:2]
    length_image = image_own * size

    cond_float = conditioning.astype(f32)
    lifted = jax.nn.silu(cond_float).astype(bf16)

    inner_full = gather_weight(attention_in[0])
    outer_full = gather_weight(attention_out[0])
    up_full = gather_weight(up_weight[0])
    down_full = gather_weight(down_weight[0])

    x_blocks = ring_gather(jnp.concatenate([image_rows, text_rows], axis=1), size)

    lifted_all = lax.all_gather(lifted, "dp", axis=0, tiled=True)
    own_depth = modulator.shape[1]
    lifted_own = lax.dynamic_slice_in_dim(
        lifted_all, lax.axis_index("dp") * own_depth, own_depth, 1
    )
    factor_terms = jnp.einsum("sd,zdke->szke", lifted_own, modulator, preferred_element_type=f32)
    factor_cols = sum_to_columns(factor_terms, "dp", dp_size, 0)
    factors = lax.all_gather(factor_cols, "tensor", axis=3, tiled=True)

    cot_blocks = ring_gather(jnp.concatenate([image_cotangent, text_cotangent], axis=1), size)

    x_all = [rows.astype(f32) for rows in split_rows(x_blocks, image_own)]
    attn_inputs = [
        modulate(x_all[m], factors[:, m, 0], factors[:, m, 1]).astype(bf16) for m in modalities
    ]
    projected = jnp.concatenate(
        [
            jnp.einsum("snd,dke->snke", attn_inputs[m], inner_full[m], preferred_element_type=f32)
            for m in modalities
        ],
        axis=1,
    ).astype(bf16)
    length = projected.shape[1]
    width = projected.shape[3]
    packed = projected.reshape(seq_count, length, 3, width // HD, HD)
    mixed, log_totals = lax.map(partial(attend_forward, scale=scale), packed)
    mixed = mixed.reshape(seq_count, length, width)
    pieces = [mixed[:, :length_image], mixed[:, length_image:]]
    outer_terms = [
        jnp.einsum("kut,tx->kux", pieces[m], outer_full[m], preferred_element_type=f32)
        for m in modalities
    ]
    attn_branch = ring_scatter(join_slots(outer_terms[0], outer_terms[1], size), size)
    attn_branch = [attn_branch[:, :image_own], attn_branch[:, image_own:]]
    start_rows = [image_rows.astype(f32), text_rows.astype(f32)]
    middle_rows = [
        start_rows[m] + factors[:, m, 2][:, None, :] * attn_branch[m] for m in modalities
    ]
    feed_entries = [
        modulate(middle_rows[m], factors[:, m, 3], factors[:, m, 4]).astype(bf16)
        for m in modalities
    ]
    feed_inputs = split_rows(ring_gather(jnp.concatenate(feed_entries, axis=1), size), image_own)

    feed_grad = [
        (factors[:, m, 5][:, None, :] * rows.astype(f32)).astype(bf16)
        for m, rows in enumerate(split_rows(cot_blocks, image_own))
    ]
    down_terms = []
    entry_terms = []
    grad_up = []
    grad_down = []
    for m in modalities:
        hidden = jnp.einsum("snd,df->snf", feed_inputs[m], up_full[m], preferred_element_type=f32)
        active, back = gelu_parts(hidden)
        active = active.astype(bf16)
        grad_active = jnp.einsum(
            "snd,fd->snf", feed_grad[m], down_full[m], preferred_element_type=f32
        )
        grad_hidden = (grad_active * back).astype(bf16)
        entry_terms.append(
            jnp.einsum("snf,df->snd", grad_hidden, up_full[m], preferred_element_type=f32)
        )
        down_terms.append(
            jnp.einsum("snf,fd->snd", active, down_full[m], preferred_element_type=f32)
        )
        grad_down.append(
            jnp.einsum("snf,snd->fd", active, feed_grad[m], preferred_element_type=f32)
        )
        grad_up.append(
            jnp.einsum("snd,snf->df", feed_inputs[m], grad_hidden, preferred_element_type=f32)
        )
    entry_grad = ring_scatter(join_slots(entry_terms[0], entry_terms[1], size), size)
    feed_branch = ring_scatter(join_slots(down_terms[0], down_terms[1], size), size)
    up_owned = scatter_weight(jnp.stack(grad_up))
    down_owned = scatter_weight(jnp.stack(grad_down))

    entry_grad = [entry_grad[:, :image_own], entry_grad[:, image_own:]]
    feed_branch = [feed_branch[:, :image_own], feed_branch[:, image_own:]]
    grads = [image_cotangent.astype(f32), text_cotangent.astype(f32)]
    carried = [
        middle_rows[m] + factors[:, m, 5][:, None, :] * feed_branch[m] for m in modalities
    ]
    gate_two = [jnp.sum(grads[m] * feed_branch[m], axis=1) for m in modalities]
    shift_two = []
    scale_two = []
    gate_one = []
    sends = []
    for m in modalities:
        row_grad, normal = modulate_back(middle_rows[m], factors[:, m, 4], entry_grad[m])
        grads[m] = grads[m] + row_grad
        shift_two.append(jnp.sum(entry_grad[m], axis=1))
        scale_two.append(jnp.sum(entry_grad[m] * normal, axis=1))
        gate_one.append(jnp.sum(grads[m] * attn_branch[m], axis=1))
        sends.append((factors[:, m, 2][:, None, :] * grads[m]).astype(bf16))
    attn_grad = split_rows(ring_gather(jnp.concatenate(sends, axis=1), size), image_own)
    grad_mixed = jnp.concatenate(
        [
            jnp.einsum("hom,rm->hor", attn_grad[m], outer_full[m], preferred_element_type=f32)
            for m in modalities
        ],
        axis=1,
    ).astype(bf16)
    grad_outer = jnp.stack(
        [
            jnp.einsum("puj,puo->jo", pieces[m], attn_grad[m], preferred_element_type=f32)
            for m in modalities
        ]
    )
    outer_owned = scatter_weight(grad_outer)
    grad_packed = lax.map(
        partial(attend_backward, scale=scale),
        (packed, grad_mixed.reshape(seq_count, length, width // HD, HD), log_totals),
    )
    grad_projected = grad_packed.reshape(seq_count, length, 3, width)
    grad_split = [grad_projected[:, :length_image], grad_projected[:, length_image:]]
    grad_inner = jnp.stack(
        [
            jnp.einsum("snd,snke->dke", attn_inputs[m], grad_split[m], preferred_element_type=f32)
            for m in modalities
        ]
    )
    inner_owned = scatter_weight(grad_inner)
    entry_terms = [
        jnp.einsum("snke,dke->snd", grad_split[m], inner_full[m], preferred_element_type=f32)
        for m in modalities
    ]
    entry_grad = ring_scatter(join_slots(entry_terms[0], entry_terms[1], size), size)
    entry_grad = [entry_grad[:, :image_own], entry_grad[:, image_own:]]

    factor_terms = []
    for m in modalities:
        row_grad, normal = modulate_back(start_rows[m], factors[:, m, 1], entry_grad[m])
        grads[m] = grads[m] + row_grad
        factor_terms.append(
            jnp.stack(
                [
                    jnp.sum(entry_terms[m], axis=1),
                    jnp.sum(entry_terms[m] * layer_norm(x_all[m]), axis=1),
                    gate_one[m],
                    shift_two[m],
                    scale_two[m],
                    gate_two[m],
                ],
                axis=1,
            )
        )
    factor_sums = sum_to_columns(jnp.stack(factor_terms, axis=1), "tensor", size, 3)
    factor_all = lax.all_gather(factor_sums, "dp", axis=0, tiled=True)
    mod_owned = jnp.einsum("sd,szke->zdke", lifted_own.astype(f32), factor_all, precision=highest)
    lifted_terms = jnp.einsum(
        "szke,zdke->sd", factor_all, modulator.astype(f32), precision=highest
    )
    swapped = lax.all_to_all(
        lifted_terms.reshape(dp_size, seq_count, own_depth), "dp", 0, 0, tiled=True
    )
    lifted_sum = jnp.moveaxis(swapped, 0, 1).reshape(seq_count, dp_size * own_depth)
    lifted_cols = sum_to_columns(lifted_sum, "tensor", size, 1)
    columns = lifted_cols.shape[1]
    own_cond = lax.dynamic_slice_in_dim(cond_float, lax.axis_index("tensor") * columns, columns, 1)
    gate = jax.nn.sigmoid(own_cond)
    cond_grad = lifted_cols * (gate * (1.0 + own_cond * (1.0 - gate)))
    return (
        carried[0].astype(bf16),
        carried[1].astype(bf16),
        grads[0],
        grads[1],
        cond_grad,
        mod_owned[None],
        inner_owned[None],
        outer_owned[None],
        up_owned[None],
        down_owned[None],
    )


def solution(mesh):
    in_specs = (
        P("dp", "tensor", None),
        P("dp", "tensor", None),
        P("dp", None),
        P(None, None, "dp", None, "tensor"),
        P(None, None, "dp", None, "tensor"),
        P(None, None, ("tensor", "dp"), None),
        P(None, None, "dp", "tensor"),
        P(None, None, ("tensor", "dp"), None),
        P("dp", "tensor", None),
        P("dp", "tensor", None),
    )
    out_specs = (
        P("dp", "tensor", None),
        P("dp", "tensor", None),
        P("dp", "tensor", None),
        P("dp", "tensor", None),
        P("dp", "tensor"),
        P(None, None, "dp", None, "tensor"),
        P(None, None, "dp", None, "tensor"),
        P(None, None, ("tensor", "dp"), None),
        P(None, None, "dp", "tensor"),
        P(None, None, ("tensor", "dp"), None),
    )
    body = partial(shards, dp_size=mesh.shape["dp"], size=mesh.shape["tensor"])
    return jax.shard_map(body, mesh=mesh, in_specs=in_specs, out_specs=out_specs, check_vma=False)
```

```python
from functools import partial

import jax
import jax.numpy as jnp
from jax import lax
from jax.experimental import pallas as pl
from jax.experimental.pallas import tpu as pltpu
from jax.sharding import PartitionSpec as P

HD = 64

norm_eps = 1e-06
highest = lax.Precision.HIGHEST
VMEM_LIMIT = 40 * 1024 * 1024
bf16 = jnp.bfloat16
f32 = jnp.float32


def layer_norm(rows):
    middle = jnp.mean(rows, axis=-1, keepdims=True)
    centered = rows - middle
    spread = jnp.mean(centered * centered, axis=-1, keepdims=True)
    return centered * lax.rsqrt(spread + norm_eps)


def modulate(rows, shift, scale):
    return layer_norm(rows) * (1.0 + scale[:, None, :]) + shift[:, None, :]


def modulate_back(rows, scale, grad):
    middle = jnp.mean(rows, axis=-1, keepdims=True)
    centered = rows - middle
    spread = jnp.mean(centered * centered, axis=-1, keepdims=True)
    inverse = lax.rsqrt(spread + norm_eps)
    normal = centered * inverse
    wide = grad * (1.0 + scale[:, None, :])
    first = jnp.mean(wide, axis=-1, keepdims=True)
    second = jnp.mean(wide * normal, axis=-1, keepdims=True)
    return inverse * (wide - first - normal * second), normal


def gelu_parts(hidden):
    slope = 0.7978845608028654
    square = hidden * hidden
    tail = jnp.tanh(slope * hidden * (1.0 + 0.044715 * square))
    active = 0.5 * hidden * (1.0 + tail)
    back = 0.5 * (1.0 + tail) + 0.5 * hidden * (1.0 - tail * tail) * (
        slope * (1.0 + 3.0 * 0.044715 * square)
    )
    return active, back


NT = (((1,), (1,)), ((), ()))
NN = (((1,), (0,)), ((), ()))
TN = (((0,), (0,)), ((), ()))


def product(left, right, numbers):
    return lax.dot_general(left, right, numbers, preferred_element_type=f32)


def cuts(length, step):
    return [(lower, min(lower + step, length)) for lower in range(0, length, step)]


def attend_forward_kernel(packed, mixed, totals, *, step, scale):
    length, width = mixed.shape[1:]
    for head in range(width // HD):
        lane = head * HD
        keys = packed[0, :, width + lane : width + lane + HD]
        values = packed[0, :, 2 * width + lane : 2 * width + lane + HD]
        for lower, upper in cuts(length, step):
            query = packed[0, lower:upper, lane : lane + HD] * scale
            scores = product(keys, query, NT)
            largest = jnp.max(scores, axis=0, keepdims=True)
            raised = jnp.exp(scores - largest)
            denominator = jnp.sum(raised, axis=0, keepdims=True)
            probs = (raised * (1.0 / denominator)).astype(bf16)
            mixed[0, lower:upper, lane : lane + HD] = product(probs, values, TN).astype(bf16)
            totals[0, head : head + 1, lower:upper] = largest + jnp.log(denominator)


def attend_forward(packed, scale):
    seqs, length, width = packed.shape[0], packed.shape[1], packed.shape[2] // 3
    heads = width // HD
    pairs = seqs * heads * length * length
    return pl.pallas_call(
        partial(attend_forward_kernel, step=640, scale=scale),
        grid=(seqs,),
        in_specs=[pl.BlockSpec((1, length, 3 * width), lambda s: (s, 0, 0))],
        out_specs=[
            pl.BlockSpec((1, length, width), lambda s: (s, 0, 0)),
            pl.BlockSpec((1, heads, length), lambda s: (s, 0, 0)),
        ],
        out_shape=[
            jax.ShapeDtypeStruct((seqs, length, width), bf16),
            jax.ShapeDtypeStruct((seqs, heads, length), f32),
        ],
        cost_estimate=pl.CostEstimate(
            flops=pairs * HD * 16, bytes_accessed=seqs * length * width * 8, transcendentals=pairs
        ),
        compiler_params=pltpu.CompilerParams(vmem_limit_bytes=VMEM_LIMIT),
        name="attend_forward",
    )(packed)


def attend_backward_kernel(packed, grad_mixed, totals, grad, key_sum, value_sum, *, step, scale):
    length, width = grad_mixed.shape[1:]
    for head in range(width // HD):
        lane = head * HD
        keys = packed[0, :, width + lane : width + lane + HD]
        values = packed[0, :, 2 * width + lane : 2 * width + lane + HD]
        for lower, upper in cuts(length, step):
            query = packed[0, lower:upper, lane : lane + HD] * scale
            block_grad = grad_mixed[0, lower:upper, lane : lane + HD]
            probs = jnp.exp(product(keys, query, NT) - totals[0, head : head + 1, lower:upper])
            weighted = probs * product(values, block_grad, NT)
            inner = jnp.sum(weighted, axis=0, keepdims=True)
            grad_scores = (weighted - probs * inner).astype(bf16)
            grad_values = product(probs.astype(bf16), block_grad, NN)
            grad_keys = product(grad_scores, query, NN)
            grad_query = product(grad_scores, keys, TN) * scale
            grad[0, lower:upper, lane : lane + HD] = grad_query.astype(bf16)
            if lower:
                key_sum[...] += grad_keys
                value_sum[...] += grad_values
            else:
                key_sum[...] = grad_keys
                value_sum[...] = grad_values
        grad[0, :, width + lane : width + lane + HD] = key_sum[...].astype(bf16)
        grad[0, :, 2 * width + lane : 2 * width + lane + HD] = value_sum[...].astype(bf16)


def attend_backward(packed, grad_mixed, totals, scale):
    seqs, length, width = grad_mixed.shape
    heads = width // HD
    pairs = seqs * heads * length * length
    return pl.pallas_call(
        partial(attend_backward_kernel, step=640, scale=scale),
        grid=(seqs,),
        in_specs=[
            pl.BlockSpec((1, length, 3 * width), lambda s: (s, 0, 0)),
            pl.BlockSpec((1, length, width), lambda s: (s, 0, 0)),
            pl.BlockSpec((1, heads, length), lambda s: (s, 0, 0)),
        ],
        out_specs=pl.BlockSpec((1, length, 3 * width), lambda s: (s, 0, 0)),
        out_shape=jax.ShapeDtypeStruct((seqs, length, 3 * width), bf16),
        scratch_shapes=[pltpu.VMEM((length, HD), f32), pltpu.VMEM((length, HD), f32)],
        cost_estimate=pl.CostEstimate(
            flops=pairs * HD * 32, bytes_accessed=seqs * length * width * 14, transcendentals=pairs
        ),
        compiler_params=pltpu.CompilerParams(vmem_limit_bytes=VMEM_LIMIT),
        name="attend_backward",
    )(packed, grad_mixed, totals)


def ring_pairs(size):
    order = list(range(0, size, 2)) + list(range(size - 1, 0, -2)) if size != 4 else [0, 1, 3, 2]
    if size == 1:
        order = [0]
    return [(order[place], order[(place + 1) % size]) for place in range(size)]


def ring_gather(block, size):
    pairs = ring_pairs(size)
    blocks = [block]
    for step in range(size - 1):
        blocks.append(lax.ppermute(blocks[-1], "tensor", pairs))
    return blocks


def ring_scatter(parts, size):
    pairs = ring_pairs(size)
    if size == 1:
        return parts[0].astype(f32)
    total = parts[1].astype(bf16)
    for slot in list(range(2, size)) + [0]:
        total = lax.ppermute(total, "tensor", pairs).astype(f32) + parts[slot].astype(f32)
        if slot:
            total = total.astype(bf16)
    return total


def split_rows(blocks, count):
    return [
        jnp.concatenate([block[:, :count] for block in blocks], axis=1),
        jnp.concatenate([block[:, count:] for block in blocks], axis=1),
    ]


def join_slots(image, text, size):
    image_rows = image.shape[1] // size
    text_rows = text.shape[1] // size
    return [
        jnp.concatenate(
            [
                image[:, slot * image_rows : (slot + 1) * image_rows],
                text[:, slot * text_rows : (slot + 1) * text_rows],
            ],
            axis=1,
        )
        for slot in range(size)
    ]


def gather_weight(weight):
    return lax.all_gather(weight, "dp", axis=1, tiled=True)


def scatter_weight(grad):
    return lax.psum_scatter(grad.astype(bf16), "dp", scatter_dimension=1, tiled=True).astype(f32)


def sum_to_columns(value, axis_name, size, axis):
    shape = value.shape
    cut = value.reshape(shape[:axis] + (size, shape[axis] // size) + shape[axis + 1 :])
    cut = jnp.moveaxis(cut, axis, 0)
    return jnp.sum(lax.all_to_all(cut, axis_name, 0, 0, tiled=True), axis=0)


def shards(
    image_rows,
    text_rows,
    conditioning,
    modulator,
    attention_in,
    attention_out,
    up_weight,
    down_weight,
    image_cotangent,
    text_cotangent,
    dp_size,
    size,
):
    scale = HD ** (-0.5)
    modalities = range(2)
    modulator = modulator[0]
    seq_count, image_own = image_rows.shape[:2]
    length_image = image_own * size

    cond_float = conditioning.astype(f32)
    lifted = jax.nn.silu(cond_float).astype(bf16)

    inner_full = gather_weight(attention_in[0].reshape(2, attention_in.shape[2], -1))
    outer_full = gather_weight(attention_out[0])
    up_full = gather_weight(up_weight[0])
    down_full = gather_weight(down_weight[0])

    x_blocks = ring_gather(jnp.concatenate([image_rows, text_rows], axis=1), size)

    lifted_all = lax.all_gather(lifted, "dp", axis=0, tiled=True)
    own_depth = modulator.shape[1]
    lifted_own = lax.dynamic_slice_in_dim(
        lifted_all, lax.axis_index("dp") * own_depth, own_depth, 1
    )
    factor_terms = jnp.einsum("sd,zdke->szke", lifted_own, modulator, preferred_element_type=f32)
    factor_cols = sum_to_columns(factor_terms, "dp", dp_size, 0)
    factors = lax.all_gather(factor_cols, "tensor", axis=3, tiled=True)

    cot_blocks = ring_gather(jnp.concatenate([image_cotangent, text_cotangent], axis=1), size)

    x_all = [rows.astype(f32) for rows in split_rows(x_blocks, image_own)]
    attn_inputs = [
        modulate(x_all[m], factors[:, m, 0], factors[:, m, 1]).astype(bf16) for m in modalities
    ]
    packed = jnp.concatenate(
        [
            jnp.einsum("snd,de->sne", attn_inputs[m], inner_full[m], preferred_element_type=f32)
            for m in modalities
        ],
        axis=1,
    ).astype(bf16)
    mixed, log_totals = attend_forward(packed, scale)
    pieces = [mixed[:, :length_image], mixed[:, length_image:]]
    outer_terms = [
        jnp.einsum("kut,tx->kux", pieces[m], outer_full[m], preferred_element_type=f32)
        for m in modalities
    ]
    attn_branch = ring_scatter(join_slots(outer_terms[0], outer_terms[1], size), size)
    attn_branch = [attn_branch[:, :image_own], attn_branch[:, image_own:]]
    start_rows = [image_rows.astype(f32), text_rows.astype(f32)]
    middle_rows = [
        start_rows[m] + factors[:, m, 2][:, None, :] * attn_branch[m] for m in modalities
    ]
    feed_entries = [
        modulate(middle_rows[m], factors[:, m, 3], factors[:, m, 4]).astype(bf16)
        for m in modalities
    ]
    feed_inputs = split_rows(ring_gather(jnp.concatenate(feed_entries, axis=1), size), image_own)

    feed_grad = [
        (factors[:, m, 5][:, None, :] * rows.astype(f32)).astype(bf16)
        for m, rows in enumerate(split_rows(cot_blocks, image_own))
    ]
    down_terms = []
    entry_terms = []
    grad_up = []
    grad_down = []
    for m in modalities:
        hidden = jnp.einsum("snd,df->snf", feed_inputs[m], up_full[m], preferred_element_type=f32)
        active, back = gelu_parts(hidden)
        active = active.astype(bf16)
        grad_active = jnp.einsum(
            "snd,fd->snf", feed_grad[m], down_full[m], preferred_element_type=f32
        )
        grad_hidden = (grad_active * back).astype(bf16)
        entry_terms.append(
            jnp.einsum("snf,df->snd", grad_hidden, up_full[m], preferred_element_type=f32)
        )
        down_terms.append(
            jnp.einsum("snf,fd->snd", active, down_full[m], preferred_element_type=f32)
        )
        grad_down.append(
            jnp.einsum("snf,snd->fd", active, feed_grad[m], preferred_element_type=f32)
        )
        grad_up.append(
            jnp.einsum("snd,snf->df", feed_inputs[m], grad_hidden, preferred_element_type=f32)
        )
    entry_grad = ring_scatter(join_slots(entry_terms[0], entry_terms[1], size), size)
    feed_branch = ring_scatter(join_slots(down_terms[0], down_terms[1], size), size)
    grad_up = jnp.stack(grad_up).astype(bf16)
    grad_down = jnp.stack(grad_down).astype(bf16)
    up_owned = scatter_weight(grad_up)
    down_owned = scatter_weight(grad_down)

    entry_grad = [entry_grad[:, :image_own], entry_grad[:, image_own:]]
    feed_branch = [feed_branch[:, :image_own], feed_branch[:, image_own:]]
    grads = [image_cotangent.astype(f32), text_cotangent.astype(f32)]
    carried = [
        middle_rows[m] + factors[:, m, 5][:, None, :] * feed_branch[m] for m in modalities
    ]
    gate_two = [jnp.sum(grads[m] * feed_branch[m], axis=1) for m in modalities]
    shift_two = []
    scale_two = []
    gate_one = []
    sends = []
    for m in modalities:
        row_grad, normal = modulate_back(middle_rows[m], factors[:, m, 4], entry_grad[m])
        grads[m] = grads[m] + row_grad
        shift_two.append(jnp.sum(entry_grad[m], axis=1))
        scale_two.append(jnp.sum(entry_grad[m] * normal, axis=1))
        gate_one.append(jnp.sum(grads[m] * attn_branch[m], axis=1))
        sends.append((factors[:, m, 2][:, None, :] * grads[m]).astype(bf16))
    attn_grad = split_rows(ring_gather(jnp.concatenate(sends, axis=1), size), image_own)
    grad_mixed = jnp.concatenate(
        [
            jnp.einsum("hom,rm->hor", attn_grad[m], outer_full[m], preferred_element_type=f32)
            for m in modalities
        ],
        axis=1,
    ).astype(bf16)
    grad_outer = jnp.stack(
        [
            jnp.einsum("puj,puo->jo", pieces[m], attn_grad[m], preferred_element_type=f32)
            for m in modalities
        ]
    )
    grad_outer, grad_up, grad_down = lax.optimization_barrier(
        (grad_outer.astype(bf16), grad_up, grad_down)
    )
    outer_owned = scatter_weight(grad_outer)
    grad_packed = attend_backward(packed, grad_mixed, log_totals, scale)
    grad_split = [grad_packed[:, :length_image], grad_packed[:, length_image:]]
    grad_inner = jnp.stack(
        [
            jnp.einsum("snd,sne->de", attn_inputs[m], grad_split[m], preferred_element_type=f32)
            for m in modalities
        ]
    )
    inner_owned = scatter_weight(grad_inner)
    entry_terms = [
        jnp.einsum("sne,de->snd", grad_split[m], inner_full[m], preferred_element_type=f32)
        for m in modalities
    ]
    entry_grad = ring_scatter(join_slots(entry_terms[0], entry_terms[1], size), size)
    entry_grad = [entry_grad[:, :image_own], entry_grad[:, image_own:]]

    factor_terms = []
    for m in modalities:
        row_grad, normal = modulate_back(start_rows[m], factors[:, m, 1], entry_grad[m])
        grads[m] = grads[m] + row_grad
        factor_terms.append(
            jnp.stack(
                [
                    jnp.sum(entry_terms[m], axis=1),
                    jnp.sum(entry_terms[m] * layer_norm(x_all[m]), axis=1),
                    gate_one[m],
                    shift_two[m],
                    scale_two[m],
                    gate_two[m],
                ],
                axis=1,
            )
        )
    factor_sums = sum_to_columns(jnp.stack(factor_terms, axis=1), "tensor", size, 3)
    factor_all = lax.all_gather(factor_sums, "dp", axis=0, tiled=True)
    mod_owned = jnp.einsum("sd,szke->zdke", lifted_own.astype(f32), factor_all, precision=highest)
    lifted_terms = jnp.einsum(
        "szke,zdke->sd", factor_all, modulator.astype(f32), precision=highest
    )
    swapped = lax.all_to_all(
        lifted_terms.reshape(dp_size, seq_count, own_depth), "dp", 0, 0, tiled=True
    )
    lifted_sum = jnp.moveaxis(swapped, 0, 1).reshape(seq_count, dp_size * own_depth)
    lifted_cols = sum_to_columns(lifted_sum, "tensor", size, 1)
    columns = lifted_cols.shape[1]
    own_cond = lax.dynamic_slice_in_dim(cond_float, lax.axis_index("tensor") * columns, columns, 1)
    gate = jax.nn.sigmoid(own_cond)
    cond_grad = lifted_cols * (gate * (1.0 + own_cond * (1.0 - gate)))
    return (
        carried[0].astype(bf16),
        carried[1].astype(bf16),
        grads[0],
        grads[1],
        cond_grad,
        mod_owned[None],
        inner_owned.reshape(attention_in.shape),
        outer_owned[None],
        up_owned[None],
        down_owned[None],
    )


def solution(mesh):
    in_specs = (
        P("dp", "tensor", None),
        P("dp", "tensor", None),
        P("dp", None),
        P(None, None, "dp", None, "tensor"),
        P(None, None, "dp", None, "tensor"),
        P(None, None, ("tensor", "dp"), None),
        P(None, None, "dp", "tensor"),
        P(None, None, ("tensor", "dp"), None),
        P("dp", "tensor", None),
        P("dp", "tensor", None),
    )
    out_specs = (
        P("dp", "tensor", None),
        P("dp", "tensor", None),
        P("dp", "tensor", None),
        P("dp", "tensor", None),
        P("dp", "tensor"),
        P(None, None, "dp", None, "tensor"),
        P(None, None, "dp", None, "tensor"),
        P(None, None, ("tensor", "dp"), None),
        P(None, None, "dp", "tensor"),
        P(None, None, ("tensor", "dp"), None),
    )
    body = partial(shards, dp_size=mesh.shape["dp"], size=mesh.shape["tensor"])
    return jax.shard_map(body, mesh=mesh, in_specs=in_specs, out_specs=out_specs, check_vma=False)
```

```python
from functools import partial

import jax
import jax.numpy as jnp
from jax import lax
from jax.experimental import pallas as pl
from jax.experimental.pallas import tpu as pltpu
from jax.sharding import Mesh
from jax.sharding import PartitionSpec as P

HD = 64

norm_eps = 1e-06
highest = lax.Precision.HIGHEST
DP = ("side", "rest")
TENSOR = ("half", "low")
GROUP = ("side", "low")
VMEM_LIMIT = 40 * 1024 * 1024
bf16 = jnp.bfloat16
f32 = jnp.float32


def layer_norm(rows):
    middle = jnp.mean(rows, axis=-1, keepdims=True)
    centered = rows - middle
    spread = jnp.mean(centered * centered, axis=-1, keepdims=True)
    return centered * lax.rsqrt(spread + norm_eps)


def modulate(rows, shift, scale):
    return layer_norm(rows) * (1.0 + scale[:, None, :]) + shift[:, None, :]


def modulate_back(rows, scale, grad):
    middle = jnp.mean(rows, axis=-1, keepdims=True)
    centered = rows - middle
    spread = jnp.mean(centered * centered, axis=-1, keepdims=True)
    inverse = lax.rsqrt(spread + norm_eps)
    normal = centered * inverse
    wide = grad * (1.0 + scale[:, None, :])
    first = jnp.mean(wide, axis=-1, keepdims=True)
    second = jnp.mean(wide * normal, axis=-1, keepdims=True)
    return inverse * (wide - first - normal * second), normal


def gelu_parts(hidden):
    slope = 0.7978845608028654
    square = hidden * hidden
    tail = jnp.tanh(slope * hidden * (1.0 + 0.044715 * square))
    active = 0.5 * hidden * (1.0 + tail)
    back = 0.5 * (1.0 + tail) + 0.5 * hidden * (1.0 - tail * tail) * (
        slope * (1.0 + 3.0 * 0.044715 * square)
    )
    return active, back


NT = (((1,), (1,)), ((), ()))
NN = (((1,), (0,)), ((), ()))
TN = (((0,), (0,)), ((), ()))


def product(left, right, numbers):
    return lax.dot_general(left, right, numbers, preferred_element_type=f32)


def cuts(length, step):
    return [(lower, min(lower + step, length)) for lower in range(0, length, step)]


def attend_forward_kernel(packed, mixed, totals, *, step, scale):
    length, width = mixed.shape[1:]
    for head in range(width // HD):
        lane = head * HD
        keys = packed[0, :, width + lane : width + lane + HD]
        values = packed[0, :, 2 * width + lane : 2 * width + lane + HD]
        for lower, upper in cuts(length, step):
            query = packed[0, lower:upper, lane : lane + HD] * scale
            scores = product(keys, query, NT)
            largest = jnp.max(scores, axis=0, keepdims=True)
            raised = jnp.exp(scores - largest)
            denominator = jnp.sum(raised, axis=0, keepdims=True)
            probs = (raised * (1.0 / denominator)).astype(bf16)
            mixed[0, lower:upper, lane : lane + HD] = product(probs, values, TN).astype(bf16)
            totals[0, head : head + 1, lower:upper] = largest + jnp.log(denominator)


def attend_forward(packed, scale):
    seqs, length, width = packed.shape[0], packed.shape[1], packed.shape[2] // 3
    heads = width // HD
    pairs = seqs * heads * length * length
    return pl.pallas_call(
        partial(attend_forward_kernel, step=640, scale=scale),
        grid=(seqs,),
        in_specs=[pl.BlockSpec((1, length, 3 * width), lambda s: (s, 0, 0))],
        out_specs=[
            pl.BlockSpec((1, length, width), lambda s: (s, 0, 0)),
            pl.BlockSpec((1, heads, length), lambda s: (s, 0, 0)),
        ],
        out_shape=[
            jax.ShapeDtypeStruct((seqs, length, width), bf16),
            jax.ShapeDtypeStruct((seqs, heads, length), f32),
        ],
        cost_estimate=pl.CostEstimate(
            flops=pairs * HD * 16, bytes_accessed=seqs * length * width * 8, transcendentals=pairs
        ),
        compiler_params=pltpu.CompilerParams(vmem_limit_bytes=VMEM_LIMIT),
        name="attend_forward",
    )(packed)


def attend_backward_kernel(packed, grad_mixed, totals, grad, key_sum, value_sum, *, step, scale):
    length, width = grad_mixed.shape[1:]
    for head in range(width // HD):
        lane = head * HD
        keys = packed[0, :, width + lane : width + lane + HD]
        values = packed[0, :, 2 * width + lane : 2 * width + lane + HD]
        for lower, upper in cuts(length, step):
            query = packed[0, lower:upper, lane : lane + HD] * scale
            block_grad = grad_mixed[0, lower:upper, lane : lane + HD]
            probs = jnp.exp(product(keys, query, NT) - totals[0, head : head + 1, lower:upper])
            weighted = probs * product(values, block_grad, NT)
            inner = jnp.sum(weighted, axis=0, keepdims=True)
            grad_scores = (weighted - probs * inner).astype(bf16)
            grad_values = product(probs.astype(bf16), block_grad, NN)
            grad_keys = product(grad_scores, query, NN)
            grad_query = product(grad_scores, keys, TN) * scale
            grad[0, lower:upper, lane : lane + HD] = grad_query.astype(bf16)
            if lower:
                key_sum[...] += grad_keys
                value_sum[...] += grad_values
            else:
                key_sum[...] = grad_keys
                value_sum[...] = grad_values
        grad[0, :, width + lane : width + lane + HD] = key_sum[...].astype(bf16)
        grad[0, :, 2 * width + lane : 2 * width + lane + HD] = value_sum[...].astype(bf16)


def attend_backward(packed, grad_mixed, totals, scale):
    seqs, length, width = grad_mixed.shape
    heads = width // HD
    pairs = seqs * heads * length * length
    return pl.pallas_call(
        partial(attend_backward_kernel, step=640, scale=scale),
        grid=(seqs,),
        in_specs=[
            pl.BlockSpec((1, length, 3 * width), lambda s: (s, 0, 0)),
            pl.BlockSpec((1, length, width), lambda s: (s, 0, 0)),
            pl.BlockSpec((1, heads, length), lambda s: (s, 0, 0)),
        ],
        out_specs=pl.BlockSpec((1, length, 3 * width), lambda s: (s, 0, 0)),
        out_shape=jax.ShapeDtypeStruct((seqs, length, 3 * width), bf16),
        scratch_shapes=[pltpu.VMEM((length, HD), f32), pltpu.VMEM((length, HD), f32)],
        cost_estimate=pl.CostEstimate(
            flops=pairs * HD * 32, bytes_accessed=seqs * length * width * 14, transcendentals=pairs
        ),
        compiler_params=pltpu.CompilerParams(vmem_limit_bytes=VMEM_LIMIT),
        name="attend_backward",
    )(packed, grad_mixed, totals)


SWAP = [(0, 0), (1, 2), (2, 1), (3, 3)]
TURN = [(0, 1), (1, 3), (2, 0), (3, 2)]
TURN_BACK = [(1, 0), (3, 1), (0, 2), (2, 3)]


def swap(value):
    return lax.ppermute(value, ("side", "half"), SWAP)


def flip(value):
    return lax.ppermute(value, "side", [(0, 1), (1, 0)])


def shift(value, step, size):
    return lax.ppermute(value, "low", [(place, (place + step) % size) for place in range(size)])


def middle_row(block):
    return max(block.shape[1] // 32 * 16, 8)


def gather_rows(block, size):
    cut = middle_row(block)
    other = flip(block)
    slots = [block, other]
    for step in range(1, size):
        near = shift(block, step, size)
        upper = shift(other[:, :cut], step, size)
        lower = flip(near[:, cut:])
        slots += [near, jnp.concatenate([upper, lower], axis=1)]
    return slots


def scatter_rows(parts, size):
    cut = middle_row(parts[0])
    other = parts[1]
    upper = other[:, :cut]
    nears = []
    for step in range(1, size):
        near, far = parts[2 * step], parts[2 * step + 1]
        upper = upper + shift(far[:, :cut].astype(bf16), -step, size).astype(f32)
        lower = near[:, cut:] + flip(far[:, cut:].astype(bf16)).astype(f32)
        nears.append(jnp.concatenate([near[:, :cut], lower], axis=1).astype(bf16))
    other = jnp.concatenate([upper, other[:, cut:]], axis=1).astype(bf16)
    total = parts[0] + flip(other).astype(f32)
    for step in range(1, size):
        total = total + shift(nears[step - 1], -step, size).astype(f32)
    return total


def split_rows(blocks, count):
    return [
        jnp.concatenate([block[:, :count] for block in blocks], axis=1),
        jnp.concatenate([block[:, count:] for block in blocks], axis=1),
    ]


def join_slots(image, text, size):
    image_rows = image.shape[1] // size
    text_rows = text.shape[1] // size
    return [
        jnp.concatenate(
            [
                image[:, slot * image_rows : (slot + 1) * image_rows],
                text[:, slot * text_rows : (slot + 1) * text_rows],
            ],
            axis=1,
        )
        for slot in range(size)
    ]


def gather_weight(weight):
    first = lax.axis_index("half") == 0
    straight = swap(weight)
    turned = lax.ppermute(weight, ("side", "half"), TURN)
    pair = jnp.stack(
        [jnp.where(first, straight, turned), jnp.where(first, turned, straight)], axis=1
    )
    full = lax.all_gather(pair, "rest", axis=2, tiled=True)
    return full.reshape(full.shape[0], -1, full.shape[3])


def scatter_weight(grad):
    first = lax.axis_index("half") == 0
    depth = grad.shape[1] // 2
    cut = grad.astype(bf16).reshape(grad.shape[0], 2, depth, grad.shape[2])
    own = lax.psum_scatter(cut, "rest", scatter_dimension=2, tiled=True)
    straight = swap(jnp.where(first, own[:, 0], own[:, 1]))
    turned = lax.ppermute(
        jnp.where(first, own[:, 1], own[:, 0]), ("side", "half"), TURN_BACK
    )
    return straight.astype(f32) + turned.astype(f32)


def sum_to_columns(value, axis_name, size, axis):
    shape = value.shape
    cut = value.reshape(shape[:axis] + (size, shape[axis] // size) + shape[axis + 1 :])
    cut = jnp.moveaxis(cut, axis, 0)
    return jnp.sum(lax.all_to_all(cut, axis_name, 0, 0, tiled=True), axis=0)


def shards(
    image_rows,
    text_rows,
    conditioning,
    modulator,
    attention_in,
    attention_out,
    up_weight,
    down_weight,
    image_cotangent,
    text_cotangent,
    dp_size,
    size,
):
    scale = HD ** (-0.5)
    modalities = range(2)
    modulator = modulator[0]
    seq_count, image_own = image_rows.shape[:2]
    length_image = image_own * size
    low = size // 2

    cond_float = conditioning.astype(f32)
    lifted = jax.nn.silu(cond_float).astype(bf16)

    inner_full = gather_weight(attention_in[0].reshape(2, attention_in.shape[2], -1))
    outer_full = gather_weight(attention_out[0])
    up_full = gather_weight(up_weight[0])
    down_full = gather_weight(down_weight[0])

    x_own = swap(jnp.concatenate([image_rows, text_rows], axis=1))
    x_blocks = gather_rows(x_own, low)

    lifted_all = lax.all_gather(lifted, DP, axis=0, tiled=True)
    own_depth = modulator.shape[1]
    lifted_own = lax.dynamic_slice_in_dim(
        lifted_all, lax.axis_index(DP) * own_depth, own_depth, 1
    )
    factor_terms = jnp.einsum("sd,zdke->szke", lifted_own, modulator, preferred_element_type=f32)
    factor_cols = swap(sum_to_columns(factor_terms, DP, dp_size, 0))
    factors = lax.all_gather(factor_cols, GROUP, axis=3, tiled=True)

    cot_own = swap(jnp.concatenate([image_cotangent, text_cotangent], axis=1))
    cot_blocks = gather_rows(cot_own, low)

    x_all = [rows.astype(f32) for rows in split_rows(x_blocks, image_own)]
    attn_inputs = [
        modulate(x_all[m], factors[:, m, 0], factors[:, m, 1]).astype(bf16) for m in modalities
    ]
    packed = jnp.concatenate(
        [
            jnp.einsum("snd,de->sne", attn_inputs[m], inner_full[m], preferred_element_type=f32)
            for m in modalities
        ],
        axis=1,
    ).astype(bf16)
    mixed, log_totals = attend_forward(packed, scale)
    pieces = [mixed[:, :length_image], mixed[:, length_image:]]
    outer_terms = [
        jnp.einsum("kut,tx->kux", pieces[m], outer_full[m], preferred_element_type=f32)
        for m in modalities
    ]
    attn_branch = scatter_rows(join_slots(outer_terms[0], outer_terms[1], size), low)
    attn_branch = [attn_branch[:, :image_own], attn_branch[:, image_own:]]
    start_rows = [x_own[:, :image_own].astype(f32), x_own[:, image_own:].astype(f32)]
    middle_rows = [
        start_rows[m] + factors[:, m, 2][:, None, :] * attn_branch[m] for m in modalities
    ]
    feed_entries = [
        modulate(middle_rows[m], factors[:, m, 3], factors[:, m, 4]).astype(bf16)
        for m in modalities
    ]
    feed_inputs = split_rows(gather_rows(jnp.concatenate(feed_entries, axis=1), low), image_own)

    feed_grad = [
        (factors[:, m, 5][:, None, :] * rows.astype(f32)).astype(bf16)
        for m, rows in enumerate(split_rows(cot_blocks, image_own))
    ]
    down_terms = []
    entry_terms = []
    grad_up = []
    grad_down = []
    for m in modalities:
        hidden = jnp.einsum("snd,df->snf", feed_inputs[m], up_full[m], preferred_element_type=f32)
        active, back = gelu_parts(hidden)
        active = active.astype(bf16)
        grad_active = jnp.einsum(
            "snd,fd->snf", feed_grad[m], down_full[m], preferred_element_type=f32
        )
        grad_hidden = (grad_active * back).astype(bf16)
        entry_terms.append(
            jnp.einsum("snf,df->snd", grad_hidden, up_full[m], preferred_element_type=f32)
        )
        down_terms.append(
            jnp.einsum("snf,fd->snd", active, down_full[m], preferred_element_type=f32)
        )
        grad_down.append(
            jnp.einsum("snf,snd->fd", active, feed_grad[m], preferred_element_type=f32)
        )
        grad_up.append(
            jnp.einsum("snd,snf->df", feed_inputs[m], grad_hidden, preferred_element_type=f32)
        )
    entry_grad = scatter_rows(join_slots(entry_terms[0], entry_terms[1], size), low)
    feed_branch = scatter_rows(join_slots(down_terms[0], down_terms[1], size), low)
    grad_up = jnp.stack(grad_up).astype(bf16)
    grad_down = jnp.stack(grad_down).astype(bf16)
    down_owned = scatter_weight(grad_down)
    up_owned = scatter_weight(grad_up)

    entry_grad = [entry_grad[:, :image_own], entry_grad[:, image_own:]]
    feed_branch = [feed_branch[:, :image_own], feed_branch[:, image_own:]]
    grads = [cot_own[:, :image_own].astype(f32), cot_own[:, image_own:].astype(f32)]
    carried = [
        middle_rows[m] + factors[:, m, 5][:, None, :] * feed_branch[m] for m in modalities
    ]
    gate_two = [jnp.sum(grads[m] * feed_branch[m], axis=1) for m in modalities]
    shift_two = []
    scale_two = []
    gate_one = []
    sends = []
    for m in modalities:
        row_grad, normal = modulate_back(middle_rows[m], factors[:, m, 4], entry_grad[m])
        grads[m] = grads[m] + row_grad
        shift_two.append(jnp.sum(entry_grad[m], axis=1))
        scale_two.append(jnp.sum(entry_grad[m] * normal, axis=1))
        gate_one.append(jnp.sum(grads[m] * attn_branch[m], axis=1))
        sends.append((factors[:, m, 2][:, None, :] * grads[m]).astype(bf16))
    attn_grad = split_rows(gather_rows(jnp.concatenate(sends, axis=1), low), image_own)
    grad_mixed = jnp.concatenate(
        [
            jnp.einsum("hom,rm->hor", attn_grad[m], outer_full[m], preferred_element_type=f32)
            for m in modalities
        ],
        axis=1,
    ).astype(bf16)
    grad_outer = jnp.stack(
        [
            jnp.einsum("puj,puo->jo", pieces[m], attn_grad[m], preferred_element_type=f32)
            for m in modalities
        ]
    )
    outer_owned = scatter_weight(grad_outer)
    grad_packed = attend_backward(packed, grad_mixed, log_totals, scale)
    grad_split = [grad_packed[:, :length_image], grad_packed[:, length_image:]]
    grad_inner = jnp.stack(
        [
            jnp.einsum("snd,sne->de", attn_inputs[m], grad_split[m], preferred_element_type=f32)
            for m in modalities
        ]
    )
    inner_owned = scatter_weight(grad_inner)
    entry_terms = [
        jnp.einsum("sne,de->snd", grad_split[m], inner_full[m], preferred_element_type=f32)
        for m in modalities
    ]
    entry_grad = scatter_rows(join_slots(entry_terms[0], entry_terms[1], size), low)
    entry_grad = [entry_grad[:, :image_own], entry_grad[:, image_own:]]

    factor_terms = []
    for m in modalities:
        row_grad, normal = modulate_back(start_rows[m], factors[:, m, 1], entry_grad[m])
        grads[m] = grads[m] + row_grad
        factor_terms.append(
            jnp.stack(
                [
                    jnp.sum(entry_terms[m], axis=1),
                    jnp.sum(entry_terms[m] * layer_norm(x_all[m]), axis=1),
                    gate_one[m],
                    shift_two[m],
                    scale_two[m],
                    gate_two[m],
                ],
                axis=1,
            )
        )
    factor_sums = swap(sum_to_columns(jnp.stack(factor_terms, axis=1), GROUP, size, 3))
    factor_all = lax.all_gather(factor_sums, DP, axis=0, tiled=True)
    mod_owned = jnp.einsum("sd,szke->zdke", lifted_own.astype(f32), factor_all, precision=highest)
    lifted_terms = jnp.einsum(
        "szke,zdke->sd", factor_all, modulator.astype(f32), precision=highest
    )
    swapped = lax.all_to_all(
        lifted_terms.reshape(dp_size, seq_count, own_depth), DP, 0, 0, tiled=True
    )
    lifted_sum = jnp.moveaxis(swapped, 0, 1).reshape(seq_count, dp_size * own_depth)
    lifted_cols = sum_to_columns(lifted_sum, TENSOR, size, 1)
    columns = lifted_cols.shape[1]
    own_cond = lax.dynamic_slice_in_dim(cond_float, lax.axis_index(TENSOR) * columns, columns, 1)
    rows_out = swap(jnp.concatenate(carried, axis=1).astype(bf16))
    rows_grad = swap(jnp.concatenate(grads, axis=1).astype(bf16)).astype(f32)
    gate = jax.nn.sigmoid(own_cond)
    cond_grad = lifted_cols * (gate * (1.0 + own_cond * (1.0 - gate)))
    return (
        rows_out[:, :image_own],
        rows_out[:, image_own:],
        rows_grad[:, :image_own],
        rows_grad[:, image_own:],
        cond_grad,
        mod_owned[None],
        inner_owned.reshape(attention_in.shape),
        outer_owned[None],
        up_owned[None],
        down_owned[None],
    )


def solution(mesh):
    in_specs = (
        P(DP, TENSOR, None),
        P(DP, TENSOR, None),
        P(DP, None),
        P(None, None, DP, None, TENSOR),
        P(None, None, DP, None, TENSOR),
        P(None, None, TENSOR + DP, None),
        P(None, None, DP, TENSOR),
        P(None, None, TENSOR + DP, None),
        P(DP, TENSOR, None),
        P(DP, TENSOR, None),
    )
    out_specs = (
        P(DP, TENSOR, None),
        P(DP, TENSOR, None),
        P(DP, TENSOR, None),
        P(DP, TENSOR, None),
        P(DP, TENSOR),
        P(None, None, DP, None, TENSOR),
        P(None, None, DP, None, TENSOR),
        P(None, None, TENSOR + DP, None),
        P(None, None, DP, TENSOR),
        P(None, None, TENSOR + DP, None),
    )
    dp_size, size = mesh.shape["dp"], mesh.shape["tensor"]
    devices = mesh.devices.reshape(2, dp_size // 2, 2, size // 2)
    cut_mesh = Mesh(devices, DP + TENSOR)
    body = partial(shards, dp_size=dp_size, size=size)
    return jax.shard_map(body, mesh=cut_mesh, in_specs=in_specs, out_specs=out_specs, check_vma=False)
```

```python
from functools import partial

import jax
import jax.numpy as jnp
from jax import lax
from jax.experimental import pallas as pl
from jax.experimental.pallas import tpu as pltpu
from jax.sharding import PartitionSpec as P

HD = 64

norm_eps = 1e-06
highest = lax.Precision.HIGHEST
VMEM_LIMIT = 40 * 1024 * 1024
bf16 = jnp.bfloat16
f32 = jnp.float32


def layer_norm(rows):
    middle = jnp.mean(rows, axis=-1, keepdims=True)
    centered = rows - middle
    spread = jnp.mean(centered * centered, axis=-1, keepdims=True)
    return centered * lax.rsqrt(spread + norm_eps)


def modulate(rows, shift, scale):
    return layer_norm(rows) * (1.0 + scale[:, None, :]) + shift[:, None, :]


def modulate_back(rows, scale, grad):
    middle = jnp.mean(rows, axis=-1, keepdims=True)
    centered = rows - middle
    spread = jnp.mean(centered * centered, axis=-1, keepdims=True)
    inverse = lax.rsqrt(spread + norm_eps)
    normal = centered * inverse
    wide = grad * (1.0 + scale[:, None, :])
    first = jnp.mean(wide, axis=-1, keepdims=True)
    second = jnp.mean(wide * normal, axis=-1, keepdims=True)
    return inverse * (wide - first - normal * second), normal


def gelu_parts(hidden):
    slope = 0.7978845608028654
    square = hidden * hidden
    tail = jnp.tanh(slope * hidden * (1.0 + 0.044715 * square))
    active = 0.5 * hidden * (1.0 + tail)
    back = 0.5 * (1.0 + tail) + 0.5 * hidden * (1.0 - tail * tail) * (
        slope * (1.0 + 3.0 * 0.044715 * square)
    )
    return active, back


NT = (((1,), (1,)), ((), ()))
NN = (((1,), (0,)), ((), ()))
TN = (((0,), (0,)), ((), ()))


def product(left, right, numbers):
    return lax.dot_general(left, right, numbers, preferred_element_type=f32)


def cuts(length, step):
    return [(lower, min(lower + step, length)) for lower in range(0, length, step)]


def attend_forward_kernel(packed, mixed, totals, *, step, scale):
    length, width = mixed.shape[1:]
    for head in range(width // HD):
        lane = head * HD
        keys = packed[0, :, width + lane : width + lane + HD]
        values = packed[0, :, 2 * width + lane : 2 * width + lane + HD]
        for lower, upper in cuts(length, step):
            query = packed[0, lower:upper, lane : lane + HD] * scale
            scores = product(keys, query, NT)
            largest = jnp.max(scores, axis=0, keepdims=True)
            raised = jnp.exp(scores - largest)
            denominator = jnp.sum(raised, axis=0, keepdims=True)
            probs = (raised * (1.0 / denominator)).astype(bf16)
            mixed[0, lower:upper, lane : lane + HD] = product(probs, values, TN).astype(bf16)
            totals[0, head : head + 1, lower:upper] = largest + jnp.log(denominator)


def attend_forward(packed, scale):
    seqs, length, width = packed.shape[0], packed.shape[1], packed.shape[2] // 3
    heads = width // HD
    pairs = seqs * heads * length * length
    return pl.pallas_call(
        partial(attend_forward_kernel, step=640, scale=scale),
        grid=(seqs,),
        in_specs=[pl.BlockSpec((1, length, 3 * width), lambda s: (s, 0, 0))],
        out_specs=[
            pl.BlockSpec((1, length, width), lambda s: (s, 0, 0)),
            pl.BlockSpec((1, heads, length), lambda s: (s, 0, 0)),
        ],
        out_shape=[
            jax.ShapeDtypeStruct((seqs, length, width), bf16),
            jax.ShapeDtypeStruct((seqs, heads, length), f32),
        ],
        cost_estimate=pl.CostEstimate(
            flops=pairs * HD * 16, bytes_accessed=seqs * length * width * 8, transcendentals=pairs
        ),
        compiler_params=pltpu.CompilerParams(vmem_limit_bytes=VMEM_LIMIT),
        name="attend_forward",
    )(packed)


def attend_backward_kernel(packed, grad_mixed, totals, grad, key_sum, value_sum, *, step, scale):
    length, width = grad_mixed.shape[1:]
    for head in range(width // HD):
        lane = head * HD
        keys = packed[0, :, width + lane : width + lane + HD]
        values = packed[0, :, 2 * width + lane : 2 * width + lane + HD]
        for lower, upper in cuts(length, step):
            query = packed[0, lower:upper, lane : lane + HD] * scale
            block_grad = grad_mixed[0, lower:upper, lane : lane + HD]
            probs = jnp.exp(product(keys, query, NT) - totals[0, head : head + 1, lower:upper])
            weighted = probs * product(values, block_grad, NT)
            inner = jnp.sum(weighted, axis=0, keepdims=True)
            grad_scores = (weighted - probs * inner).astype(bf16)
            grad_values = product(probs.astype(bf16), block_grad, NN)
            grad_keys = product(grad_scores, query, NN)
            grad_query = product(grad_scores, keys, TN) * scale
            grad[0, lower:upper, lane : lane + HD] = grad_query.astype(bf16)
            if lower:
                key_sum[...] += grad_keys
                value_sum[...] += grad_values
            else:
                key_sum[...] = grad_keys
                value_sum[...] = grad_values
        grad[0, :, width + lane : width + lane + HD] = key_sum[...].astype(bf16)
        grad[0, :, 2 * width + lane : 2 * width + lane + HD] = value_sum[...].astype(bf16)


def attend_backward(packed, grad_mixed, totals, scale):
    seqs, length, width = grad_mixed.shape
    heads = width // HD
    pairs = seqs * heads * length * length
    return pl.pallas_call(
        partial(attend_backward_kernel, step=640, scale=scale),
        grid=(seqs,),
        in_specs=[
            pl.BlockSpec((1, length, 3 * width), lambda s: (s, 0, 0)),
            pl.BlockSpec((1, length, width), lambda s: (s, 0, 0)),
            pl.BlockSpec((1, heads, length), lambda s: (s, 0, 0)),
        ],
        out_specs=pl.BlockSpec((1, length, 3 * width), lambda s: (s, 0, 0)),
        out_shape=jax.ShapeDtypeStruct((seqs, length, 3 * width), bf16),
        scratch_shapes=[pltpu.VMEM((length, HD), f32), pltpu.VMEM((length, HD), f32)],
        cost_estimate=pl.CostEstimate(
            flops=pairs * HD * 32, bytes_accessed=seqs * length * width * 14, transcendentals=pairs
        ),
        compiler_params=pltpu.CompilerParams(vmem_limit_bytes=VMEM_LIMIT),
        name="attend_backward",
    )(packed, grad_mixed, totals)


def weight_grad_kernel(image_left, text_left, image_right, text_right, *rest):
    out = rest[-1]

    def total(left, right):
        value = product(left[0], right[0], TN)
        for seq in range(1, left.shape[0]):
            value = value + product(left[seq], right[seq], TN)
        return value.astype(bf16)

    @pl.when(pl.program_id(0) == 0)
    def _():
        out[0] = total(image_left, image_right)

    @pl.when(pl.program_id(0) == 1)
    def _():
        out[0] = total(text_left, text_right)


def weight_grad(lefts, rights, slots=2, place=0, into=None):
    seqs, image_rows, depth = lefts[0].shape
    text_rows = lefts[1].shape[1]
    width = rights[0].shape[2]
    tile = 768 if depth % 768 == 0 else 384 if depth % 384 == 0 else depth
    tiles = depth // tile
    operands = [*lefts, *rights]
    in_specs = [
        pl.BlockSpec((seqs, image_rows, tile), lambda z, j: (0, 0, jnp.where(z == 0, j, tiles - 1))),
        pl.BlockSpec((seqs, text_rows, tile), lambda z, j: (0, 0, jnp.where(z == 1, j, 0))),
        pl.BlockSpec((seqs, image_rows, width), lambda z, j: (0, 0, 0)),
        pl.BlockSpec((seqs, text_rows, width), lambda z, j: (0, 0, 0)),
    ]
    aliases = {}
    if into is not None:
        aliases = {len(operands): 0}
        operands.append(into)
        in_specs.append(pl.BlockSpec(memory_space=pl.ANY))
    rows = seqs * (image_rows + text_rows)
    return pl.pallas_call(
        weight_grad_kernel,
        grid=(2, tiles),
        in_specs=in_specs,
        out_specs=pl.BlockSpec((1, tile, width), lambda z, j: (z + place, j, 0)),
        out_shape=jax.ShapeDtypeStruct((slots, depth, width), bf16),
        input_output_aliases=aliases,
        cost_estimate=pl.CostEstimate(
            flops=2 * rows * depth * width,
            bytes_accessed=2 * (rows * (depth + width) + 2 * depth * width),
            transcendentals=0,
        ),
        compiler_params=pltpu.CompilerParams(vmem_limit_bytes=VMEM_LIMIT),
        name="weight_grad",
    )(*operands)


def ring_pairs(size):
    order = list(range(0, size, 2)) + list(range(size - 1, 0, -2)) if size != 4 else [0, 1, 3, 2]
    if size == 1:
        order = [0]
    return [(order[place], order[(place + 1) % size]) for place in range(size)]


def ring_gather(block, size):
    pairs = ring_pairs(size)
    blocks = [block]
    for step in range(size - 1):
        blocks.append(lax.ppermute(blocks[-1], "tensor", pairs))
    return blocks


def tie(value, other):
    return lax.optimization_barrier((value, other))


def ring_places(size):
    before = {target: source for source, target in ring_pairs(size)}
    tables = [list(range(size))]
    for step in range(size - 1):
        tables.append([before[place] for place in tables[-1]])
    index = lax.axis_index("tensor")
    return [jnp.asarray(table, jnp.int32)[index] for table in tables]


def ring_add(total, part):
    pairs = ring_pairs(lax.axis_size("tensor"))
    return lax.ppermute(total, "tensor", pairs).astype(f32) + part.astype(f32)


def ring_scatter(parts, size):
    pairs = ring_pairs(size)
    if size == 1:
        return parts[0].astype(f32)
    total = parts[1].astype(bf16)
    for slot in list(range(2, size)) + [0]:
        total = lax.ppermute(total, "tensor", pairs).astype(f32) + parts[slot].astype(f32)
        if slot:
            total = total.astype(bf16)
    return total


def split_rows(blocks, count):
    return [
        jnp.concatenate([block[:, :count] for block in blocks], axis=1),
        jnp.concatenate([block[:, count:] for block in blocks], axis=1),
    ]


def join_slots(image, text, size):
    image_rows = image.shape[1] // size
    text_rows = text.shape[1] // size
    return [
        jnp.concatenate(
            [
                image[:, slot * image_rows : (slot + 1) * image_rows],
                text[:, slot * text_rows : (slot + 1) * text_rows],
            ],
            axis=1,
        )
        for slot in range(size)
    ]


def gather_weight(weight):
    return lax.all_gather(weight, "dp", axis=1, tiled=True)


def scatter_weight(grad):
    return lax.psum_scatter(grad, "dp", scatter_dimension=1, tiled=True)


def sum_to_columns(value, axis_name, size, axis):
    shape = value.shape
    cut = value.reshape(shape[:axis] + (size, shape[axis] // size) + shape[axis + 1 :])
    cut = jnp.moveaxis(cut, axis, 0)
    return jnp.sum(lax.all_to_all(cut, axis_name, 0, 0, tiled=True), axis=0)


def shards(
    image_rows,
    text_rows,
    conditioning,
    modulator,
    attention_in,
    attention_out,
    up_weight,
    down_weight,
    image_cotangent,
    text_cotangent,
    dp_size,
    size,
):
    scale = HD ** (-0.5)
    modalities = range(2)
    modulator = modulator[0]
    seq_count, image_own = image_rows.shape[:2]
    length_image = image_own * size

    cond_float = conditioning.astype(f32)
    lifted = jax.nn.silu(cond_float).astype(bf16)

    inner_full = gather_weight(attention_in[0].reshape(2, attention_in.shape[2], -1))
    x_blocks = ring_gather(jnp.concatenate([image_rows, text_rows], axis=1), size)

    lifted, x_blocks[1] = tie(lifted, x_blocks[1])
    lifted_all = lax.all_gather(lifted, "dp", axis=0, tiled=True)
    outer_local, lifted_all = tie(attention_out[0], lifted_all)
    outer_full = gather_weight(outer_local)
    own_depth = modulator.shape[1]
    lifted_own = lax.dynamic_slice_in_dim(
        lifted_all, lax.axis_index("dp") * own_depth, own_depth, 1
    )
    factor_terms = jnp.einsum("sd,zdke->szke", lifted_own, modulator, preferred_element_type=f32)
    factor_terms, x_blocks[2 % size] = tie(factor_terms, x_blocks[2 % size])
    factor_cols = sum_to_columns(factor_terms, "dp", dp_size, 0)
    factor_cols, x_blocks[-1] = tie(factor_cols, x_blocks[-1])
    cotangents, x_blocks[-1] = tie(
        jnp.concatenate([image_cotangent, text_cotangent], axis=1), x_blocks[-1]
    )
    cotangents = lax.all_gather(cotangents, "tensor", axis=1)
    factors = lax.all_gather(factor_cols, "tensor", axis=3, tiled=True)
    up_local, factors = tie(up_weight[0], factors)
    up_full = gather_weight(up_local)
    down_local, factors = tie(down_weight[0], factors)
    down_full = gather_weight(down_local)
    cot_blocks = [
        lax.dynamic_index_in_dim(cotangents, place, 1, keepdims=False)
        for place in ring_places(size)
    ]

    x_all = [rows.astype(f32) for rows in split_rows(x_blocks, image_own)]
    attn_inputs = [
        modulate(x_all[m], factors[:, m, 0], factors[:, m, 1]).astype(bf16) for m in modalities
    ]
    packed = jnp.concatenate(
        [
            jnp.einsum("snd,de->sne", attn_inputs[m], inner_full[m], preferred_element_type=f32)
            for m in modalities
        ],
        axis=1,
    ).astype(bf16)
    mixed, log_totals = attend_forward(packed, scale)
    pieces = [mixed[:, :length_image], mixed[:, length_image:]]
    outer_terms = [
        jnp.einsum("kut,tx->kux", pieces[m], outer_full[m], preferred_element_type=f32)
        for m in modalities
    ]
    attn_branch = ring_scatter(join_slots(outer_terms[0], outer_terms[1], size), size)
    attn_branch = [attn_branch[:, :image_own], attn_branch[:, image_own:]]
    start_rows = [image_rows.astype(f32), text_rows.astype(f32)]
    middle_rows = [
        start_rows[m] + factors[:, m, 2][:, None, :] * attn_branch[m] for m in modalities
    ]
    feed_entries = [
        modulate(middle_rows[m], factors[:, m, 3], factors[:, m, 4]).astype(bf16)
        for m in modalities
    ]
    feed_inputs = split_rows(ring_gather(jnp.concatenate(feed_entries, axis=1), size), image_own)

    feed_grad = [
        (factors[:, m, 5][:, None, :] * rows.astype(f32)).astype(bf16)
        for m, rows in enumerate(split_rows(cot_blocks, image_own))
    ]
    down_terms = []
    entry_terms = []
    actives = []
    grad_hiddens = []
    for m in modalities:
        hidden = jnp.einsum("snd,df->snf", feed_inputs[m], up_full[m], preferred_element_type=f32)
        active, back = gelu_parts(hidden)
        active = active.astype(bf16)
        grad_active = jnp.einsum(
            "snd,fd->snf", feed_grad[m], down_full[m], preferred_element_type=f32
        )
        grad_hidden = (grad_active * back).astype(bf16)
        entry_terms.append(
            jnp.einsum("snf,df->snd", grad_hidden, up_full[m], preferred_element_type=f32)
        )
        down_terms.append(
            jnp.einsum("snf,fd->snd", active, down_full[m], preferred_element_type=f32)
        )
        actives.append(active)
        grad_hiddens.append(grad_hidden)
    entry_slots = join_slots(entry_terms[0], entry_terms[1], size)
    entry_slots[1], grad_hiddens[0], actives[0] = lax.optimization_barrier(
        (entry_slots[1].astype(bf16), grad_hiddens[0], actives[0])
    )
    entry_grad = ring_scatter(entry_slots, size)
    if up_full.shape == down_full.shape:
        grad_feed = weight_grad(actives, feed_grad, 4, 2)
        grad_feed = weight_grad(feed_inputs, grad_hiddens, 4, 0, grad_feed)
        feed_owned = [scatter_weight(grad_feed)]
    else:
        feed_owned = [
            scatter_weight(weight_grad(feed_inputs, grad_hiddens)),
            scatter_weight(weight_grad(actives, feed_grad)),
        ]
    entry_grad = [entry_grad[:, :image_own], entry_grad[:, image_own:]]
    grads = [image_cotangent.astype(f32), text_cotangent.astype(f32)]
    cots = list(grads)
    shift_two = []
    scale_two = []
    gate_one = []
    sends = []
    for m in modalities:
        row_grad, normal = modulate_back(middle_rows[m], factors[:, m, 4], entry_grad[m])
        grads[m] = grads[m] + row_grad
        shift_two.append(jnp.sum(entry_grad[m], axis=1))
        scale_two.append(jnp.sum(entry_grad[m] * normal, axis=1))
        gate_one.append(jnp.sum(grads[m] * attn_branch[m], axis=1))
        sends.append((factors[:, m, 2][:, None, :] * grads[m]).astype(bf16))
    attn_blocks = ring_gather(jnp.concatenate(sends, axis=1), size)
    attn_grad = split_rows(attn_blocks, image_own)
    feed_slots = join_slots(down_terms[0], down_terms[1], size)
    feed_slots[1], last_block = tie(feed_slots[1].astype(bf16), attn_blocks[-1])
    late_grad = split_rows(attn_blocks[:-1] + [last_block], image_own)
    grad_mixed = jnp.concatenate(
        [
            jnp.einsum("hom,rm->hor", attn_grad[m], outer_full[m], preferred_element_type=f32)
            for m in modalities
        ],
        axis=1,
    ).astype(bf16)
    grad_outer, feed_owned = tie(weight_grad(pieces, late_grad), feed_owned)
    outer_owned = scatter_weight(grad_outer)
    grad_packed = attend_backward(packed, grad_mixed, log_totals, scale)
    feed_total = ring_add(feed_slots[1], feed_slots[2]).astype(bf16)
    feed_total, grad_packed = tie(feed_total, grad_packed)
    grad_split = [grad_packed[:, :length_image], grad_packed[:, length_image:]]
    grad_inner, outer_owned = tie(weight_grad(attn_inputs, grad_split), outer_owned)
    grad_inner, grad_split[0] = tie(grad_inner, grad_split[0])
    inner_owned = scatter_weight(grad_inner)
    entry_terms = [
        jnp.einsum("sne,de->snd", grad_split[m], inner_full[m], preferred_element_type=f32)
        for m in modalities
    ]
    entry_slots = join_slots(entry_terms[0], entry_terms[1], size)
    feed_total = ring_add(feed_total, feed_slots[3 % size])
    if size > 3:
        feed_total = feed_total.astype(bf16)
    entry_slots[1], entry_terms[0], feed_total = lax.optimization_barrier(
        (entry_slots[1].astype(bf16), entry_terms[0], feed_total)
    )
    entry_grad = ring_scatter(entry_slots, size)
    entry_grad = [entry_grad[:, :image_own], entry_grad[:, image_own:]]

    for slot in list(range(4, size)) + [0]:
        feed_total = ring_add(feed_total.astype(bf16), feed_slots[slot])
    feed_branch = feed_total
    feed_branch = [feed_branch[:, :image_own], feed_branch[:, image_own:]]
    carried = [
        middle_rows[m] + factors[:, m, 5][:, None, :] * feed_branch[m] for m in modalities
    ]
    gate_two = [jnp.sum(cots[m] * feed_branch[m], axis=1) for m in modalities]
    if len(feed_owned) == 1:
        feed_owned = [feed_owned[0][:2], feed_owned[0][2:]]
    factor_terms = []
    for m in modalities:
        row_grad, normal = modulate_back(start_rows[m], factors[:, m, 1], entry_grad[m])
        grads[m] = grads[m] + row_grad
        factor_terms.append(
            jnp.stack(
                [
                    jnp.sum(entry_terms[m], axis=1),
                    jnp.sum(entry_terms[m] * layer_norm(x_all[m]), axis=1),
                    gate_one[m],
                    shift_two[m],
                    scale_two[m],
                    gate_two[m],
                ],
                axis=1,
            )
        )
    factor_sums = sum_to_columns(jnp.stack(factor_terms, axis=1), "tensor", size, 3)
    factor_all = lax.all_gather(factor_sums, "dp", axis=0, tiled=True)
    mod_owned = jnp.einsum("sd,szke->zdke", lifted_own.astype(f32), factor_all, precision=highest)
    lifted_terms = jnp.einsum(
        "szke,zdke->sd", factor_all, modulator.astype(f32), precision=highest
    )
    swapped = lax.all_to_all(
        lifted_terms.reshape(dp_size, seq_count, own_depth), "dp", 0, 0, tiled=True
    )
    lifted_sum = jnp.moveaxis(swapped, 0, 1).reshape(seq_count, dp_size * own_depth)
    lifted_cols = sum_to_columns(lifted_sum, "tensor", size, 1)
    columns = lifted_cols.shape[1]
    own_cond = lax.dynamic_slice_in_dim(cond_float, lax.axis_index("tensor") * columns, columns, 1)
    gate = jax.nn.sigmoid(own_cond)
    cond_grad = lifted_cols * (gate * (1.0 + own_cond * (1.0 - gate)))
    return (
        carried[0].astype(bf16),
        carried[1].astype(bf16),
        grads[0],
        grads[1],
        cond_grad,
        mod_owned[None],
        inner_owned.reshape(attention_in.shape).astype(f32),
        outer_owned[None].astype(f32),
        feed_owned[0][None].astype(f32),
        feed_owned[1][None].astype(f32),
    )


def solution(mesh):
    in_specs = (
        P("dp", "tensor", None),
        P("dp", "tensor", None),
        P("dp", None),
        P(None, None, "dp", None, "tensor"),
        P(None, None, "dp", None, "tensor"),
        P(None, None, ("tensor", "dp"), None),
        P(None, None, "dp", "tensor"),
        P(None, None, ("tensor", "dp"), None),
        P("dp", "tensor", None),
        P("dp", "tensor", None),
    )
    out_specs = (
        P("dp", "tensor", None),
        P("dp", "tensor", None),
        P("dp", "tensor", None),
        P("dp", "tensor", None),
        P("dp", "tensor"),
        P(None, None, "dp", None, "tensor"),
        P(None, None, "dp", None, "tensor"),
        P(None, None, ("tensor", "dp"), None),
        P(None, None, "dp", "tensor"),
        P(None, None, ("tensor", "dp"), None),
    )
    body = partial(shards, dp_size=mesh.shape["dp"], size=mesh.shape["tensor"])
    return jax.shard_map(body, mesh=mesh, in_specs=in_specs, out_specs=out_specs, check_vma=False)
```

```python
from functools import partial

import jax
import jax.numpy as jnp
from jax import lax
from jax.experimental import pallas as pl
from jax.experimental.pallas import tpu as pltpu
from jax.sharding import PartitionSpec as P

HD = 64

norm_eps = 1e-06
highest = lax.Precision.HIGHEST
VMEM_LIMIT = 40 * 1024 * 1024
bf16 = jnp.bfloat16
f32 = jnp.float32


def layer_norm(rows):
    middle = jnp.mean(rows, axis=-1, keepdims=True)
    centered = rows - middle
    spread = jnp.mean(centered * centered, axis=-1, keepdims=True)
    return centered * lax.rsqrt(spread + norm_eps)


def modulate(rows, shift, scale):
    return layer_norm(rows) * (1.0 + scale[:, None, :]) + shift[:, None, :]


def modulate_back(rows, scale, grad):
    middle = jnp.mean(rows, axis=-1, keepdims=True)
    centered = rows - middle
    spread = jnp.mean(centered * centered, axis=-1, keepdims=True)
    inverse = lax.rsqrt(spread + norm_eps)
    normal = centered * inverse
    wide = grad * (1.0 + scale[:, None, :])
    first = jnp.mean(wide, axis=-1, keepdims=True)
    second = jnp.mean(wide * normal, axis=-1, keepdims=True)
    return inverse * (wide - first - normal * second), normal


def gelu_parts(hidden):
    slope = 0.7978845608028654
    square = hidden * hidden
    tail = jnp.tanh(slope * hidden * (1.0 + 0.044715 * square))
    active = 0.5 * hidden * (1.0 + tail)
    back = 0.5 * (1.0 + tail) + 0.5 * hidden * (1.0 - tail * tail) * (
        slope * (1.0 + 3.0 * 0.044715 * square)
    )
    return active, back


NT = (((1,), (1,)), ((), ()))
NN = (((1,), (0,)), ((), ()))
TN = (((0,), (0,)), ((), ()))


def product(left, right, numbers):
    return lax.dot_general(left, right, numbers, preferred_element_type=f32)


def cuts(length, step):
    return [(lower, min(lower + step, length)) for lower in range(0, length, step)]


def attend_forward_kernel(packed, mixed, totals, *, step, scale):
    length, width = mixed.shape[1:]
    for head in range(width // HD):
        lane = head * HD
        keys = packed[0, :, width + lane : width + lane + HD]
        values = packed[0, :, 2 * width + lane : 2 * width + lane + HD]
        for lower, upper in cuts(length, step):
            query = packed[0, lower:upper, lane : lane + HD] * scale
            scores = product(keys, query, NT)
            largest = jnp.max(scores, axis=0, keepdims=True)
            raised = jnp.exp(scores - largest)
            denominator = jnp.sum(raised, axis=0, keepdims=True)
            probs = (raised * (1.0 / denominator)).astype(bf16)
            mixed[0, lower:upper, lane : lane + HD] = product(probs, values, TN).astype(bf16)
            totals[0, head : head + 1, lower:upper] = largest + jnp.log(denominator)


def attend_forward(packed, scale):
    seqs, length, width = packed.shape[0], packed.shape[1], packed.shape[2] // 3
    heads = width // HD
    pairs = seqs * heads * length * length
    return pl.pallas_call(
        partial(attend_forward_kernel, step=640, scale=scale),
        grid=(seqs,),
        in_specs=[pl.BlockSpec((1, length, 3 * width), lambda s: (s, 0, 0))],
        out_specs=[
            pl.BlockSpec((1, length, width), lambda s: (s, 0, 0)),
            pl.BlockSpec((1, heads, length), lambda s: (s, 0, 0)),
        ],
        out_shape=[
            jax.ShapeDtypeStruct((seqs, length, width), bf16),
            jax.ShapeDtypeStruct((seqs, heads, length), f32),
        ],
        cost_estimate=pl.CostEstimate(
            flops=pairs * HD * 16, bytes_accessed=seqs * length * width * 8, transcendentals=pairs
        ),
        compiler_params=pltpu.CompilerParams(vmem_limit_bytes=VMEM_LIMIT),
        name="attend_forward",
    )(packed)


def attend_backward_kernel(packed, grad_mixed, totals, grad, key_sum, value_sum, *, step, scale):
    length, width = grad_mixed.shape[1:]
    for head in range(width // HD):
        lane = head * HD
        keys = packed[0, :, width + lane : width + lane + HD]
        values = packed[0, :, 2 * width + lane : 2 * width + lane + HD]
        for lower, upper in cuts(length, step):
            query = packed[0, lower:upper, lane : lane + HD] * scale
            block_grad = grad_mixed[0, lower:upper, lane : lane + HD]
            probs = jnp.exp(product(keys, query, NT) - totals[0, head : head + 1, lower:upper])
            weighted = probs * product(values, block_grad, NT)
            inner = jnp.sum(weighted, axis=0, keepdims=True)
            grad_scores = (weighted - probs * inner).astype(bf16)
            grad_values = product(probs.astype(bf16), block_grad, NN)
            grad_keys = product(grad_scores, query, NN)
            grad_query = product(grad_scores, keys, TN) * scale
            grad[0, lower:upper, lane : lane + HD] = grad_query.astype(bf16)
            if lower:
                key_sum[...] += grad_keys
                value_sum[...] += grad_values
            else:
                key_sum[...] = grad_keys
                value_sum[...] = grad_values
        grad[0, :, width + lane : width + lane + HD] = key_sum[...].astype(bf16)
        grad[0, :, 2 * width + lane : 2 * width + lane + HD] = value_sum[...].astype(bf16)


def attend_backward(packed, grad_mixed, totals, scale):
    seqs, length, width = grad_mixed.shape
    heads = width // HD
    pairs = seqs * heads * length * length
    return pl.pallas_call(
        partial(attend_backward_kernel, step=640, scale=scale),
        grid=(seqs,),
        in_specs=[
            pl.BlockSpec((1, length, 3 * width), lambda s: (s, 0, 0)),
            pl.BlockSpec((1, length, width), lambda s: (s, 0, 0)),
            pl.BlockSpec((1, heads, length), lambda s: (s, 0, 0)),
        ],
        out_specs=pl.BlockSpec((1, length, 3 * width), lambda s: (s, 0, 0)),
        out_shape=jax.ShapeDtypeStruct((seqs, length, 3 * width), bf16),
        scratch_shapes=[pltpu.VMEM((length, HD), f32), pltpu.VMEM((length, HD), f32)],
        cost_estimate=pl.CostEstimate(
            flops=pairs * HD * 32, bytes_accessed=seqs * length * width * 14, transcendentals=pairs
        ),
        compiler_params=pltpu.CompilerParams(vmem_limit_bytes=VMEM_LIMIT),
        name="attend_backward",
    )(packed, grad_mixed, totals)


def weight_grad_kernel(*refs, terms):
    out = refs[-1]

    def total(pairs):
        value = None
        for (left, left_rows), (right, right_rows) in pairs:
            for seq in range(refs[left].shape[0]):
                term = product(
                    refs[left][seq, left_rows[0] : left_rows[1]],
                    refs[right][seq, right_rows[0] : right_rows[1]],
                    TN,
                )
                value = term if value is None else value + term
        return value.astype(bf16)

    for modality in range(2):

        @pl.when(pl.program_id(0) == modality)
        def _(pairs=terms[modality]):
            out[0] = total(pairs)


def rows_of(array, lower=0, upper=None):
    return (array, (lower, array.shape[1] if upper is None else upper))


def weight_grad(terms, slots=2, place=0, into=None):
    depth, width = terms[0][0][0][0].shape[2], terms[0][0][1][0].shape[2]
    tile = 768 if depth % 768 == 0 else 384 if depth % 384 == 0 else depth
    tiles = depth // tile
    operands, in_specs, found, numbered, rows = [], [], {}, [], 0
    for modality, pairs in enumerate(terms):
        numbered.append([])
        for pair in pairs:
            numbers = []
            for side, (array, window) in enumerate(pair):
                key = (id(array), side)
                if key not in found:
                    found[key] = len(operands)
                    operands.append(array)
                    both = all(
                        any(entry[side][0] is array for entry in other) for other in terms
                    )
                    if side:
                        spec = pl.BlockSpec(array.shape[:2] + (width,), lambda z, j: (0, 0, 0))
                    elif both:
                        spec = pl.BlockSpec(array.shape[:2] + (tile,), lambda z, j: (0, 0, j))
                    elif modality == 0:
                        spec = pl.BlockSpec(
                            array.shape[:2] + (tile,),
                            lambda z, j: (0, 0, jnp.where(z == 0, j, tiles - 1)),
                        )
                    else:
                        spec = pl.BlockSpec(
                            array.shape[:2] + (tile,),
                            lambda z, j: (0, 0, jnp.where(z == 1, j, 0)),
                        )
                    in_specs.append(spec)
                numbers.append((found[key], window))
            rows += array.shape[0] * (window[1] - window[0])
            numbered[-1].append(tuple(numbers))
    aliases = {}
    if into is not None:
        aliases = {len(operands): 0}
        operands.append(into)
        in_specs.append(pl.BlockSpec(memory_space=pl.ANY))
    return pl.pallas_call(
        partial(weight_grad_kernel, terms=numbered),
        grid=(2, tiles),
        in_specs=in_specs,
        out_specs=pl.BlockSpec((1, tile, width), lambda z, j: (z + place, j, 0)),
        out_shape=jax.ShapeDtypeStruct((slots, depth, width), bf16),
        input_output_aliases=aliases,
        cost_estimate=pl.CostEstimate(
            flops=2 * rows * depth * width,
            bytes_accessed=2 * (rows * (depth + width) + 2 * depth * width),
            transcendentals=0,
        ),
        compiler_params=pltpu.CompilerParams(vmem_limit_bytes=VMEM_LIMIT),
        name="weight_grad",
    )(*operands)


def feed_block_kernel(rows, grads, up, down, active, hidden_grad, entry, feed, entry_sum, feed_sum):
    place, last = pl.program_id(1), pl.num_programs(1) - 1
    upper, lower = up[0], down[0]
    hidden = product(rows[0], upper, NN)
    block_active, back = gelu_parts(hidden)
    block_active = block_active.astype(bf16)
    active[0] = block_active
    block_grad = (product(grads[0], lower, NT) * back).astype(bf16)
    hidden_grad[0] = block_grad
    entry_term = product(block_grad, upper, NT)
    feed_term = product(block_active, lower, NN)

    @pl.when(place == 0)
    def _():
        entry_sum[...] = entry_term
        feed_sum[...] = feed_term

    @pl.when(place > 0)
    def _():
        entry_sum[...] += entry_term
        feed_sum[...] += feed_term

    @pl.when(place == last)
    def _():
        entry[0] = entry_sum[...].astype(bf16)
        feed[0] = feed_sum[...].astype(bf16)


def feed_block(rows, grads, up_planes, down_planes, modality):
    (up, up_first), (down, down_first) = up_planes, down_planes
    seqs, count, depth = rows.shape
    width = up.shape[2]
    tile = next(step for step in (768, 512, 384, 256, 128, width) if width % step == 0)
    whole = pl.BlockSpec((1, count, depth), lambda s, f: (s, 0, 0))
    part = pl.BlockSpec((1, count, tile), lambda s, f: (s, 0, f))
    shapes = [jax.ShapeDtypeStruct((seqs, count, size), bf16) for size in (width, width, depth, depth)]
    return pl.pallas_call(
        feed_block_kernel,
        grid=(seqs, width // tile),
        in_specs=[
            whole,
            whole,
            pl.BlockSpec((1, depth, tile), lambda s, f: (up_first + modality, 0, f)),
            pl.BlockSpec((1, tile, depth), lambda s, f: (down_first + modality, f, 0)),
        ],
        out_specs=[part, part, whole, whole],
        out_shape=shapes,
        scratch_shapes=[pltpu.VMEM((count, depth), f32), pltpu.VMEM((count, depth), f32)],
        cost_estimate=pl.CostEstimate(
            flops=8 * seqs * count * depth * width,
            bytes_accessed=4 * depth * width + 8 * seqs * count * (depth + width),
            transcendentals=seqs * count * width,
        ),
        compiler_params=pltpu.CompilerParams(vmem_limit_bytes=VMEM_LIMIT),
        name="feed_block",
    )(rows, grads, up, down)


def ring_pairs(size):
    order = list(range(0, size, 2)) + list(range(size - 1, 0, -2)) if size != 4 else [0, 1, 3, 2]
    if size == 1:
        order = [0]
    return [(order[place], order[(place + 1) % size]) for place in range(size)]


def ring_gather(block, size):
    pairs = ring_pairs(size)
    blocks = [block]
    for step in range(size - 1):
        blocks.append(lax.ppermute(blocks[-1], "tensor", pairs))
    return blocks


def tie(value, other):
    return lax.optimization_barrier((value, other))


def ring_add(total, part):
    pairs = ring_pairs(lax.axis_size("tensor"))
    return lax.ppermute(total, "tensor", pairs).astype(f32) + part.astype(f32)


def ring_scatter_pair(image, text, size, fence, at):
    pairs = ring_pairs(size)
    image_total, text_total = image[1].astype(bf16), text[1].astype(bf16)
    for step, slot in enumerate(list(range(2, size)) + [0]):
        if step == at:
            image_total, text_total = tie(image_total, text_total)
        image_next = lax.ppermute(image_total, "tensor", pairs).astype(f32)
        text_next = lax.ppermute(text_total, "tensor", pairs)
        if step == at:
            text_next, *fence = lax.optimization_barrier((text_next, *fence))
        image_total = image_next + image[slot].astype(f32)
        text_total = text_next.astype(f32) + text[slot].astype(f32)
        if slot:
            image_total, text_total = image_total.astype(bf16), text_total.astype(bf16)
    return [image_total, text_total], fence


def ring_scatter(parts, size):
    pairs = ring_pairs(size)
    if size == 1:
        return parts[0].astype(f32)
    total = parts[1].astype(bf16)
    for slot in list(range(2, size)) + [0]:
        total = lax.ppermute(total, "tensor", pairs).astype(f32) + parts[slot].astype(f32)
        if slot:
            total = total.astype(bf16)
    return total


def split_rows(blocks, count):
    return [
        jnp.concatenate([block[:, :count] for block in blocks], axis=1),
        jnp.concatenate([block[:, count:] for block in blocks], axis=1),
    ]


def join_slots(image, text, size):
    image_rows = image.shape[1] // size
    text_rows = text.shape[1] // size
    return [
        jnp.concatenate(
            [
                image[:, slot * image_rows : (slot + 1) * image_rows],
                text[:, slot * text_rows : (slot + 1) * text_rows],
            ],
            axis=1,
        )
        for slot in range(size)
    ]


def cut_rows(value, size):
    count = value.shape[1] // size
    return [value[:, slot * count : (slot + 1) * count] for slot in range(size)]


def gather_weight(weight):
    return lax.all_gather(weight, "dp", axis=1, tiled=True)


def scatter_weight(grad):
    return lax.psum_scatter(grad, "dp", scatter_dimension=1, tiled=True)


def sum_to_columns(value, axis_name, size, axis):
    shape = value.shape
    cut = value.reshape(shape[:axis] + (size, shape[axis] // size) + shape[axis + 1 :])
    cut = jnp.moveaxis(cut, axis, 0)
    return jnp.sum(lax.all_to_all(cut, axis_name, 0, 0, tiled=True), axis=0)


def shards(
    image_rows,
    text_rows,
    conditioning,
    modulator,
    attention_in,
    attention_out,
    up_weight,
    down_weight,
    image_cotangent,
    text_cotangent,
    dp_size,
    size,
):
    scale = HD ** (-0.5)
    modalities = range(2)
    modulator = modulator[0]
    seq_count, image_own = image_rows.shape[:2]
    length_image = image_own * size

    cond_float = conditioning.astype(f32)
    lifted = jax.nn.silu(cond_float).astype(bf16)

    inner_full = gather_weight(attention_in[0].reshape(2, attention_in.shape[2], -1))
    pairs = ring_pairs(size)
    x_blocks = [jnp.concatenate([image_rows, text_rows], axis=1)]
    x_blocks.append(lax.ppermute(x_blocks[0], "tensor", pairs))

    lifted_all = lax.all_gather(lifted, "dp", axis=0, tiled=True)
    outer_local, lifted_all = tie(attention_out[0], lifted_all)
    outer_full = gather_weight(outer_local)
    own_depth = modulator.shape[1]
    lifted_own = lax.dynamic_slice_in_dim(
        lifted_all, lax.axis_index("dp") * own_depth, own_depth, 1
    )
    factor_terms = jnp.einsum("sd,zdke->szke", lifted_own, modulator, preferred_element_type=f32)
    factor_cols = sum_to_columns(factor_terms, "dp", dp_size, 0)
    x_blocks[1], factor_cols = tie(x_blocks[1], factor_cols)
    x_blocks.append(lax.ppermute(x_blocks[1], "tensor", pairs))
    factors = lax.all_gather(factor_cols, "tensor", axis=3, tiled=True)
    x_blocks[2], factors = tie(x_blocks[2], factors)
    for step in range(3, size):
        x_blocks.append(lax.ppermute(x_blocks[-1], "tensor", pairs))
    x_blocks = x_blocks[:size]
    cotangent, up_local, down_local, x_blocks[-1] = lax.optimization_barrier(
        (
            jnp.concatenate([image_cotangent, text_cotangent], axis=1),
            up_weight[0],
            down_weight[0],
            x_blocks[-1],
        )
    )
    if up_local.shape == down_local.shape:
        weights = gather_weight(jnp.concatenate([up_local, down_local], axis=0))
        up_full, down_full = (weights, 0), (weights, 2)
    else:
        up_full, down_full = (gather_weight(up_local), 0), (gather_weight(down_local), 0)
    cot_blocks = [cotangent, lax.ppermute(cotangent, "tensor", ring_pairs(size))]
    x_all = [rows.astype(f32) for rows in split_rows(x_blocks, image_own)]
    attn_inputs = [
        modulate(x_all[m], factors[:, m, 0], factors[:, m, 1]).astype(bf16) for m in modalities
    ]
    packed = jnp.concatenate(
        [
            jnp.einsum("snd,de->sne", attn_inputs[m], inner_full[m], preferred_element_type=f32)
            for m in modalities
        ],
        axis=1,
    ).astype(bf16)
    cot_blocks[1], packed = tie(cot_blocks[1], packed)
    cot_blocks.append(lax.ppermute(cot_blocks[1], "tensor", ring_pairs(size)))
    mixed, log_totals = attend_forward(packed, scale)
    cot_blocks[2], mixed = tie(cot_blocks[2], mixed)
    for step in range(3, size):
        cot_blocks.append(lax.ppermute(cot_blocks[-1], "tensor", ring_pairs(size)))
    cot_blocks = cot_blocks[:size]
    pieces = [mixed[:, :length_image], mixed[:, length_image:]]
    outer_terms = [
        jnp.einsum("kut,tx->kux", pieces[m], outer_full[m], preferred_element_type=f32)
        for m in modalities
    ]
    outer_slots = join_slots(outer_terms[0], outer_terms[1], size)
    attn_total = ring_add(outer_slots[1].astype(bf16), outer_slots[2 % size])
    attn_total, cot_blocks[-1] = tie(attn_total, cot_blocks[-1])
    for slot in list(range(3, size)) + [0] * (size > 2):
        attn_total = ring_add(attn_total.astype(bf16), outer_slots[slot])
    attn_branch = attn_total
    attn_branch = [attn_branch[:, :image_own], attn_branch[:, image_own:]]
    start_rows = [image_rows.astype(f32), text_rows.astype(f32)]
    middle_rows = [
        start_rows[m] + factors[:, m, 2][:, None, :] * attn_branch[m] for m in modalities
    ]
    feed_entries = [
        modulate(middle_rows[m], factors[:, m, 3], factors[:, m, 4]).astype(bf16)
        for m in modalities
    ]
    if up_weight.shape == down_weight.shape:
        weights, feed_entries[0] = tie(weights, feed_entries[0])
        up_full, down_full = (weights, 0), (weights, 2)
    text_entries = jnp.concatenate(ring_gather(feed_entries[1], size), axis=1)
    image_entries = [feed_entries[0], lax.ppermute(feed_entries[0], "tensor", pairs)]
    text_cot = jnp.concatenate([block[:, image_own:] for block in cot_blocks], axis=1)
    text_send = (factors[:, 1, 5][:, None, :] * text_cot.astype(f32)).astype(bf16)
    image_sends = [
        (factors[:, 0, 5][:, None, :] * block[:, :image_own].astype(f32)).astype(bf16)
        for block in cot_blocks
    ]
    image_feeds = []
    for slot in range(size):
        feed = list(feed_block(image_entries[slot], image_sends[slot], up_full, down_full, 0))
        if slot + 2 < size:
            image_entries[slot + 1], feed[2] = tie(image_entries[slot + 1], feed[2])
            image_entries.append(lax.ppermute(image_entries[slot + 1], "tensor", pairs))
        image_feeds.append(feed)
    text_feed = feed_block(text_entries, text_send, up_full, down_full, 1)
    entry_grad, (text_active, text_hidden) = ring_scatter_pair(
        [feed[2] for feed in image_feeds],
        cut_rows(text_feed[2], size),
        size,
        [text_feed[0], text_feed[1]],
        min(1, size - 2),
    )
    up_terms = [
        [
            (rows_of(image_entries[slot]), rows_of(image_feeds[slot][1]))
            for slot in range(size)
        ],
        [(rows_of(text_entries), rows_of(text_hidden))],
    ]
    down_terms = [
        [
            (rows_of(image_feeds[slot][0]), rows_of(image_sends[slot]))
            for slot in range(size)
        ],
        [(rows_of(text_active), rows_of(text_send))],
    ]
    if up_weight.shape == down_weight.shape:
        grad_feed = weight_grad(down_terms, 4, 2)
        grad_feed = weight_grad(up_terms, 4, 0, grad_feed)
        feed_owned = [scatter_weight(grad_feed)]
    else:
        feed_owned = [
            scatter_weight(weight_grad(up_terms)),
            scatter_weight(weight_grad(down_terms)),
        ]

    grads = [image_cotangent.astype(f32), text_cotangent.astype(f32)]
    cots = list(grads)
    shift_two = []
    scale_two = []
    gate_one = []
    sends = []
    for m in modalities:
        row_grad, normal = modulate_back(middle_rows[m], factors[:, m, 4], entry_grad[m])
        grads[m] = grads[m] + row_grad
        shift_two.append(jnp.sum(entry_grad[m], axis=1))
        scale_two.append(jnp.sum(entry_grad[m] * normal, axis=1))
        gate_one.append(jnp.sum(grads[m] * attn_branch[m], axis=1))
        sends.append((factors[:, m, 2][:, None, :] * grads[m]).astype(bf16))
    attn_blocks = ring_gather(jnp.concatenate(sends, axis=1), size)
    attn_grad = split_rows(attn_blocks, image_own)
    feed_slots = [
        jnp.concatenate([image_feeds[slot][3], part], axis=1)
        for slot, part in enumerate(cut_rows(text_feed[3], size))
    ]
    feed_slots[1], last_block = tie(feed_slots[1], attn_blocks[-1])
    late_grad = split_rows(attn_blocks[:-1] + [last_block], image_own)
    grad_mixed = jnp.concatenate(
        [
            jnp.einsum("hom,rm->hor", attn_grad[m], outer_full[m], preferred_element_type=f32)
            for m in modalities
        ],
        axis=1,
    ).astype(bf16)
    feed_total = ring_add(feed_slots[1], feed_slots[2 % size])
    if size > 2:
        feed_total = feed_total.astype(bf16)
    feed_total, grad_mixed = tie(feed_total, grad_mixed)
    grad_outer, feed_owned = tie(weight_grad(
            [
                [(rows_of(mixed, 0, length_image), rows_of(late_grad[0]))],
                [(rows_of(mixed, length_image), rows_of(late_grad[1]))],
            ]
        ), feed_owned)
    outer_owned = scatter_weight(grad_outer)
    grad_packed = attend_backward(packed, grad_mixed, log_totals, scale)
    feed_total = ring_add(feed_total, feed_slots[3 % size])
    if size > 3:
        feed_total = feed_total.astype(bf16)
    feed_total, grad_packed = tie(feed_total, grad_packed)
    grad_split = [grad_packed[:, :length_image], grad_packed[:, length_image:]]
    grad_inner = weight_grad(
        [
            [(rows_of(attn_inputs[0]), rows_of(grad_packed, 0, length_image))],
            [(rows_of(attn_inputs[1]), rows_of(grad_packed, length_image))],
        ]
    )
    grad_inner, outer_owned, grad_split[0] = lax.optimization_barrier(
        (grad_inner, outer_owned, grad_split[0])
    )
    inner_owned = scatter_weight(grad_inner)
    entry_terms = [
        jnp.einsum("sne,de->snd", grad_split[m], inner_full[m], preferred_element_type=f32)
        for m in modalities
    ]
    image_slots = cut_rows(entry_terms[0], size)
    text_slots = cut_rows(entry_terms[1], size)
    for slot in list(range(4, size)) + [0] * (size > 3):
        feed_total = ring_add(feed_total.astype(bf16), feed_slots[slot])
    image_slots[1], feed_total = tie(image_slots[1].astype(bf16), feed_total)
    image_total, text_total = tie(image_slots[1], text_slots[1].astype(bf16))
    image_next = lax.ppermute(image_total, "tensor", pairs)
    text_next, entry_terms[0], entry_terms[1] = lax.optimization_barrier(
        (lax.ppermute(text_total, "tensor", pairs), entry_terms[0], entry_terms[1])
    )
    image_total = image_next.astype(f32) + image_slots[2 % size]
    text_total = text_next.astype(f32) + text_slots[2 % size]
    feed_branch = feed_total
    feed_branch = [feed_branch[:, :image_own], feed_branch[:, image_own:]]
    carried = [
        middle_rows[m] + factors[:, m, 5][:, None, :] * feed_branch[m] for m in modalities
    ]
    gate_two = [jnp.sum(cots[m] * feed_branch[m], axis=1) for m in modalities]
    if len(feed_owned) == 1:
        feed_owned = [feed_owned[0][:2], feed_owned[0][2:]]
    factor_terms = [
        jnp.stack(
            [
                jnp.sum(entry_terms[m], axis=1),
                jnp.sum(entry_terms[m] * layer_norm(x_all[m]), axis=1),
                gate_one[m],
                shift_two[m],
                scale_two[m],
                gate_two[m],
            ],
            axis=1,
        )
        for m in modalities
    ]
    factor_sums = sum_to_columns(jnp.stack(factor_terms, axis=1), "tensor", size, 3)
    if size > 2:
        image_total, text_total, factor_sums = lax.optimization_barrier(
            (image_total.astype(bf16), text_total.astype(bf16), factor_sums)
        )
        image_total = ring_add(image_total, image_slots[3 % size])
        text_total = ring_add(text_total, text_slots[3 % size])
    factor_all = lax.all_gather(factor_sums, "dp", axis=0, tiled=True)
    if size > 3:
        image_total, text_total, factor_all = lax.optimization_barrier(
            (image_total.astype(bf16), text_total.astype(bf16), factor_all)
        )
        for slot in list(range(4, size)) + [0]:
            image_total = ring_add(image_total.astype(bf16), image_slots[slot])
            text_total = ring_add(text_total.astype(bf16), text_slots[slot])
    entry_grad = [image_total, text_total]
    for m in modalities:
        row_grad, normal = modulate_back(start_rows[m], factors[:, m, 1], entry_grad[m])
        grads[m] = grads[m] + row_grad
    mod_owned = jnp.einsum("sd,szke->zdke", lifted_own.astype(f32), factor_all, precision=highest)
    lifted_terms = jnp.einsum(
        "szke,zdke->sd", factor_all, modulator.astype(f32), precision=highest
    )
    swapped = lax.all_to_all(
        lifted_terms.reshape(dp_size, seq_count, own_depth), "dp", 0, 0, tiled=True
    )
    lifted_sum = jnp.moveaxis(swapped, 0, 1).reshape(seq_count, dp_size * own_depth)
    lifted_cols = sum_to_columns(lifted_sum, "tensor", size, 1)
    columns = lifted_cols.shape[1]
    own_cond = lax.dynamic_slice_in_dim(cond_float, lax.axis_index("tensor") * columns, columns, 1)
    gate = jax.nn.sigmoid(own_cond)
    cond_grad = lifted_cols * (gate * (1.0 + own_cond * (1.0 - gate)))
    return (
        carried[0].astype(bf16),
        carried[1].astype(bf16),
        grads[0],
        grads[1],
        cond_grad,
        mod_owned[None],
        inner_owned.reshape(attention_in.shape).astype(f32),
        outer_owned[None].astype(f32),
        feed_owned[0][None].astype(f32),
        feed_owned[1][None].astype(f32),
    )


def solution(mesh):
    in_specs = (
        P("dp", "tensor", None),
        P("dp", "tensor", None),
        P("dp", None),
        P(None, None, "dp", None, "tensor"),
        P(None, None, "dp", None, "tensor"),
        P(None, None, ("tensor", "dp"), None),
        P(None, None, "dp", "tensor"),
        P(None, None, ("tensor", "dp"), None),
        P("dp", "tensor", None),
        P("dp", "tensor", None),
    )
    out_specs = (
        P("dp", "tensor", None),
        P("dp", "tensor", None),
        P("dp", "tensor", None),
        P("dp", "tensor", None),
        P("dp", "tensor"),
        P(None, None, "dp", None, "tensor"),
        P(None, None, "dp", None, "tensor"),
        P(None, None, ("tensor", "dp"), None),
        P(None, None, "dp", "tensor"),
        P(None, None, ("tensor", "dp"), None),
    )
    body = partial(shards, dp_size=mesh.shape["dp"], size=mesh.shape["tensor"])
    return jax.shard_map(body, mesh=mesh, in_specs=in_specs, out_specs=out_specs, check_vma=False)
```

```python
from functools import partial

import jax
import jax.numpy as jnp
from jax import lax
from jax.experimental import pallas as pl
from jax.experimental.pallas import tpu as pltpu
from jax.sharding import PartitionSpec as P

HD = 64

norm_eps = 1e-06
highest = lax.Precision.HIGHEST
VMEM_LIMIT = 40 * 1024 * 1024
bf16 = jnp.bfloat16
f32 = jnp.float32


def layer_norm(rows):
    middle = jnp.mean(rows, axis=-1, keepdims=True)
    centered = rows - middle
    spread = jnp.mean(centered * centered, axis=-1, keepdims=True)
    return centered * lax.rsqrt(spread + norm_eps)


def modulate(rows, shift, scale):
    return layer_norm(rows) * (1.0 + scale[:, None, :]) + shift[:, None, :]


def modulate_back(rows, scale, grad):
    middle = jnp.mean(rows, axis=-1, keepdims=True)
    centered = rows - middle
    spread = jnp.mean(centered * centered, axis=-1, keepdims=True)
    inverse = lax.rsqrt(spread + norm_eps)
    normal = centered * inverse
    wide = grad * (1.0 + scale[:, None, :])
    first = jnp.mean(wide, axis=-1, keepdims=True)
    second = jnp.mean(wide * normal, axis=-1, keepdims=True)
    return inverse * (wide - first - normal * second), normal


def gelu_parts(hidden):
    slope = 0.7978845608028654
    square = hidden * hidden
    tail = jnp.tanh(slope * hidden * (1.0 + 0.044715 * square))
    active = 0.5 * hidden * (1.0 + tail)
    back = 0.5 * (1.0 + tail) + 0.5 * hidden * (1.0 - tail * tail) * (
        slope * (1.0 + 3.0 * 0.044715 * square)
    )
    return active, back


NT = (((1,), (1,)), ((), ()))
NN = (((1,), (0,)), ((), ()))
TN = (((0,), (0,)), ((), ()))


def product(left, right, numbers):
    return lax.dot_general(left, right, numbers, preferred_element_type=f32)


def cuts(length, step):
    return [(lower, min(lower + step, length)) for lower in range(0, length, step)]


def attend_forward_kernel(packed, mixed, totals, *, step, scale):
    length, width = mixed.shape[1:]
    for head in range(width // HD):
        lane = head * HD
        keys = packed[0, :, width + lane : width + lane + HD]
        values = packed[0, :, 2 * width + lane : 2 * width + lane + HD]
        for lower, upper in cuts(length, step):
            query = packed[0, lower:upper, lane : lane + HD] * scale
            scores = product(keys, query, NT)
            largest = jnp.max(scores, axis=0, keepdims=True)
            raised = jnp.exp(scores - largest)
            denominator = jnp.sum(raised, axis=0, keepdims=True)
            probs = (raised * (1.0 / denominator)).astype(bf16)
            mixed[0, lower:upper, lane : lane + HD] = product(probs, values, TN).astype(bf16)
            totals[0, head : head + 1, lower:upper] = largest + jnp.log(denominator)


def attend_forward(packed, scale):
    seqs, length, width = packed.shape[0], packed.shape[1], packed.shape[2] // 3
    heads = width // HD
    pairs = seqs * heads * length * length
    return pl.pallas_call(
        partial(attend_forward_kernel, step=640, scale=scale),
        grid=(seqs,),
        in_specs=[pl.BlockSpec((1, length, 3 * width), lambda s: (s, 0, 0))],
        out_specs=[
            pl.BlockSpec((1, length, width), lambda s: (s, 0, 0)),
            pl.BlockSpec((1, heads, length), lambda s: (s, 0, 0)),
        ],
        out_shape=[
            jax.ShapeDtypeStruct((seqs, length, width), bf16),
            jax.ShapeDtypeStruct((seqs, heads, length), f32),
        ],
        cost_estimate=pl.CostEstimate(
            flops=pairs * HD * 16, bytes_accessed=seqs * length * width * 8, transcendentals=pairs
        ),
        compiler_params=pltpu.CompilerParams(vmem_limit_bytes=VMEM_LIMIT),
        name="attend_forward",
    )(packed)


def attend_backward_kernel(packed, grad_mixed, totals, grad, key_sum, value_sum, *, step, scale):
    length, width = grad_mixed.shape[1:]
    for head in range(width // HD):
        lane = head * HD
        keys = packed[0, :, width + lane : width + lane + HD]
        values = packed[0, :, 2 * width + lane : 2 * width + lane + HD]
        for lower, upper in cuts(length, step):
            query = packed[0, lower:upper, lane : lane + HD] * scale
            block_grad = grad_mixed[0, lower:upper, lane : lane + HD]
            probs = jnp.exp(product(keys, query, NT) - totals[0, head : head + 1, lower:upper])
            weighted = probs * product(values, block_grad, NT)
            inner = jnp.sum(weighted, axis=0, keepdims=True)
            grad_scores = (weighted - probs * inner).astype(bf16)
            grad_values = product(probs.astype(bf16), block_grad, NN)
            grad_keys = product(grad_scores, query, NN)
            grad_query = product(grad_scores, keys, TN) * scale
            grad[0, lower:upper, lane : lane + HD] = grad_query.astype(bf16)
            if lower:
                key_sum[...] += grad_keys
                value_sum[...] += grad_values
            else:
                key_sum[...] = grad_keys
                value_sum[...] = grad_values
        grad[0, :, width + lane : width + lane + HD] = key_sum[...].astype(bf16)
        grad[0, :, 2 * width + lane : 2 * width + lane + HD] = value_sum[...].astype(bf16)


def attend_backward(packed, grad_mixed, totals, scale):
    seqs, length, width = grad_mixed.shape
    heads = width // HD
    pairs = seqs * heads * length * length
    return pl.pallas_call(
        partial(attend_backward_kernel, step=640, scale=scale),
        grid=(seqs,),
        in_specs=[
            pl.BlockSpec((1, length, 3 * width), lambda s: (s, 0, 0)),
            pl.BlockSpec((1, length, width), lambda s: (s, 0, 0)),
            pl.BlockSpec((1, heads, length), lambda s: (s, 0, 0)),
        ],
        out_specs=pl.BlockSpec((1, length, 3 * width), lambda s: (s, 0, 0)),
        out_shape=jax.ShapeDtypeStruct((seqs, length, 3 * width), bf16),
        scratch_shapes=[pltpu.VMEM((length, HD), f32), pltpu.VMEM((length, HD), f32)],
        cost_estimate=pl.CostEstimate(
            flops=pairs * HD * 32, bytes_accessed=seqs * length * width * 14, transcendentals=pairs
        ),
        compiler_params=pltpu.CompilerParams(vmem_limit_bytes=VMEM_LIMIT),
        name="attend_backward",
    )(packed, grad_mixed, totals)


def weight_grad_kernel(*refs, terms):
    out = refs[-1]

    def total(pairs):
        value = None
        for (left, left_rows), (right, right_rows) in pairs:
            for seq in range(refs[left].shape[0]):
                term = product(
                    refs[left][seq, left_rows[0] : left_rows[1]],
                    refs[right][seq, right_rows[0] : right_rows[1]],
                    TN,
                )
                value = term if value is None else value + term
        return value.astype(bf16)

    for modality in range(2):

        @pl.when(pl.program_id(0) == modality)
        def _(pairs=terms[modality]):
            out[0] = total(pairs)


def rows_of(array, lower=0, upper=None):
    return (array, (lower, array.shape[1] if upper is None else upper))


def weight_grad(terms, slots=2, place=0, into=None):
    depth, width = terms[0][0][0][0].shape[2], terms[0][0][1][0].shape[2]
    tile = 768 if depth % 768 == 0 else 384 if depth % 384 == 0 else depth
    tiles = depth // tile
    operands, in_specs, found, numbered, rows = [], [], {}, [], 0
    for modality, pairs in enumerate(terms):
        numbered.append([])
        for pair in pairs:
            numbers = []
            for side, (array, window) in enumerate(pair):
                key = (id(array), side)
                if key not in found:
                    found[key] = len(operands)
                    operands.append(array)
                    both = all(
                        any(entry[side][0] is array for entry in other) for other in terms
                    )
                    if side:
                        spec = pl.BlockSpec(array.shape[:2] + (width,), lambda z, j: (0, 0, 0))
                    elif both:
                        spec = pl.BlockSpec(array.shape[:2] + (tile,), lambda z, j: (0, 0, j))
                    elif modality == 0:
                        spec = pl.BlockSpec(
                            array.shape[:2] + (tile,),
                            lambda z, j: (0, 0, jnp.where(z == 0, j, tiles - 1)),
                        )
                    else:
                        spec = pl.BlockSpec(
                            array.shape[:2] + (tile,),
                            lambda z, j: (0, 0, jnp.where(z == 1, j, 0)),
                        )
                    in_specs.append(spec)
                numbers.append((found[key], window))
            rows += array.shape[0] * (window[1] - window[0])
            numbered[-1].append(tuple(numbers))
    aliases = {}
    if into is not None:
        aliases = {len(operands): 0}
        operands.append(into)
        in_specs.append(pl.BlockSpec(memory_space=pl.ANY))
    return pl.pallas_call(
        partial(weight_grad_kernel, terms=numbered),
        grid=(2, tiles),
        in_specs=in_specs,
        out_specs=pl.BlockSpec((1, tile, width), lambda z, j: (z + place, j, 0)),
        out_shape=jax.ShapeDtypeStruct((slots, depth, width), bf16),
        input_output_aliases=aliases,
        cost_estimate=pl.CostEstimate(
            flops=2 * rows * depth * width,
            bytes_accessed=2 * (rows * (depth + width) + 2 * depth * width),
            transcendentals=0,
        ),
        compiler_params=pltpu.CompilerParams(vmem_limit_bytes=VMEM_LIMIT),
        name="weight_grad",
    )(*operands)


def entry_block_kernel(rows, shift, scale, weight, entry, packed):
    value = layer_norm(rows[0].astype(f32)) * (1.0 + scale[0]) + shift[0]
    value = value.astype(bf16)
    entry[0] = value
    packed[0] = product(value, weight[0], NN).astype(bf16)


def entry_block(rows, count, shift, scale, weight, modality):
    seqs, depth = rows.shape[0], rows.shape[2]
    width = weight.shape[2]
    factor = pl.BlockSpec((1, 1, depth), lambda s: (s, 0, 0))
    return pl.pallas_call(
        entry_block_kernel,
        grid=(seqs,),
        in_specs=[
            pl.BlockSpec((1, count, depth), lambda s: (s, 0, 0)),
            factor,
            factor,
            pl.BlockSpec((1, depth, width), lambda s: (modality, 0, 0)),
        ],
        out_specs=[
            pl.BlockSpec((1, count, depth), lambda s: (s, 0, 0)),
            pl.BlockSpec((1, count, width), lambda s: (s, 0, 0)),
        ],
        out_shape=[
            jax.ShapeDtypeStruct((seqs, count, depth), bf16),
            jax.ShapeDtypeStruct((seqs, count, width), bf16),
        ],
        cost_estimate=pl.CostEstimate(
            flops=2 * seqs * count * depth * width,
            bytes_accessed=2 * depth * width + 2 * seqs * count * (2 * depth + width),
            transcendentals=seqs * count,
        ),
        compiler_params=pltpu.CompilerParams(vmem_limit_bytes=VMEM_LIMIT),
        name="entry_block",
    )(rows, shift[:, None, :], scale[:, None, :], weight)


def feed_block_kernel(rows, grads, up, down, active, hidden_grad, entry, feed, entry_sum, feed_sum):
    place, last = pl.program_id(1), pl.num_programs(1) - 1
    upper, lower = up[0], down[0]
    hidden = product(rows[0], upper, NN)
    block_active, back = gelu_parts(hidden)
    block_active = block_active.astype(bf16)
    active[0] = block_active
    block_grad = (product(grads[0], lower, NT) * back).astype(bf16)
    hidden_grad[0] = block_grad
    entry_term = product(block_grad, upper, NT)
    feed_term = product(block_active, lower, NN)

    @pl.when(place == 0)
    def _():
        entry_sum[...] = entry_term
        feed_sum[...] = feed_term

    @pl.when(place > 0)
    def _():
        entry_sum[...] += entry_term
        feed_sum[...] += feed_term

    @pl.when(place == last)
    def _():
        entry[0] = entry_sum[...].astype(bf16)
        feed[0] = feed_sum[...].astype(bf16)


def feed_block(rows, grads, up_planes, down_planes, modality):
    (up, up_first), (down, down_first) = up_planes, down_planes
    seqs, count, depth = rows.shape
    width = up.shape[2]
    tile = next(step for step in (768, 512, 384, 256, 128, width) if width % step == 0)
    whole = pl.BlockSpec((1, count, depth), lambda s, f: (s, 0, 0))
    part = pl.BlockSpec((1, count, tile), lambda s, f: (s, 0, f))
    shapes = [jax.ShapeDtypeStruct((seqs, count, size), bf16) for size in (width, width, depth, depth)]
    return pl.pallas_call(
        feed_block_kernel,
        grid=(seqs, width // tile),
        in_specs=[
            whole,
            whole,
            pl.BlockSpec((1, depth, tile), lambda s, f: (up_first + modality, 0, f)),
            pl.BlockSpec((1, tile, depth), lambda s, f: (down_first + modality, f, 0)),
        ],
        out_specs=[part, part, whole, whole],
        out_shape=shapes,
        scratch_shapes=[pltpu.VMEM((count, depth), f32), pltpu.VMEM((count, depth), f32)],
        cost_estimate=pl.CostEstimate(
            flops=8 * seqs * count * depth * width,
            bytes_accessed=4 * depth * width + 8 * seqs * count * (depth + width),
            transcendentals=seqs * count * width,
        ),
        compiler_params=pltpu.CompilerParams(vmem_limit_bytes=VMEM_LIMIT),
        name="feed_block",
    )(rows, grads, up, down)


def ring_pairs(size):
    order = list(range(0, size, 2)) + list(range(size - 1, 0, -2)) if size != 4 else [0, 1, 3, 2]
    if size == 1:
        order = [0]
    return [(order[place], order[(place + 1) % size]) for place in range(size)]


def ring_gather(block, size):
    pairs = ring_pairs(size)
    blocks = [block]
    for step in range(size - 1):
        blocks.append(lax.ppermute(blocks[-1], "tensor", pairs))
    return blocks


def tie(value, other):
    return lax.optimization_barrier((value, other))


def ring_add(total, part):
    pairs = ring_pairs(lax.axis_size("tensor"))
    return lax.ppermute(total, "tensor", pairs).astype(f32) + part.astype(f32)


def ring_scatter_pair(image, text, size, fence, at):
    pairs = ring_pairs(size)
    image_total, text_total = image[1].astype(bf16), text[1].astype(bf16)
    for step, slot in enumerate(list(range(2, size)) + [0]):
        if step == at:
            image_total, text_total = tie(image_total, text_total)
        image_next = lax.ppermute(image_total, "tensor", pairs).astype(f32)
        text_next = lax.ppermute(text_total, "tensor", pairs)
        if step == at:
            text_next, *fence = lax.optimization_barrier((text_next, *fence))
        image_total = image_next + image[slot].astype(f32)
        text_total = text_next.astype(f32) + text[slot].astype(f32)
        if slot:
            image_total, text_total = image_total.astype(bf16), text_total.astype(bf16)
    return [image_total, text_total], fence


def ring_scatter(parts, size):
    pairs = ring_pairs(size)
    if size == 1:
        return parts[0].astype(f32)
    total = parts[1].astype(bf16)
    for slot in list(range(2, size)) + [0]:
        total = lax.ppermute(total, "tensor", pairs).astype(f32) + parts[slot].astype(f32)
        if slot:
            total = total.astype(bf16)
    return total


def split_rows(blocks, count):
    return [
        jnp.concatenate([block[:, :count] for block in blocks], axis=1),
        jnp.concatenate([block[:, count:] for block in blocks], axis=1),
    ]


def join_slots(image, text, size):
    image_rows = image.shape[1] // size
    text_rows = text.shape[1] // size
    return [
        jnp.concatenate(
            [
                image[:, slot * image_rows : (slot + 1) * image_rows],
                text[:, slot * text_rows : (slot + 1) * text_rows],
            ],
            axis=1,
        )
        for slot in range(size)
    ]


def cut_rows(value, size):
    count = value.shape[1] // size
    return [value[:, slot * count : (slot + 1) * count] for slot in range(size)]


def gather_weight(weight):
    return lax.all_gather(weight, "dp", axis=1, tiled=True)


def scatter_weight(grad):
    return lax.psum_scatter(grad, "dp", scatter_dimension=1, tiled=True)


def sum_to_columns(value, axis_name, size, axis):
    shape = value.shape
    cut = value.reshape(shape[:axis] + (size, shape[axis] // size) + shape[axis + 1 :])
    cut = jnp.moveaxis(cut, axis, 0)
    return jnp.sum(lax.all_to_all(cut, axis_name, 0, 0, tiled=True), axis=0)


def shards(
    image_rows,
    text_rows,
    conditioning,
    modulator,
    attention_in,
    attention_out,
    up_weight,
    down_weight,
    image_cotangent,
    text_cotangent,
    dp_size,
    size,
):
    scale = HD ** (-0.5)
    modalities = range(2)
    modulator = modulator[0]
    seq_count, image_own = image_rows.shape[:2]
    length_image = image_own * size

    cond_float = conditioning.astype(f32)
    lifted = jax.nn.silu(cond_float).astype(bf16)

    inner_full = gather_weight(attention_in[0].reshape(2, attention_in.shape[2], -1))
    pairs = ring_pairs(size)
    x_blocks = [jnp.concatenate([image_rows, text_rows], axis=1)]
    x_blocks.append(lax.ppermute(x_blocks[0], "tensor", pairs))

    lifted_all = lax.all_gather(lifted, "dp", axis=0, tiled=True)
    outer_local, lifted_all = tie(attention_out[0], lifted_all)
    outer_full = gather_weight(outer_local)
    own_depth = modulator.shape[1]
    lifted_own = lax.dynamic_slice_in_dim(
        lifted_all, lax.axis_index("dp") * own_depth, own_depth, 1
    )
    factor_terms = jnp.einsum("sd,zdke->szke", lifted_own, modulator, preferred_element_type=f32)
    factor_cols = sum_to_columns(factor_terms, "dp", dp_size, 0)
    x_blocks[1], factor_cols = tie(x_blocks[1], factor_cols)
    x_blocks.append(lax.ppermute(x_blocks[1], "tensor", pairs))
    factor_parts = lax.all_to_all(
        jnp.broadcast_to(factor_cols[None], (size,) + factor_cols.shape), "tensor", 0, 0, tiled=True
    )
    x_blocks[2], factor_parts = tie(x_blocks[2], factor_parts)
    factors = jnp.concatenate([factor_parts[place] for place in range(size)], axis=3)
    for step in range(3, size):
        x_blocks.append(lax.ppermute(x_blocks[-1], "tensor", pairs))
    x_blocks = x_blocks[:size]
    cotangent, up_local, down_local, x_blocks[-1] = lax.optimization_barrier(
        (
            jnp.concatenate([image_cotangent, text_cotangent], axis=1),
            up_weight[0],
            down_weight[0],
            x_blocks[-1],
        )
    )
    if up_local.shape == down_local.shape:
        weights = gather_weight(jnp.concatenate([up_local, down_local], axis=0))
        up_full, down_full = (weights, 0), (weights, 2)
    else:
        up_full, down_full = (gather_weight(up_local), 0), (gather_weight(down_local), 0)
    cot_blocks = [cotangent, lax.ppermute(cotangent, "tensor", ring_pairs(size))]
    x_all = [rows.astype(f32) for rows in split_rows(x_blocks, image_own)]
    parts = [
        entry_block(block, image_own, factors[:, 0, 0], factors[:, 0, 1], inner_full, 0)
        for block in x_blocks
    ]
    text_all = jnp.concatenate([block[:, image_own:] for block in x_blocks], axis=1)
    parts.append(
        entry_block(text_all, text_all.shape[1], factors[:, 1, 0], factors[:, 1, 1], inner_full, 1)
    )
    packed = jnp.concatenate([part[1] for part in parts], axis=1)
    cot_blocks[1], packed = tie(cot_blocks[1], packed)
    cot_blocks.append(lax.ppermute(cot_blocks[1], "tensor", ring_pairs(size)))
    mixed, log_totals = attend_forward(packed, scale)
    cot_blocks[2], mixed = tie(cot_blocks[2], mixed)
    for step in range(3, size):
        cot_blocks.append(lax.ppermute(cot_blocks[-1], "tensor", ring_pairs(size)))
    cot_blocks = cot_blocks[:size]
    pieces = [mixed[:, :length_image], mixed[:, length_image:]]
    outer_terms = [
        jnp.einsum("kut,tx->kux", pieces[m], outer_full[m], preferred_element_type=f32)
        for m in modalities
    ]
    outer_slots = join_slots(outer_terms[0], outer_terms[1], size)
    attn_total = ring_add(outer_slots[1].astype(bf16), outer_slots[2 % size])
    attn_total, cot_blocks[-1] = tie(attn_total, cot_blocks[-1])
    for slot in list(range(3, size)) + [0] * (size > 2):
        attn_total = ring_add(attn_total.astype(bf16), outer_slots[slot])
    attn_branch = attn_total
    attn_branch = [attn_branch[:, :image_own], attn_branch[:, image_own:]]
    start_rows = [image_rows.astype(f32), text_rows.astype(f32)]
    middle_rows = [
        start_rows[m] + factors[:, m, 2][:, None, :] * attn_branch[m] for m in modalities
    ]
    feed_entries = [
        modulate(middle_rows[m], factors[:, m, 3], factors[:, m, 4]).astype(bf16)
        for m in modalities
    ]
    if up_weight.shape == down_weight.shape:
        weights, feed_entries[0] = tie(weights, feed_entries[0])
        up_full, down_full = (weights, 0), (weights, 2)
    text_entries = jnp.concatenate(ring_gather(feed_entries[1], size), axis=1)
    image_entries = [feed_entries[0], lax.ppermute(feed_entries[0], "tensor", pairs)]
    text_cot = jnp.concatenate([block[:, image_own:] for block in cot_blocks], axis=1)
    text_send = (factors[:, 1, 5][:, None, :] * text_cot.astype(f32)).astype(bf16)
    image_sends = [
        (factors[:, 0, 5][:, None, :] * block[:, :image_own].astype(f32)).astype(bf16)
        for block in cot_blocks
    ]
    image_feeds = []
    for slot in range(size):
        feed = list(feed_block(image_entries[slot], image_sends[slot], up_full, down_full, 0))
        if slot + 2 < size:
            image_entries[slot + 1], feed[2] = tie(image_entries[slot + 1], feed[2])
            image_entries.append(lax.ppermute(image_entries[slot + 1], "tensor", pairs))
        image_feeds.append(feed)
    text_feed = feed_block(text_entries, text_send, up_full, down_full, 1)
    entry_grad, (text_active, text_hidden) = ring_scatter_pair(
        [feed[2] for feed in image_feeds],
        cut_rows(text_feed[2], size),
        size,
        [text_feed[0], text_feed[1]],
        min(1, size - 2),
    )
    up_terms = [
        [
            (rows_of(image_entries[slot]), rows_of(image_feeds[slot][1]))
            for slot in range(size)
        ],
        [(rows_of(text_entries), rows_of(text_hidden))],
    ]
    down_terms = [
        [
            (rows_of(image_feeds[slot][0]), rows_of(image_sends[slot]))
            for slot in range(size)
        ],
        [(rows_of(text_active), rows_of(text_send))],
    ]
    if up_weight.shape == down_weight.shape:
        grad_feed = weight_grad(down_terms, 4, 2)
        grad_feed = weight_grad(up_terms, 4, 0, grad_feed)
        feed_owned = [scatter_weight(grad_feed)]
    else:
        feed_owned = [
            scatter_weight(weight_grad(up_terms)),
            scatter_weight(weight_grad(down_terms)),
        ]

    grads = [image_cotangent.astype(f32), text_cotangent.astype(f32)]
    cots = list(grads)
    shift_two = []
    scale_two = []
    gate_one = []
    sends = []
    for m in modalities:
        row_grad, normal = modulate_back(middle_rows[m], factors[:, m, 4], entry_grad[m])
        grads[m] = grads[m] + row_grad
        shift_two.append(jnp.sum(entry_grad[m], axis=1))
        scale_two.append(jnp.sum(entry_grad[m] * normal, axis=1))
        gate_one.append(jnp.sum(grads[m] * attn_branch[m], axis=1))
        sends.append((factors[:, m, 2][:, None, :] * grads[m]).astype(bf16))
    attn_blocks = ring_gather(jnp.concatenate(sends, axis=1), size)
    attn_grad = split_rows(attn_blocks, image_own)
    feed_slots = [
        jnp.concatenate([image_feeds[slot][3], part], axis=1)
        for slot, part in enumerate(cut_rows(text_feed[3], size))
    ]
    feed_slots[1], last_block = tie(feed_slots[1], attn_blocks[-1])
    late_grad = split_rows(attn_blocks[:-1] + [last_block], image_own)
    grad_mixed = jnp.concatenate(
        [
            jnp.einsum("hom,rm->hor", attn_grad[m], outer_full[m], preferred_element_type=f32)
            for m in modalities
        ],
        axis=1,
    ).astype(bf16)
    feed_total = ring_add(feed_slots[1], feed_slots[2 % size])
    if size > 2:
        feed_total = feed_total.astype(bf16)
    feed_total, grad_mixed = tie(feed_total, grad_mixed)
    grad_outer, feed_owned = tie(weight_grad(
            [
                [(rows_of(mixed, 0, length_image), rows_of(late_grad[0]))],
                [(rows_of(mixed, length_image), rows_of(late_grad[1]))],
            ]
        ), feed_owned)
    outer_owned = scatter_weight(grad_outer)
    grad_packed = attend_backward(packed, grad_mixed, log_totals, scale)
    feed_total = ring_add(feed_total, feed_slots[3 % size])
    if size > 3:
        feed_total = feed_total.astype(bf16)
    feed_total, grad_packed = tie(feed_total, grad_packed)
    grad_split = [grad_packed[:, :length_image], grad_packed[:, length_image:]]
    grad_inner = weight_grad(
        [
            [
                (
                    rows_of(parts[slot][0]),
                    rows_of(grad_packed, slot * image_own, (slot + 1) * image_own),
                )
                for slot in range(size)
            ],
            [(rows_of(parts[size][0]), rows_of(grad_packed, length_image))],
        ]
    )
    grad_inner, outer_owned, grad_split[0] = lax.optimization_barrier(
        (grad_inner, outer_owned, grad_split[0])
    )
    inner_owned = scatter_weight(grad_inner)
    entry_terms = [
        jnp.einsum("sne,de->snd", grad_split[m], inner_full[m], preferred_element_type=f32)
        for m in modalities
    ]
    image_slots = cut_rows(entry_terms[0], size)
    text_slots = cut_rows(entry_terms[1], size)
    for slot in list(range(4, size)) + [0] * (size > 3):
        feed_total = ring_add(feed_total.astype(bf16), feed_slots[slot])
    image_slots[1], feed_total = tie(image_slots[1].astype(bf16), feed_total)
    image_total, text_total = tie(image_slots[1], text_slots[1].astype(bf16))
    image_next = lax.ppermute(image_total, "tensor", pairs)
    text_next, entry_terms[0], entry_terms[1] = lax.optimization_barrier(
        (lax.ppermute(text_total, "tensor", pairs), entry_terms[0], entry_terms[1])
    )
    image_total = image_next.astype(f32) + image_slots[2 % size]
    text_total = text_next.astype(f32) + text_slots[2 % size]
    feed_branch = feed_total
    feed_branch = [feed_branch[:, :image_own], feed_branch[:, image_own:]]
    carried = [
        middle_rows[m] + factors[:, m, 5][:, None, :] * feed_branch[m] for m in modalities
    ]
    gate_two = [jnp.sum(cots[m] * feed_branch[m], axis=1) for m in modalities]
    if len(feed_owned) == 1:
        feed_owned = [feed_owned[0][:2], feed_owned[0][2:]]
    factor_terms = jnp.stack(
        [
            term
            for m in modalities
            for term in (
                jnp.sum(entry_terms[m], axis=1),
                jnp.sum(entry_terms[m] * layer_norm(x_all[m]), axis=1),
                gate_one[m],
                shift_two[m],
                scale_two[m],
                gate_two[m],
            )
        ],
        axis=1,
    ).reshape(seq_count, 2, 6, -1)
    factor_sums = sum_to_columns(factor_terms, "tensor", size, 3)
    if size > 2:
        image_total, text_total, factor_sums = lax.optimization_barrier(
            (image_total.astype(bf16), text_total.astype(bf16), factor_sums)
        )
        image_total = ring_add(image_total, image_slots[3 % size])
        text_total = ring_add(text_total, text_slots[3 % size])
    factor_all = lax.all_gather(factor_sums, "dp", axis=0, tiled=True)
    if size > 3:
        image_total, text_total, factor_all = lax.optimization_barrier(
            (image_total.astype(bf16), text_total.astype(bf16), factor_all)
        )
        for slot in list(range(4, size)) + [0]:
            image_total = ring_add(image_total.astype(bf16), image_slots[slot])
            text_total = ring_add(text_total.astype(bf16), text_slots[slot])
    mod_owned = jnp.einsum("sd,szke->zdke", lifted_own.astype(f32), factor_all, precision=highest)
    lifted_terms = jnp.einsum(
        "szke,zdke->sd", factor_all, modulator.astype(f32), precision=highest
    )
    share = dp_size // size
    owner = lax.axis_index("dp") // share
    terms = lifted_terms.reshape(dp_size, 1, seq_count, own_depth)
    terms = jnp.where(jnp.arange(size)[None, :, None, None] == owner, terms, 0.0)
    terms = lax.all_to_all(
        terms.reshape(dp_size * size, seq_count, own_depth), ("dp", "tensor"), 0, 0, tiled=True
    )
    terms = jnp.sum(terms.reshape(dp_size, size, seq_count, own_depth), axis=1)
    terms = lax.dynamic_slice_in_dim(terms, lax.axis_index("tensor") * share, share, 0)
    lifted_cols = jnp.moveaxis(terms, 0, 1).reshape(seq_count, share * own_depth)
    entry_grad = [image_total, text_total]
    for m in modalities:
        row_grad, normal = modulate_back(start_rows[m], factors[:, m, 1], entry_grad[m])
        grads[m] = grads[m] + row_grad
    columns = lifted_cols.shape[1]
    own_cond = lax.dynamic_slice_in_dim(cond_float, lax.axis_index("tensor") * columns, columns, 1)
    gate = jax.nn.sigmoid(own_cond)
    cond_grad = lifted_cols * (gate * (1.0 + own_cond * (1.0 - gate)))
    return (
        carried[0].astype(bf16),
        carried[1].astype(bf16),
        grads[0],
        grads[1],
        cond_grad,
        mod_owned[None],
        inner_owned.reshape(attention_in.shape).astype(f32),
        outer_owned[None].astype(f32),
        feed_owned[0][None].astype(f32),
        feed_owned[1][None].astype(f32),
    )


def solution(mesh):
    in_specs = (
        P("dp", "tensor", None),
        P("dp", "tensor", None),
        P("dp", None),
        P(None, None, "dp", None, "tensor"),
        P(None, None, "dp", None, "tensor"),
        P(None, None, ("tensor", "dp"), None),
        P(None, None, "dp", "tensor"),
        P(None, None, ("tensor", "dp"), None),
        P("dp", "tensor", None),
        P("dp", "tensor", None),
    )
    out_specs = (
        P("dp", "tensor", None),
        P("dp", "tensor", None),
        P("dp", "tensor", None),
        P("dp", "tensor", None),
        P("dp", "tensor"),
        P(None, None, "dp", None, "tensor"),
        P(None, None, "dp", None, "tensor"),
        P(None, None, ("tensor", "dp"), None),
        P(None, None, "dp", "tensor"),
        P(None, None, ("tensor", "dp"), None),
    )
    body = partial(shards, dp_size=mesh.shape["dp"], size=mesh.shape["tensor"])
    return jax.shard_map(body, mesh=mesh, in_specs=in_specs, out_specs=out_specs, check_vma=False)
```

```python
from functools import partial

import jax
import jax.numpy as jnp
from jax import lax
from jax.experimental import pallas as pl
from jax.experimental.pallas import tpu as pltpu
from jax.sharding import PartitionSpec as P

HD = 64

norm_eps = 1e-06
highest = lax.Precision.HIGHEST
VMEM_LIMIT = 40 * 1024 * 1024
bf16 = jnp.bfloat16
f32 = jnp.float32


def layer_norm(rows):
    middle = jnp.mean(rows, axis=-1, keepdims=True)
    centered = rows - middle
    spread = jnp.mean(centered * centered, axis=-1, keepdims=True)
    return centered * lax.rsqrt(spread + norm_eps)


def modulate(rows, shift, scale):
    return layer_norm(rows) * (1.0 + scale[:, None, :]) + shift[:, None, :]


def modulate_back(rows, scale, grad):
    middle = jnp.mean(rows, axis=-1, keepdims=True)
    centered = rows - middle
    spread = jnp.mean(centered * centered, axis=-1, keepdims=True)
    inverse = lax.rsqrt(spread + norm_eps)
    normal = centered * inverse
    wide = grad * (1.0 + scale[:, None, :])
    first = jnp.mean(wide, axis=-1, keepdims=True)
    second = jnp.mean(wide * normal, axis=-1, keepdims=True)
    return inverse * (wide - first - normal * second), normal


def gelu_parts(hidden):
    slope = 0.7978845608028654
    square = hidden * hidden
    tail = jnp.tanh(slope * hidden * (1.0 + 0.044715 * square))
    active = 0.5 * hidden * (1.0 + tail)
    back = 0.5 * (1.0 + tail) + 0.5 * hidden * (1.0 - tail * tail) * (
        slope * (1.0 + 3.0 * 0.044715 * square)
    )
    return active, back


NT = (((1,), (1,)), ((), ()))
NN = (((1,), (0,)), ((), ()))
TN = (((0,), (0,)), ((), ()))


def product(left, right, numbers):
    return lax.dot_general(left, right, numbers, preferred_element_type=f32)


def cuts(length, step):
    return [(lower, min(lower + step, length)) for lower in range(0, length, step)]


def attend_forward_kernel(packed, mixed, totals, *, step, scale):
    length, width = mixed.shape[1:]
    for head in range(width // HD):
        lane = head * HD
        keys = packed[0, :, width + lane : width + lane + HD]
        values = packed[0, :, 2 * width + lane : 2 * width + lane + HD]
        for lower, upper in cuts(length, step):
            query = packed[0, lower:upper, lane : lane + HD] * scale
            scores = product(keys, query, NT)
            largest = jnp.max(scores, axis=0, keepdims=True)
            raised = jnp.exp(scores - largest)
            denominator = jnp.sum(raised, axis=0, keepdims=True)
            probs = (raised * (1.0 / denominator)).astype(bf16)
            mixed[0, lower:upper, lane : lane + HD] = product(probs, values, TN).astype(bf16)
            totals[0, head : head + 1, lower:upper] = largest + jnp.log(denominator)


def attend_forward(packed, scale):
    seqs, length, width = packed.shape[0], packed.shape[1], packed.shape[2] // 3
    heads = width // HD
    pairs = seqs * heads * length * length
    return pl.pallas_call(
        partial(attend_forward_kernel, step=640, scale=scale),
        grid=(seqs,),
        in_specs=[pl.BlockSpec((1, length, 3 * width), lambda s: (s, 0, 0))],
        out_specs=[
            pl.BlockSpec((1, length, width), lambda s: (s, 0, 0)),
            pl.BlockSpec((1, heads, length), lambda s: (s, 0, 0)),
        ],
        out_shape=[
            jax.ShapeDtypeStruct((seqs, length, width), bf16),
            jax.ShapeDtypeStruct((seqs, heads, length), f32),
        ],
        cost_estimate=pl.CostEstimate(
            flops=pairs * HD * 16, bytes_accessed=seqs * length * width * 8, transcendentals=pairs
        ),
        compiler_params=pltpu.CompilerParams(vmem_limit_bytes=VMEM_LIMIT),
        name="attend_forward",
    )(packed)


def attend_backward_kernel(packed, grad_mixed, totals, grad, key_sum, value_sum, *, step, scale):
    length, width = grad_mixed.shape[1:]
    for head in range(width // HD):
        lane = head * HD
        keys = packed[0, :, width + lane : width + lane + HD]
        values = packed[0, :, 2 * width + lane : 2 * width + lane + HD]
        for lower, upper in cuts(length, step):
            query = packed[0, lower:upper, lane : lane + HD] * scale
            block_grad = grad_mixed[0, lower:upper, lane : lane + HD]
            probs = jnp.exp(product(keys, query, NT) - totals[0, head : head + 1, lower:upper])
            weighted = probs * product(values, block_grad, NT)
            inner = jnp.sum(weighted, axis=0, keepdims=True)
            grad_scores = (weighted - probs * inner).astype(bf16)
            grad_values = product(probs.astype(bf16), block_grad, NN)
            grad_keys = product(grad_scores, query, NN)
            grad_query = product(grad_scores, keys, TN) * scale
            grad[0, lower:upper, lane : lane + HD] = grad_query.astype(bf16)
            if lower:
                key_sum[...] += grad_keys
                value_sum[...] += grad_values
            else:
                key_sum[...] = grad_keys
                value_sum[...] = grad_values
        grad[0, :, width + lane : width + lane + HD] = key_sum[...].astype(bf16)
        grad[0, :, 2 * width + lane : 2 * width + lane + HD] = value_sum[...].astype(bf16)


def attend_backward(packed, grad_mixed, totals, scale):
    seqs, length, width = grad_mixed.shape
    heads = width // HD
    pairs = seqs * heads * length * length
    return pl.pallas_call(
        partial(attend_backward_kernel, step=640, scale=scale),
        grid=(seqs,),
        in_specs=[
            pl.BlockSpec((1, length, 3 * width), lambda s: (s, 0, 0)),
            pl.BlockSpec((1, length, width), lambda s: (s, 0, 0)),
            pl.BlockSpec((1, heads, length), lambda s: (s, 0, 0)),
        ],
        out_specs=pl.BlockSpec((1, length, 3 * width), lambda s: (s, 0, 0)),
        out_shape=jax.ShapeDtypeStruct((seqs, length, 3 * width), bf16),
        scratch_shapes=[pltpu.VMEM((length, HD), f32), pltpu.VMEM((length, HD), f32)],
        cost_estimate=pl.CostEstimate(
            flops=pairs * HD * 32, bytes_accessed=seqs * length * width * 14, transcendentals=pairs
        ),
        compiler_params=pltpu.CompilerParams(vmem_limit_bytes=VMEM_LIMIT),
        name="attend_backward",
    )(packed, grad_mixed, totals)


def weight_grad_kernel(*refs, terms):
    out = refs[-1]

    def total(pairs):
        value = None
        for (left, left_rows), (right, right_rows) in pairs:
            for seq in range(refs[left].shape[0]):
                term = product(
                    refs[left][seq, left_rows[0] : left_rows[1]],
                    refs[right][seq, right_rows[0] : right_rows[1]],
                    TN,
                )
                value = term if value is None else value + term
        return value.astype(bf16)

    for modality in range(2):

        @pl.when(pl.program_id(0) == modality)
        def _(pairs=terms[modality]):
            out[0] = total(pairs)


def rows_of(array, lower=0, upper=None):
    return (array, (lower, array.shape[1] if upper is None else upper))


def weight_grad(terms, slots=2, place=0, into=None):
    depth, width = terms[0][0][0][0].shape[2], terms[0][0][1][0].shape[2]
    tile = 768 if depth % 768 == 0 else 384 if depth % 384 == 0 else depth
    tiles = depth // tile
    operands, in_specs, found, numbered, rows = [], [], {}, [], 0
    for modality, pairs in enumerate(terms):
        numbered.append([])
        for pair in pairs:
            numbers = []
            for side, (array, window) in enumerate(pair):
                key = (id(array), side)
                if key not in found:
                    found[key] = len(operands)
                    operands.append(array)
                    both = all(
                        any(entry[side][0] is array for entry in other) for other in terms
                    )
                    if side:
                        spec = pl.BlockSpec(array.shape[:2] + (width,), lambda z, j: (0, 0, 0))
                    elif both:
                        spec = pl.BlockSpec(array.shape[:2] + (tile,), lambda z, j: (0, 0, j))
                    elif modality == 0:
                        spec = pl.BlockSpec(
                            array.shape[:2] + (tile,),
                            lambda z, j: (0, 0, jnp.where(z == 0, j, tiles - 1)),
                        )
                    else:
                        spec = pl.BlockSpec(
                            array.shape[:2] + (tile,),
                            lambda z, j: (0, 0, jnp.where(z == 1, j, 0)),
                        )
                    in_specs.append(spec)
                numbers.append((found[key], window))
            rows += array.shape[0] * (window[1] - window[0])
            numbered[-1].append(tuple(numbers))
    aliases = {}
    if into is not None:
        aliases = {len(operands): 0}
        operands.append(into)
        in_specs.append(pl.BlockSpec(memory_space=pl.ANY))
    return pl.pallas_call(
        partial(weight_grad_kernel, terms=numbered),
        grid=(2, tiles),
        in_specs=in_specs,
        out_specs=pl.BlockSpec((1, tile, width), lambda z, j: (z + place, j, 0)),
        out_shape=jax.ShapeDtypeStruct((slots, depth, width), bf16),
        input_output_aliases=aliases,
        cost_estimate=pl.CostEstimate(
            flops=2 * rows * depth * width,
            bytes_accessed=2 * (rows * (depth + width) + 2 * depth * width),
            transcendentals=0,
        ),
        compiler_params=pltpu.CompilerParams(vmem_limit_bytes=VMEM_LIMIT),
        name="weight_grad",
    )(*operands)


def entry_block_kernel(rows, shift, scale, weight, entry, packed):
    value = layer_norm(rows[0].astype(f32)) * (1.0 + scale[0]) + shift[0]
    value = value.astype(bf16)
    entry[0] = value
    packed[0] = product(value, weight[0], NN).astype(bf16)


def entry_block(rows, count, shift, scale, weight, modality):
    seqs, depth = rows.shape[0], rows.shape[2]
    width = weight.shape[2]
    factor = pl.BlockSpec((1, 1, depth), lambda s: (s, 0, 0))
    return pl.pallas_call(
        entry_block_kernel,
        grid=(seqs,),
        in_specs=[
            pl.BlockSpec((1, count, depth), lambda s: (s, 0, 0)),
            factor,
            factor,
            pl.BlockSpec((1, depth, width), lambda s: (modality, 0, 0)),
        ],
        out_specs=[
            pl.BlockSpec((1, count, depth), lambda s: (s, 0, 0)),
            pl.BlockSpec((1, count, width), lambda s: (s, 0, 0)),
        ],
        out_shape=[
            jax.ShapeDtypeStruct((seqs, count, depth), bf16),
            jax.ShapeDtypeStruct((seqs, count, width), bf16),
        ],
        cost_estimate=pl.CostEstimate(
            flops=2 * seqs * count * depth * width,
            bytes_accessed=2 * depth * width + 2 * seqs * count * (2 * depth + width),
            transcendentals=seqs * count,
        ),
        compiler_params=pltpu.CompilerParams(vmem_limit_bytes=VMEM_LIMIT),
        name="entry_block",
    )(rows, shift[:, None, :], scale[:, None, :], weight)


def entry_back_kernel(grads, weight, rows, terms, sums):
    value = product(grads[0], weight[0], NT)
    terms[0] = value.astype(bf16)
    normal = layer_norm(rows[0].astype(f32))
    sums[0, 0:1] = jnp.sum(value, axis=0, keepdims=True)
    sums[0, 1:2] = jnp.sum(value * normal, axis=0, keepdims=True)


def entry_back(grads, place, count, weight, rows, modality):
    seqs, depth = rows.shape[0], rows.shape[2]
    width = weight.shape[2]
    return pl.pallas_call(
        entry_back_kernel,
        grid=(seqs,),
        in_specs=[
            pl.BlockSpec((1, count, width), lambda s: (s, place, 0)),
            pl.BlockSpec((1, depth, width), lambda s: (modality, 0, 0)),
            pl.BlockSpec((1, count, depth), lambda s: (s, 0, 0)),
        ],
        out_specs=[
            pl.BlockSpec((1, count, depth), lambda s: (s, 0, 0)),
            pl.BlockSpec((1, 2, depth), lambda s: (s, 0, 0)),
        ],
        out_shape=[
            jax.ShapeDtypeStruct((seqs, count, depth), bf16),
            jax.ShapeDtypeStruct((seqs, 2, depth), f32),
        ],
        cost_estimate=pl.CostEstimate(
            flops=2 * seqs * count * depth * width,
            bytes_accessed=2 * depth * width + 2 * seqs * count * (2 * depth + width),
            transcendentals=seqs * count,
        ),
        compiler_params=pltpu.CompilerParams(vmem_limit_bytes=VMEM_LIMIT),
        name="entry_back",
    )(grads, weight, rows)


def feed_block_kernel(rows, grads, up, down, active, hidden_grad, entry, feed, entry_sum, feed_sum):
    place, last = pl.program_id(1), pl.num_programs(1) - 1
    upper, lower = up[0], down[0]
    hidden = product(rows[0], upper, NN)
    block_active, back = gelu_parts(hidden)
    block_active = block_active.astype(bf16)
    active[0] = block_active
    block_grad = (product(grads[0], lower, NT) * back).astype(bf16)
    hidden_grad[0] = block_grad
    entry_term = product(block_grad, upper, NT)
    feed_term = product(block_active, lower, NN)

    @pl.when(place == 0)
    def _():
        entry_sum[...] = entry_term
        feed_sum[...] = feed_term

    @pl.when(place > 0)
    def _():
        entry_sum[...] += entry_term
        feed_sum[...] += feed_term

    @pl.when(place == last)
    def _():
        entry[0] = entry_sum[...].astype(bf16)
        feed[0] = feed_sum[...].astype(bf16)


def feed_block(rows, grads, up_planes, down_planes, modality):
    (up, up_first), (down, down_first) = up_planes, down_planes
    seqs, count, depth = rows.shape
    width = up.shape[2]
    tile = next(step for step in (768, 512, 384, 256, 128, width) if width % step == 0)
    whole = pl.BlockSpec((1, count, depth), lambda s, f: (s, 0, 0))
    part = pl.BlockSpec((1, count, tile), lambda s, f: (s, 0, f))
    shapes = [jax.ShapeDtypeStruct((seqs, count, size), bf16) for size in (width, width, depth, depth)]
    return pl.pallas_call(
        feed_block_kernel,
        grid=(seqs, width // tile),
        in_specs=[
            whole,
            whole,
            pl.BlockSpec((1, depth, tile), lambda s, f: (up_first + modality, 0, f)),
            pl.BlockSpec((1, tile, depth), lambda s, f: (down_first + modality, f, 0)),
        ],
        out_specs=[part, part, whole, whole],
        out_shape=shapes,
        scratch_shapes=[pltpu.VMEM((count, depth), f32), pltpu.VMEM((count, depth), f32)],
        cost_estimate=pl.CostEstimate(
            flops=8 * seqs * count * depth * width,
            bytes_accessed=4 * depth * width + 8 * seqs * count * (depth + width),
            transcendentals=seqs * count * width,
        ),
        compiler_params=pltpu.CompilerParams(vmem_limit_bytes=VMEM_LIMIT),
        name="feed_block",
    )(rows, grads, up, down)


def ring_pairs(size):
    order = list(range(0, size, 2)) + list(range(size - 1, 0, -2)) if size != 4 else [0, 1, 3, 2]
    if size == 1:
        order = [0]
    return [(order[place], order[(place + 1) % size]) for place in range(size)]


def ring_gather(block, size):
    pairs = ring_pairs(size)
    blocks = [block]
    for step in range(size - 1):
        blocks.append(lax.ppermute(blocks[-1], "tensor", pairs))
    return blocks


def tie(value, other):
    return lax.optimization_barrier((value, other))


def ring_add(total, part):
    pairs = ring_pairs(lax.axis_size("tensor"))
    return lax.ppermute(total, "tensor", pairs).astype(f32) + part.astype(f32)


def ring_scatter_pair(image, text, size, fence, at):
    pairs = ring_pairs(size)
    image_total, text_total = image[1].astype(bf16), text[1].astype(bf16)
    for step, slot in enumerate(list(range(2, size)) + [0]):
        if step == at:
            image_total, text_total = tie(image_total, text_total)
        image_next = lax.ppermute(image_total, "tensor", pairs).astype(f32)
        text_next = lax.ppermute(text_total, "tensor", pairs)
        if step == at:
            text_next, *fence = lax.optimization_barrier((text_next, *fence))
        image_total = image_next + image[slot].astype(f32)
        text_total = text_next.astype(f32) + text[slot].astype(f32)
        if slot:
            image_total, text_total = image_total.astype(bf16), text_total.astype(bf16)
    return [image_total, text_total], fence


def ring_scatter(parts, size):
    pairs = ring_pairs(size)
    if size == 1:
        return parts[0].astype(f32)
    total = parts[1].astype(bf16)
    for slot in list(range(2, size)) + [0]:
        total = lax.ppermute(total, "tensor", pairs).astype(f32) + parts[slot].astype(f32)
        if slot:
            total = total.astype(bf16)
    return total


def split_rows(blocks, count):
    return [
        jnp.concatenate([block[:, :count] for block in blocks], axis=1),
        jnp.concatenate([block[:, count:] for block in blocks], axis=1),
    ]


def join_slots(image, text, size):
    image_rows = image.shape[1] // size
    text_rows = text.shape[1] // size
    return [
        jnp.concatenate(
            [
                image[:, slot * image_rows : (slot + 1) * image_rows],
                text[:, slot * text_rows : (slot + 1) * text_rows],
            ],
            axis=1,
        )
        for slot in range(size)
    ]


def cut_rows(value, size):
    count = value.shape[1] // size
    return [value[:, slot * count : (slot + 1) * count] for slot in range(size)]


def gather_weight(weight):
    return lax.all_gather(weight, "dp", axis=1, tiled=True)


def scatter_weight(grad):
    return lax.psum_scatter(grad, "dp", scatter_dimension=1, tiled=True)


def sum_to_columns(value, axis_name, size, axis):
    shape = value.shape
    cut = value.reshape(shape[:axis] + (size, shape[axis] // size) + shape[axis + 1 :])
    cut = jnp.moveaxis(cut, axis, 0)
    return jnp.sum(lax.all_to_all(cut, axis_name, 0, 0, tiled=True), axis=0)


def shards(
    image_rows,
    text_rows,
    conditioning,
    modulator,
    attention_in,
    attention_out,
    up_weight,
    down_weight,
    image_cotangent,
    text_cotangent,
    dp_size,
    size,
):
    scale = HD ** (-0.5)
    modalities = range(2)
    modulator = modulator[0]
    seq_count, image_own = image_rows.shape[:2]
    length_image = image_own * size

    cond_float = conditioning.astype(f32)
    lifted = jax.nn.silu(cond_float).astype(bf16)

    inner_full = gather_weight(attention_in[0].reshape(2, attention_in.shape[2], -1))
    pairs = ring_pairs(size)
    x_blocks = [jnp.concatenate([image_rows, text_rows], axis=1)]
    x_blocks.append(lax.ppermute(x_blocks[0], "tensor", pairs))

    lifted_all = lax.all_gather(lifted, "dp", axis=0, tiled=True)
    outer_local, lifted_all = tie(attention_out[0], lifted_all)
    outer_full = gather_weight(outer_local)
    own_depth = modulator.shape[1]
    lifted_own = lax.dynamic_slice_in_dim(
        lifted_all, lax.axis_index("dp") * own_depth, own_depth, 1
    )
    factor_terms = jnp.einsum("sd,zdke->szke", lifted_own, modulator, preferred_element_type=f32)
    factor_cols = sum_to_columns(factor_terms, "dp", dp_size, 0)
    x_blocks[1], factor_cols = tie(x_blocks[1], factor_cols)
    x_blocks.append(lax.ppermute(x_blocks[1], "tensor", pairs))
    factor_parts = lax.all_to_all(
        jnp.broadcast_to(factor_cols[None], (size,) + factor_cols.shape), "tensor", 0, 0, tiled=True
    )
    x_blocks[2], factor_parts = tie(x_blocks[2], factor_parts)
    factors = jnp.concatenate([factor_parts[place] for place in range(size)], axis=3)
    for step in range(3, size):
        x_blocks.append(lax.ppermute(x_blocks[-1], "tensor", pairs))
    x_blocks = x_blocks[:size]
    cotangent, up_local, down_local, x_blocks[-1] = lax.optimization_barrier(
        (
            jnp.concatenate([image_cotangent, text_cotangent], axis=1),
            up_weight[0],
            down_weight[0],
            x_blocks[-1],
        )
    )
    if up_local.shape == down_local.shape:
        weights = gather_weight(jnp.concatenate([up_local, down_local], axis=0))
        up_full, down_full = (weights, 0), (weights, 2)
    else:
        up_full, down_full = (gather_weight(up_local), 0), (gather_weight(down_local), 0)
    cot_blocks = [cotangent, lax.ppermute(cotangent, "tensor", ring_pairs(size))]
    parts = [
        entry_block(block, image_own, factors[:, 0, 0], factors[:, 0, 1], inner_full, 0)
        for block in x_blocks
    ]
    text_all = jnp.concatenate([block[:, image_own:] for block in x_blocks], axis=1)
    parts.append(
        entry_block(text_all, text_all.shape[1], factors[:, 1, 0], factors[:, 1, 1], inner_full, 1)
    )
    packed = jnp.concatenate([part[1] for part in parts], axis=1)
    cot_blocks[1], packed = tie(cot_blocks[1], packed)
    cot_blocks.append(lax.ppermute(cot_blocks[1], "tensor", ring_pairs(size)))
    mixed, log_totals = attend_forward(packed, scale)
    cot_blocks[2], mixed = tie(cot_blocks[2], mixed)
    for step in range(3, size):
        cot_blocks.append(lax.ppermute(cot_blocks[-1], "tensor", ring_pairs(size)))
    cot_blocks = cot_blocks[:size]
    pieces = [mixed[:, :length_image], mixed[:, length_image:]]
    outer_terms = [
        jnp.einsum("kut,tx->kux", pieces[m], outer_full[m], preferred_element_type=f32)
        for m in modalities
    ]
    outer_slots = join_slots(outer_terms[0], outer_terms[1], size)
    attn_total = ring_add(outer_slots[1].astype(bf16), outer_slots[2 % size])
    attn_total, cot_blocks[-1] = tie(attn_total, cot_blocks[-1])
    for slot in list(range(3, size)) + [0] * (size > 2):
        attn_total = ring_add(attn_total.astype(bf16), outer_slots[slot])
    attn_branch = attn_total
    attn_branch = [attn_branch[:, :image_own], attn_branch[:, image_own:]]
    start_rows = [image_rows.astype(f32), text_rows.astype(f32)]
    middle_rows = [
        start_rows[m] + factors[:, m, 2][:, None, :] * attn_branch[m] for m in modalities
    ]
    feed_entries = [
        modulate(middle_rows[m], factors[:, m, 3], factors[:, m, 4]).astype(bf16)
        for m in modalities
    ]
    if up_weight.shape == down_weight.shape:
        weights, feed_entries[0] = tie(weights, feed_entries[0])
        up_full, down_full = (weights, 0), (weights, 2)
    text_entries = jnp.concatenate(ring_gather(feed_entries[1], size), axis=1)
    image_entries = [feed_entries[0], lax.ppermute(feed_entries[0], "tensor", pairs)]
    text_cot = jnp.concatenate([block[:, image_own:] for block in cot_blocks], axis=1)
    text_send = (factors[:, 1, 5][:, None, :] * text_cot.astype(f32)).astype(bf16)
    image_sends = [
        (factors[:, 0, 5][:, None, :] * block[:, :image_own].astype(f32)).astype(bf16)
        for block in cot_blocks
    ]
    image_feeds = []
    for slot in range(size):
        feed = list(feed_block(image_entries[slot], image_sends[slot], up_full, down_full, 0))
        if slot + 2 < size:
            image_entries[slot + 1], feed[2] = tie(image_entries[slot + 1], feed[2])
            image_entries.append(lax.ppermute(image_entries[slot + 1], "tensor", pairs))
        image_feeds.append(feed)
    text_feed = feed_block(text_entries, text_send, up_full, down_full, 1)
    entry_grad, (text_active, text_hidden) = ring_scatter_pair(
        [feed[2] for feed in image_feeds],
        cut_rows(text_feed[2], size),
        size,
        [text_feed[0], text_feed[1]],
        min(1, size - 2),
    )
    up_terms = [
        [
            (rows_of(image_entries[slot]), rows_of(image_feeds[slot][1]))
            for slot in range(size)
        ],
        [(rows_of(text_entries), rows_of(text_hidden))],
    ]
    down_terms = [
        [
            (rows_of(image_feeds[slot][0]), rows_of(image_sends[slot]))
            for slot in range(size)
        ],
        [(rows_of(text_active), rows_of(text_send))],
    ]
    if up_weight.shape == down_weight.shape:
        grad_feed = weight_grad(down_terms, 4, 2)
        grad_feed = weight_grad(up_terms, 4, 0, grad_feed)
        feed_owned = [scatter_weight(grad_feed)]
    else:
        feed_owned = [
            scatter_weight(weight_grad(up_terms)),
            scatter_weight(weight_grad(down_terms)),
        ]

    grads = [image_cotangent.astype(f32), text_cotangent.astype(f32)]
    cots = list(grads)
    shift_two = []
    scale_two = []
    gate_one = []
    sends = []
    for m in modalities:
        row_grad, normal = modulate_back(middle_rows[m], factors[:, m, 4], entry_grad[m])
        grads[m] = grads[m] + row_grad
        shift_two.append(jnp.sum(entry_grad[m], axis=1))
        scale_two.append(jnp.sum(entry_grad[m] * normal, axis=1))
        gate_one.append(jnp.sum(grads[m] * attn_branch[m], axis=1))
        sends.append((factors[:, m, 2][:, None, :] * grads[m]).astype(bf16))
    attn_blocks = ring_gather(jnp.concatenate(sends, axis=1), size)
    attn_grad = split_rows(attn_blocks, image_own)
    feed_slots = [
        jnp.concatenate([image_feeds[slot][3], part], axis=1)
        for slot, part in enumerate(cut_rows(text_feed[3], size))
    ]
    feed_slots[1], last_block = tie(feed_slots[1], attn_blocks[-1])
    late_grad = split_rows(attn_blocks[:-1] + [last_block], image_own)
    grad_mixed = jnp.concatenate(
        [
            jnp.einsum("hom,rm->hor", attn_grad[m], outer_full[m], preferred_element_type=f32)
            for m in modalities
        ],
        axis=1,
    ).astype(bf16)
    feed_total = ring_add(feed_slots[1], feed_slots[2 % size])
    if size > 2:
        feed_total = feed_total.astype(bf16)
    feed_total, grad_mixed = tie(feed_total, grad_mixed)
    grad_outer, feed_owned = tie(weight_grad(
            [
                [(rows_of(mixed, 0, length_image), rows_of(late_grad[0]))],
                [(rows_of(mixed, length_image), rows_of(late_grad[1]))],
            ]
        ), feed_owned)
    outer_owned = scatter_weight(grad_outer)
    grad_packed = attend_backward(packed, grad_mixed, log_totals, scale)
    feed_total = ring_add(feed_total, feed_slots[3 % size])
    if size > 3:
        feed_total = feed_total.astype(bf16)
    feed_total, grad_packed = tie(feed_total, grad_packed)
    grad_inner = weight_grad(
        [
            [
                (
                    rows_of(parts[slot][0]),
                    rows_of(grad_packed, slot * image_own, (slot + 1) * image_own),
                )
                for slot in range(size)
            ],
            [(rows_of(parts[size][0]), rows_of(grad_packed, length_image))],
        ]
    )
    grad_inner, outer_owned, late_packed = lax.optimization_barrier(
        (grad_inner, outer_owned, grad_packed)
    )
    inner_owned = scatter_weight(grad_inner)
    image_backs = [
        entry_back(late_packed, slot, image_own, inner_full, x_blocks[slot], 0)
        for slot in range(size)
    ]
    text_back = entry_back(
        late_packed[:, length_image:], 0, text_all.shape[1], inner_full, text_all, 1
    )
    entry_sums = [sum(back[1] for back in image_backs), text_back[1]]
    image_slots = [back[0] for back in image_backs]
    text_slots = cut_rows(text_back[0], size)
    for slot in range(4, size):
        feed_total = ring_add(feed_total.astype(bf16), feed_slots[slot])
    if size > 3:
        feed_total = lax.ppermute(feed_total.astype(bf16), "tensor", pairs)
    image_total, text_total = tie(image_slots[1], text_slots[1].astype(bf16))
    image_next = lax.ppermute(image_total, "tensor", pairs)
    text_next, entry_sums[0], entry_sums[1], feed_slots[0] = lax.optimization_barrier(
        (lax.ppermute(text_total, "tensor", pairs), entry_sums[0], entry_sums[1], feed_slots[0])
    )
    if size > 3:
        feed_total = feed_total.astype(f32) + feed_slots[0].astype(f32)
    image_total = image_next.astype(f32) + image_slots[2 % size].astype(f32)
    text_total = text_next.astype(f32) + text_slots[2 % size].astype(f32)
    feed_branch = feed_total
    feed_branch = [feed_branch[:, :image_own], feed_branch[:, image_own:]]
    carried = [
        middle_rows[m] + factors[:, m, 5][:, None, :] * feed_branch[m] for m in modalities
    ]
    gate_two = [jnp.sum(cots[m] * feed_branch[m], axis=1) for m in modalities]
    if len(feed_owned) == 1:
        feed_owned = [feed_owned[0][:2], feed_owned[0][2:]]
    factor_terms = jnp.stack(
        [
            term
            for m in modalities
            for term in (
                entry_sums[m][:, 0],
                entry_sums[m][:, 1],
                gate_one[m],
                shift_two[m],
                scale_two[m],
                gate_two[m],
            )
        ],
        axis=1,
    ).reshape(seq_count, 2, 6, -1)
    factor_sums = sum_to_columns(factor_terms, "tensor", size, 3)
    if size > 2:
        image_total, text_total, factor_sums = lax.optimization_barrier(
            (image_total.astype(bf16), text_total.astype(bf16), factor_sums)
        )
        image_total = ring_add(image_total, image_slots[3 % size])
        text_total = ring_add(text_total, text_slots[3 % size])
    factor_all = lax.all_gather(factor_sums, "dp", axis=0, tiled=True)
    factor_all, *feed_owned = lax.optimization_barrier((factor_all, *feed_owned))
    if size > 3:
        image_total, text_total, factor_all = lax.optimization_barrier(
            (image_total.astype(bf16), text_total.astype(bf16), factor_all)
        )
        for slot in range(4, size):
            image_total = ring_add(image_total, image_slots[slot]).astype(bf16)
            text_total = ring_add(text_total, text_slots[slot]).astype(bf16)
        image_total = ring_add(image_total, image_slots[0])
        text_total = lax.ppermute(text_total, "tensor", pairs)
    mod_owned = jnp.einsum("sd,szke->zdke", lifted_own.astype(f32), factor_all, precision=highest)
    lifted_terms = jnp.einsum(
        "szke,zdke->sd", factor_all, modulator.astype(f32), precision=highest
    )
    if size > 3:
        text_total, lifted_terms = tie(text_total, lifted_terms)
        text_total = text_total.astype(f32) + text_slots[0].astype(f32)
    share = dp_size // size
    owner = lax.axis_index("dp") // share
    terms = lifted_terms.reshape(dp_size, 1, seq_count, own_depth)
    terms = jnp.where(jnp.arange(size)[None, :, None, None] == owner, terms, 0.0)
    terms = lax.all_to_all(
        terms.reshape(dp_size * size, seq_count, own_depth), ("dp", "tensor"), 0, 0, tiled=True
    )
    terms = jnp.sum(terms.reshape(dp_size, size, seq_count, own_depth), axis=1)
    terms = lax.dynamic_slice_in_dim(terms, lax.axis_index("tensor") * share, share, 0)
    lifted_cols = jnp.moveaxis(terms, 0, 1).reshape(seq_count, share * own_depth)
    entry_grad = [image_total, text_total]
    for m in modalities:
        row_grad, normal = modulate_back(start_rows[m], factors[:, m, 1], entry_grad[m])
        grads[m] = grads[m] + row_grad
    columns = lifted_cols.shape[1]
    own_cond = lax.dynamic_slice_in_dim(cond_float, lax.axis_index("tensor") * columns, columns, 1)
    gate = jax.nn.sigmoid(own_cond)
    cond_grad = lifted_cols * (gate * (1.0 + own_cond * (1.0 - gate)))
    return (
        carried[0].astype(bf16),
        carried[1].astype(bf16),
        grads[0],
        grads[1],
        cond_grad,
        mod_owned[None],
        inner_owned.reshape(attention_in.shape).astype(f32),
        outer_owned[None].astype(f32),
        feed_owned[0][None].astype(f32),
        feed_owned[1][None].astype(f32),
    )


def solution(mesh):
    in_specs = (
        P("dp", "tensor", None),
        P("dp", "tensor", None),
        P("dp", None),
        P(None, None, "dp", None, "tensor"),
        P(None, None, "dp", None, "tensor"),
        P(None, None, ("tensor", "dp"), None),
        P(None, None, "dp", "tensor"),
        P(None, None, ("tensor", "dp"), None),
        P("dp", "tensor", None),
        P("dp", "tensor", None),
    )
    out_specs = (
        P("dp", "tensor", None),
        P("dp", "tensor", None),
        P("dp", "tensor", None),
        P("dp", "tensor", None),
        P("dp", "tensor"),
        P(None, None, "dp", None, "tensor"),
        P(None, None, "dp", None, "tensor"),
        P(None, None, ("tensor", "dp"), None),
        P(None, None, "dp", "tensor"),
        P(None, None, ("tensor", "dp"), None),
    )
    body = partial(shards, dp_size=mesh.shape["dp"], size=mesh.shape["tensor"])
    return jax.shard_map(body, mesh=mesh, in_specs=in_specs, out_specs=out_specs, check_vma=False)
```

```python
from functools import partial

import jax
import jax.numpy as jnp
from jax import lax
from jax.experimental import pallas as pl
from jax.experimental.pallas import tpu as pltpu
from jax.sharding import PartitionSpec as P

HD = 64

norm_eps = 1e-06
highest = lax.Precision.HIGHEST
VMEM_LIMIT = 40 * 1024 * 1024
bf16 = jnp.bfloat16
f32 = jnp.float32


def layer_norm(rows):
    middle = jnp.mean(rows, axis=-1, keepdims=True)
    centered = rows - middle
    spread = jnp.mean(centered * centered, axis=-1, keepdims=True)
    return centered * lax.rsqrt(spread + norm_eps)


def modulate(rows, shift, scale):
    return layer_norm(rows) * (1.0 + scale[:, None, :]) + shift[:, None, :]


def modulate_back(rows, scale, grad):
    middle = jnp.mean(rows, axis=-1, keepdims=True)
    centered = rows - middle
    spread = jnp.mean(centered * centered, axis=-1, keepdims=True)
    inverse = lax.rsqrt(spread + norm_eps)
    normal = centered * inverse
    wide = grad * (1.0 + scale[:, None, :])
    first = jnp.mean(wide, axis=-1, keepdims=True)
    second = jnp.mean(wide * normal, axis=-1, keepdims=True)
    return inverse * (wide - first - normal * second), normal


def gelu_parts(hidden):
    slope = 0.7978845608028654
    square = hidden * hidden
    tail = jnp.tanh(slope * hidden * (1.0 + 0.044715 * square))
    active = 0.5 * hidden * (1.0 + tail)
    back = 0.5 * (1.0 + tail) + 0.5 * hidden * (1.0 - tail * tail) * (
        slope * (1.0 + 3.0 * 0.044715 * square)
    )
    return active, back


NT = (((1,), (1,)), ((), ()))
NN = (((1,), (0,)), ((), ()))
TN = (((0,), (0,)), ((), ()))


def product(left, right, numbers):
    return lax.dot_general(left, right, numbers, preferred_element_type=f32)


def cuts(length, step):
    return [(lower, min(lower + step, length)) for lower in range(0, length, step)]


def attend_forward_kernel(packed, mixed, totals, *, step, scale):
    length, width = mixed.shape[1:]
    for head in range(width // HD):
        lane = head * HD
        keys = packed[0, :, width + lane : width + lane + HD]
        values = packed[0, :, 2 * width + lane : 2 * width + lane + HD]
        for lower, upper in cuts(length, step):
            query = packed[0, lower:upper, lane : lane + HD] * scale
            scores = product(keys, query, NT)
            largest = jnp.max(scores, axis=0, keepdims=True)
            raised = jnp.exp(scores - largest)
            denominator = jnp.sum(raised, axis=0, keepdims=True)
            probs = (raised * (1.0 / denominator)).astype(bf16)
            mixed[0, lower:upper, lane : lane + HD] = product(probs, values, TN).astype(bf16)
            totals[0, head : head + 1, lower:upper] = largest + jnp.log(denominator)


def attend_forward(packed, scale):
    seqs, length, width = packed.shape[0], packed.shape[1], packed.shape[2] // 3
    heads = width // HD
    pairs = seqs * heads * length * length
    return pl.pallas_call(
        partial(attend_forward_kernel, step=640, scale=scale),
        grid=(seqs,),
        in_specs=[pl.BlockSpec((1, length, 3 * width), lambda s: (s, 0, 0))],
        out_specs=[
            pl.BlockSpec((1, length, width), lambda s: (s, 0, 0)),
            pl.BlockSpec((1, heads, length), lambda s: (s, 0, 0)),
        ],
        out_shape=[
            jax.ShapeDtypeStruct((seqs, length, width), bf16),
            jax.ShapeDtypeStruct((seqs, heads, length), f32),
        ],
        cost_estimate=pl.CostEstimate(
            flops=pairs * HD * 16, bytes_accessed=seqs * length * width * 8, transcendentals=pairs
        ),
        compiler_params=pltpu.CompilerParams(vmem_limit_bytes=VMEM_LIMIT),
        name="attend_forward",
    )(packed)


def attend_backward_kernel(packed, grad_mixed, totals, grad, key_sum, value_sum, *, step, scale):
    length, width = grad_mixed.shape[1:]
    for head in range(width // HD):
        lane = head * HD
        keys = packed[0, :, width + lane : width + lane + HD]
        values = packed[0, :, 2 * width + lane : 2 * width + lane + HD]
        for lower, upper in cuts(length, step):
            query = packed[0, lower:upper, lane : lane + HD] * scale
            block_grad = grad_mixed[0, lower:upper, lane : lane + HD]
            probs = jnp.exp(product(keys, query, NT) - totals[0, head : head + 1, lower:upper])
            weighted = probs * product(values, block_grad, NT)
            inner = jnp.sum(weighted, axis=0, keepdims=True)
            grad_scores = (weighted - probs * inner).astype(bf16)
            grad_values = product(probs.astype(bf16), block_grad, NN)
            grad_keys = product(grad_scores, query, NN)
            grad_query = product(grad_scores, keys, TN) * scale
            grad[0, lower:upper, lane : lane + HD] = grad_query.astype(bf16)
            if lower:
                key_sum[...] += grad_keys
                value_sum[...] += grad_values
            else:
                key_sum[...] = grad_keys
                value_sum[...] = grad_values
        grad[0, :, width + lane : width + lane + HD] = key_sum[...].astype(bf16)
        grad[0, :, 2 * width + lane : 2 * width + lane + HD] = value_sum[...].astype(bf16)


def attend_backward(packed, grad_mixed, totals, scale):
    seqs, length, width = grad_mixed.shape
    heads = width // HD
    pairs = seqs * heads * length * length
    return pl.pallas_call(
        partial(attend_backward_kernel, step=640, scale=scale),
        grid=(seqs,),
        in_specs=[
            pl.BlockSpec((1, length, 3 * width), lambda s: (s, 0, 0)),
            pl.BlockSpec((1, length, width), lambda s: (s, 0, 0)),
            pl.BlockSpec((1, heads, length), lambda s: (s, 0, 0)),
        ],
        out_specs=pl.BlockSpec((1, length, 3 * width), lambda s: (s, 0, 0)),
        out_shape=jax.ShapeDtypeStruct((seqs, length, 3 * width), bf16),
        scratch_shapes=[pltpu.VMEM((length, HD), f32), pltpu.VMEM((length, HD), f32)],
        cost_estimate=pl.CostEstimate(
            flops=pairs * HD * 32, bytes_accessed=seqs * length * width * 14, transcendentals=pairs
        ),
        compiler_params=pltpu.CompilerParams(vmem_limit_bytes=VMEM_LIMIT),
        name="attend_backward",
    )(packed, grad_mixed, totals)


def weight_grad_kernel(*refs, terms):
    out = refs[-1]

    def total(pairs):
        value = None
        for (left, left_rows), (right, right_rows) in pairs:
            for seq in range(refs[left].shape[0]):
                term = product(
                    refs[left][seq, left_rows[0] : left_rows[1]],
                    refs[right][seq, right_rows[0] : right_rows[1]],
                    TN,
                )
                value = term if value is None else value + term
        return value.astype(bf16)

    for modality in range(2):

        @pl.when(pl.program_id(0) == modality)
        def _(pairs=terms[modality]):
            out[0] = total(pairs)


def rows_of(array, lower=0, upper=None):
    return (array, (lower, array.shape[1] if upper is None else upper))


def weight_grad(terms, slots=2, place=0, into=None):
    depth, width = terms[0][0][0][0].shape[2], terms[0][0][1][0].shape[2]
    tile = 768 if depth % 768 == 0 else 384 if depth % 384 == 0 else depth
    tiles = depth // tile
    operands, in_specs, found, numbered, rows = [], [], {}, [], 0
    for modality, pairs in enumerate(terms):
        numbered.append([])
        for pair in pairs:
            numbers = []
            for side, (array, window) in enumerate(pair):
                key = (id(array), side)
                if key not in found:
                    found[key] = len(operands)
                    operands.append(array)
                    both = all(
                        any(entry[side][0] is array for entry in other) for other in terms
                    )
                    if side:
                        spec = pl.BlockSpec(array.shape[:2] + (width,), lambda z, j: (0, 0, 0))
                    elif both:
                        spec = pl.BlockSpec(array.shape[:2] + (tile,), lambda z, j: (0, 0, j))
                    elif modality == 0:
                        spec = pl.BlockSpec(
                            array.shape[:2] + (tile,),
                            lambda z, j: (0, 0, jnp.where(z == 0, j, tiles - 1)),
                        )
                    else:
                        spec = pl.BlockSpec(
                            array.shape[:2] + (tile,),
                            lambda z, j: (0, 0, jnp.where(z == 1, j, 0)),
                        )
                    in_specs.append(spec)
                numbers.append((found[key], window))
            rows += array.shape[0] * (window[1] - window[0])
            numbered[-1].append(tuple(numbers))
    aliases = {}
    if into is not None:
        aliases = {len(operands): 0}
        operands.append(into)
        in_specs.append(pl.BlockSpec(memory_space=pl.ANY))
    return pl.pallas_call(
        partial(weight_grad_kernel, terms=numbered),
        grid=(2, tiles),
        in_specs=in_specs,
        out_specs=pl.BlockSpec((1, tile, width), lambda z, j: (z + place, j, 0)),
        out_shape=jax.ShapeDtypeStruct((slots, depth, width), bf16),
        input_output_aliases=aliases,
        cost_estimate=pl.CostEstimate(
            flops=2 * rows * depth * width,
            bytes_accessed=2 * (rows * (depth + width) + 2 * depth * width),
            transcendentals=0,
        ),
        compiler_params=pltpu.CompilerParams(vmem_limit_bytes=VMEM_LIMIT),
        name="weight_grad",
    )(*operands)


def entry_block_kernel(rows, shift, scale, weight, entry, packed):
    value = layer_norm(rows[0].astype(f32)) * (1.0 + scale[0]) + shift[0]
    value = value.astype(bf16)
    entry[0] = value
    packed[0] = product(value, weight[0], NN).astype(bf16)


def entry_block(rows, count, shift, scale, weight, modality):
    seqs, depth = rows.shape[0], rows.shape[2]
    width = weight.shape[2]
    factor = pl.BlockSpec((1, 1, depth), lambda s: (s, 0, 0))
    return pl.pallas_call(
        entry_block_kernel,
        grid=(seqs,),
        in_specs=[
            pl.BlockSpec((1, count, depth), lambda s: (s, 0, 0)),
            factor,
            factor,
            pl.BlockSpec((1, depth, width), lambda s: (modality, 0, 0)),
        ],
        out_specs=[
            pl.BlockSpec((1, count, depth), lambda s: (s, 0, 0)),
            pl.BlockSpec((1, count, width), lambda s: (s, 0, 0)),
        ],
        out_shape=[
            jax.ShapeDtypeStruct((seqs, count, depth), bf16),
            jax.ShapeDtypeStruct((seqs, count, width), bf16),
        ],
        cost_estimate=pl.CostEstimate(
            flops=2 * seqs * count * depth * width,
            bytes_accessed=2 * depth * width + 2 * seqs * count * (2 * depth + width),
            transcendentals=seqs * count,
        ),
        compiler_params=pltpu.CompilerParams(vmem_limit_bytes=VMEM_LIMIT),
        name="entry_block",
    )(rows, shift[:, None, :], scale[:, None, :], weight)


def entry_back_kernel(grads, weight, rows, terms, sums):
    value = product(grads[0], weight[0], NT)
    terms[0] = value.astype(bf16)
    normal = layer_norm(rows[0].astype(f32))
    sums[0, 0:1] = jnp.sum(value, axis=0, keepdims=True)
    sums[0, 1:2] = jnp.sum(value * normal, axis=0, keepdims=True)


def entry_back(grads, place, count, weight, rows, modality):
    seqs, depth = rows.shape[0], rows.shape[2]
    width = weight.shape[2]
    return pl.pallas_call(
        entry_back_kernel,
        grid=(seqs,),
        in_specs=[
            pl.BlockSpec((1, count, width), lambda s: (s, place, 0)),
            pl.BlockSpec((1, depth, width), lambda s: (modality, 0, 0)),
            pl.BlockSpec((1, count, depth), lambda s: (s, 0, 0)),
        ],
        out_specs=[
            pl.BlockSpec((1, count, depth), lambda s: (s, 0, 0)),
            pl.BlockSpec((1, 2, depth), lambda s: (s, 0, 0)),
        ],
        out_shape=[
            jax.ShapeDtypeStruct((seqs, count, depth), bf16),
            jax.ShapeDtypeStruct((seqs, 2, depth), f32),
        ],
        cost_estimate=pl.CostEstimate(
            flops=2 * seqs * count * depth * width,
            bytes_accessed=2 * depth * width + 2 * seqs * count * (2 * depth + width),
            transcendentals=seqs * count,
        ),
        compiler_params=pltpu.CompilerParams(vmem_limit_bytes=VMEM_LIMIT),
        name="entry_back",
    )(grads, weight, rows)


def feed_block_kernel(rows, grads, up, down, active, hidden_grad, entry, feed, entry_sum, feed_sum):
    place, last = pl.program_id(1), pl.num_programs(1) - 1
    upper, lower = up[0], down[0]
    hidden = product(rows[0], upper, NN)
    block_active, back = gelu_parts(hidden)
    block_active = block_active.astype(bf16)
    active[0] = block_active
    block_grad = (product(grads[0], lower, NT) * back).astype(bf16)
    hidden_grad[0] = block_grad
    entry_term = product(block_grad, upper, NT)
    feed_term = product(block_active, lower, NN)

    @pl.when(place == 0)
    def _():
        entry_sum[...] = entry_term
        feed_sum[...] = feed_term

    @pl.when(place > 0)
    def _():
        entry_sum[...] += entry_term
        feed_sum[...] += feed_term

    @pl.when(place == last)
    def _():
        entry[0] = entry_sum[...].astype(bf16)
        feed[0] = feed_sum[...].astype(bf16)


def feed_block(rows, grads, up_planes, down_planes, modality):
    (up, up_first), (down, down_first) = up_planes, down_planes
    seqs, count, depth = rows.shape
    width = up.shape[2]
    tile = next(step for step in (1536, 768, 512, 384, 256, 128, width) if width % step == 0)
    whole = pl.BlockSpec((1, count, depth), lambda s, f: (s, 0, 0))
    part = pl.BlockSpec((1, count, tile), lambda s, f: (s, 0, f))
    shapes = [jax.ShapeDtypeStruct((seqs, count, size), bf16) for size in (width, width, depth, depth)]
    return pl.pallas_call(
        feed_block_kernel,
        grid=(seqs, width // tile),
        in_specs=[
            whole,
            whole,
            pl.BlockSpec((1, depth, tile), lambda s, f: (up_first + modality, 0, f)),
            pl.BlockSpec((1, tile, depth), lambda s, f: (down_first + modality, f, 0)),
        ],
        out_specs=[part, part, whole, whole],
        out_shape=shapes,
        scratch_shapes=[pltpu.VMEM((count, depth), f32), pltpu.VMEM((count, depth), f32)],
        cost_estimate=pl.CostEstimate(
            flops=8 * seqs * count * depth * width,
            bytes_accessed=4 * depth * width + 8 * seqs * count * (depth + width),
            transcendentals=seqs * count * width,
        ),
        compiler_params=pltpu.CompilerParams(vmem_limit_bytes=VMEM_LIMIT),
        name="feed_block",
    )(rows, grads, up, down)


def ring_pairs(size):
    order = list(range(0, size, 2)) + list(range(size - 1, 0, -2)) if size != 4 else [0, 1, 3, 2]
    if size == 1:
        order = [0]
    return [(order[place], order[(place + 1) % size]) for place in range(size)]


def ring_gather(block, size):
    pairs = ring_pairs(size)
    blocks = [block]
    for step in range(size - 1):
        blocks.append(lax.ppermute(blocks[-1], "tensor", pairs))
    return blocks


def tie(value, other):
    return lax.optimization_barrier((value, other))


def ring_add(total, part):
    pairs = ring_pairs(lax.axis_size("tensor"))
    return lax.ppermute(total, "tensor", pairs).astype(f32) + part.astype(f32)


def ring_scatter_pair(image, text, size, fence, at):
    pairs = ring_pairs(size)
    image_total, text_total = image[1].astype(bf16), text[1].astype(bf16)
    for step, slot in enumerate(list(range(2, size)) + [0]):
        if step == at:
            image_total, text_total = tie(image_total, text_total)
        image_next = lax.ppermute(image_total, "tensor", pairs).astype(f32)
        text_next = lax.ppermute(text_total, "tensor", pairs)
        if step == at:
            text_next, *fence = lax.optimization_barrier((text_next, *fence))
        image_total = image_next + image[slot].astype(f32)
        text_total = text_next.astype(f32) + text[slot].astype(f32)
        if slot:
            image_total, text_total = image_total.astype(bf16), text_total.astype(bf16)
    return [image_total, text_total], fence


def ring_scatter(parts, size):
    pairs = ring_pairs(size)
    if size == 1:
        return parts[0].astype(f32)
    total = parts[1].astype(bf16)
    for slot in list(range(2, size)) + [0]:
        total = lax.ppermute(total, "tensor", pairs).astype(f32) + parts[slot].astype(f32)
        if slot:
            total = total.astype(bf16)
    return total


def split_rows(blocks, count):
    return [
        jnp.concatenate([block[:, :count] for block in blocks], axis=1),
        jnp.concatenate([block[:, count:] for block in blocks], axis=1),
    ]


def join_slots(image, text, size):
    image_rows = image.shape[1] // size
    text_rows = text.shape[1] // size
    return [
        jnp.concatenate(
            [
                image[:, slot * image_rows : (slot + 1) * image_rows],
                text[:, slot * text_rows : (slot + 1) * text_rows],
            ],
            axis=1,
        )
        for slot in range(size)
    ]


def cut_rows(value, size):
    count = value.shape[1] // size
    return [value[:, slot * count : (slot + 1) * count] for slot in range(size)]


def gather_weight(weight):
    return lax.all_gather(weight, "dp", axis=1, tiled=True)


def scatter_weight(grad):
    return lax.psum_scatter(grad, "dp", scatter_dimension=1, tiled=True)


def sum_to_columns(value, axis_name, size, axis):
    shape = value.shape
    cut = value.reshape(shape[:axis] + (size, shape[axis] // size) + shape[axis + 1 :])
    cut = jnp.moveaxis(cut, axis, 0)
    return jnp.sum(lax.all_to_all(cut, axis_name, 0, 0, tiled=True), axis=0)


def shards(
    image_rows,
    text_rows,
    conditioning,
    modulator,
    attention_in,
    attention_out,
    up_weight,
    down_weight,
    image_cotangent,
    text_cotangent,
    dp_size,
    size,
):
    scale = HD ** (-0.5)
    modalities = range(2)
    modulator = modulator[0]
    seq_count, image_own = image_rows.shape[:2]
    length_image = image_own * size

    cond_float = conditioning.astype(f32)
    lifted = jax.nn.silu(cond_float).astype(bf16)

    inner_full = gather_weight(attention_in[0].reshape(2, attention_in.shape[2], -1))
    pairs = ring_pairs(size)
    x_blocks = [jnp.concatenate([image_rows, text_rows], axis=1)]
    x_blocks.append(lax.ppermute(x_blocks[0], "tensor", pairs))

    lifted_all = lax.all_gather(lifted, "dp", axis=0, tiled=True)
    outer_local, lifted_all = tie(attention_out[0], lifted_all)
    outer_full = gather_weight(outer_local)
    own_depth = modulator.shape[1]
    lifted_own = lax.dynamic_slice_in_dim(
        lifted_all, lax.axis_index("dp") * own_depth, own_depth, 1
    )
    factor_terms = jnp.einsum("sd,zdke->szke", lifted_own, modulator, preferred_element_type=f32)
    factor_cols = sum_to_columns(factor_terms, "dp", dp_size, 0)
    x_blocks[1], factor_cols = tie(x_blocks[1], factor_cols)
    x_blocks.append(lax.ppermute(x_blocks[1], "tensor", pairs))
    factor_parts = lax.all_to_all(
        jnp.broadcast_to(factor_cols[None], (size,) + factor_cols.shape), "tensor", 0, 0, tiled=True
    )
    x_blocks[2], factor_parts = tie(x_blocks[2], factor_parts)
    factors = jnp.concatenate([factor_parts[place] for place in range(size)], axis=3)
    for step in range(3, size):
        x_blocks.append(lax.ppermute(x_blocks[-1], "tensor", pairs))
    x_blocks = x_blocks[:size]
    cotangent, up_local, down_local, x_blocks[-1] = lax.optimization_barrier(
        (
            jnp.concatenate([image_cotangent, text_cotangent], axis=1),
            up_weight[0],
            down_weight[0],
            x_blocks[-1],
        )
    )
    if up_local.shape == down_local.shape:
        weights = gather_weight(jnp.concatenate([up_local, down_local], axis=0))
        up_full, down_full = (weights, 0), (weights, 2)
    else:
        up_full, down_full = (gather_weight(up_local), 0), (gather_weight(down_local), 0)
    cot_blocks = [cotangent, lax.ppermute(cotangent, "tensor", ring_pairs(size))]
    parts = [
        entry_block(block, image_own, factors[:, 0, 0], factors[:, 0, 1], inner_full, 0)
        for block in x_blocks
    ]
    text_all = jnp.concatenate([block[:, image_own:] for block in x_blocks], axis=1)
    parts.append(
        entry_block(text_all, text_all.shape[1], factors[:, 1, 0], factors[:, 1, 1], inner_full, 1)
    )
    packed = jnp.concatenate([part[1] for part in parts], axis=1)
    cot_blocks[1], packed = tie(cot_blocks[1], packed)
    cot_blocks.append(lax.ppermute(cot_blocks[1], "tensor", ring_pairs(size)))
    mixed, log_totals = attend_forward(packed, scale)
    cot_blocks[2], mixed = tie(cot_blocks[2], mixed)
    for step in range(3, size):
        cot_blocks.append(lax.ppermute(cot_blocks[-1], "tensor", ring_pairs(size)))
    cot_blocks = cot_blocks[:size]
    pieces = [mixed[:, :length_image], mixed[:, length_image:]]
    outer_terms = [
        jnp.einsum("kut,tx->kux", pieces[m], outer_full[m], preferred_element_type=f32)
        for m in modalities
    ]
    outer_slots = join_slots(outer_terms[0], outer_terms[1], size)
    attn_total = ring_add(outer_slots[1].astype(bf16), outer_slots[2 % size])
    attn_total, cot_blocks[-1] = tie(attn_total, cot_blocks[-1])
    for slot in list(range(3, size)) + [0] * (size > 2):
        attn_total = ring_add(attn_total.astype(bf16), outer_slots[slot])
    attn_branch = attn_total
    attn_branch = [attn_branch[:, :image_own], attn_branch[:, image_own:]]
    start_rows = [image_rows.astype(f32), text_rows.astype(f32)]
    middle_rows = [
        start_rows[m] + factors[:, m, 2][:, None, :] * attn_branch[m] for m in modalities
    ]
    feed_entries = [
        modulate(middle_rows[m], factors[:, m, 3], factors[:, m, 4]).astype(bf16)
        for m in modalities
    ]
    if up_weight.shape == down_weight.shape:
        weights, feed_entries[0] = tie(weights, feed_entries[0])
        up_full, down_full = (weights, 0), (weights, 2)
    text_entries = jnp.concatenate(ring_gather(feed_entries[1], size), axis=1)
    image_entries = [feed_entries[0], lax.ppermute(feed_entries[0], "tensor", pairs)]
    text_cot = jnp.concatenate([block[:, image_own:] for block in cot_blocks], axis=1)
    text_send = (factors[:, 1, 5][:, None, :] * text_cot.astype(f32)).astype(bf16)
    image_sends = [
        (factors[:, 0, 5][:, None, :] * block[:, :image_own].astype(f32)).astype(bf16)
        for block in cot_blocks
    ]
    image_feeds = []
    for slot in range(size):
        feed = list(feed_block(image_entries[slot], image_sends[slot], up_full, down_full, 0))
        if slot + 2 < size:
            image_entries[slot + 1], feed[2] = tie(image_entries[slot + 1], feed[2])
            image_entries.append(lax.ppermute(image_entries[slot + 1], "tensor", pairs))
        image_feeds.append(feed)
    text_feed = feed_block(text_entries, text_send, up_full, down_full, 1)
    entry_grad, (text_active, text_hidden) = ring_scatter_pair(
        [feed[2] for feed in image_feeds],
        cut_rows(text_feed[2], size),
        size,
        [text_feed[0], text_feed[1]],
        min(1, size - 2),
    )
    up_terms = [
        [
            (rows_of(image_entries[slot]), rows_of(image_feeds[slot][1]))
            for slot in range(size)
        ],
        [(rows_of(text_entries), rows_of(text_hidden))],
    ]
    down_terms = [
        [
            (rows_of(image_feeds[slot][0]), rows_of(image_sends[slot]))
            for slot in range(size)
        ],
        [(rows_of(text_active), rows_of(text_send))],
    ]
    if up_weight.shape == down_weight.shape:
        grad_feed = weight_grad(down_terms, 4, 2)
        grad_feed = weight_grad(up_terms, 4, 0, grad_feed)
        feed_owned = [scatter_weight(grad_feed)]
    else:
        feed_owned = [
            scatter_weight(weight_grad(up_terms)),
            scatter_weight(weight_grad(down_terms)),
        ]

    grads = [image_cotangent.astype(f32), text_cotangent.astype(f32)]
    cots = list(grads)
    shift_two = []
    scale_two = []
    gate_one = []
    sends = []
    for m in modalities:
        row_grad, normal = modulate_back(middle_rows[m], factors[:, m, 4], entry_grad[m])
        grads[m] = grads[m] + row_grad
        shift_two.append(jnp.sum(entry_grad[m], axis=1))
        scale_two.append(jnp.sum(entry_grad[m] * normal, axis=1))
        gate_one.append(jnp.sum(grads[m] * attn_branch[m], axis=1))
        sends.append((factors[:, m, 2][:, None, :] * grads[m]).astype(bf16))
    attn_blocks = ring_gather(jnp.concatenate(sends, axis=1), size)
    attn_grad = split_rows(attn_blocks, image_own)
    feed_slots = [
        jnp.concatenate([image_feeds[slot][3], part], axis=1)
        for slot, part in enumerate(cut_rows(text_feed[3], size))
    ]
    feed_slots[1], last_block = tie(feed_slots[1], attn_blocks[-1])
    late_grad = split_rows(attn_blocks[:-1] + [last_block], image_own)
    grad_mixed = jnp.concatenate(
        [
            jnp.einsum("hom,rm->hor", attn_grad[m], outer_full[m], preferred_element_type=f32)
            for m in modalities
        ],
        axis=1,
    ).astype(bf16)
    feed_total = ring_add(feed_slots[1], feed_slots[2 % size])
    if size > 2:
        feed_total = feed_total.astype(bf16)
    feed_total, grad_mixed = tie(feed_total, grad_mixed)
    grad_outer, feed_owned = tie(weight_grad(
            [
                [(rows_of(mixed, 0, length_image), rows_of(late_grad[0]))],
                [(rows_of(mixed, length_image), rows_of(late_grad[1]))],
            ]
        ), feed_owned)
    outer_owned = scatter_weight(grad_outer)
    grad_packed = attend_backward(packed, grad_mixed, log_totals, scale)
    feed_total = ring_add(feed_total, feed_slots[3 % size])
    if size > 3:
        feed_total = feed_total.astype(bf16)
    feed_total, grad_packed = tie(feed_total, grad_packed)
    grad_inner = weight_grad(
        [
            [
                (
                    rows_of(parts[slot][0]),
                    rows_of(grad_packed, slot * image_own, (slot + 1) * image_own),
                )
                for slot in range(size)
            ],
            [(rows_of(parts[size][0]), rows_of(grad_packed, length_image))],
        ]
    )
    grad_inner, outer_owned, late_packed = lax.optimization_barrier(
        (grad_inner, outer_owned, grad_packed)
    )
    inner_owned = scatter_weight(grad_inner)
    image_backs = [
        entry_back(late_packed, slot, image_own, inner_full, x_blocks[slot], 0)
        for slot in range(size)
    ]
    text_back = entry_back(
        late_packed[:, length_image:], 0, text_all.shape[1], inner_full, text_all, 1
    )
    entry_sums = [sum(back[1] for back in image_backs), text_back[1]]
    image_slots = [back[0] for back in image_backs]
    text_slots = cut_rows(text_back[0], size)
    for slot in range(4, size):
        feed_total = ring_add(feed_total.astype(bf16), feed_slots[slot])
    if size > 3:
        feed_total = lax.ppermute(feed_total.astype(bf16), "tensor", pairs)
    image_total, text_total = tie(image_slots[1], text_slots[1].astype(bf16))
    image_next = lax.ppermute(image_total, "tensor", pairs)
    text_next, entry_sums[0], entry_sums[1], feed_slots[0] = lax.optimization_barrier(
        (lax.ppermute(text_total, "tensor", pairs), entry_sums[0], entry_sums[1], feed_slots[0])
    )
    if size > 3:
        feed_total = feed_total.astype(f32) + feed_slots[0].astype(f32)
    image_total = image_next.astype(f32) + image_slots[2 % size].astype(f32)
    text_total = text_next.astype(f32) + text_slots[2 % size].astype(f32)
    feed_branch = feed_total
    feed_branch = [feed_branch[:, :image_own], feed_branch[:, image_own:]]
    carried = [
        middle_rows[m] + factors[:, m, 5][:, None, :] * feed_branch[m] for m in modalities
    ]
    gate_two = [jnp.sum(cots[m] * feed_branch[m], axis=1) for m in modalities]
    if len(feed_owned) == 1:
        feed_owned = [feed_owned[0][:2], feed_owned[0][2:]]
    factor_terms = jnp.stack(
        [
            term
            for m in modalities
            for term in (
                entry_sums[m][:, 0],
                entry_sums[m][:, 1],
                gate_one[m],
                shift_two[m],
                scale_two[m],
                gate_two[m],
            )
        ],
        axis=1,
    ).reshape(seq_count, 2, 6, -1)
    factor_sums = sum_to_columns(factor_terms, "tensor", size, 3)
    if size > 2:
        image_total, text_total, factor_sums = lax.optimization_barrier(
            (image_total.astype(bf16), text_total.astype(bf16), factor_sums)
        )
        image_total = ring_add(image_total, image_slots[3 % size])
        text_total = ring_add(text_total, text_slots[3 % size])
    factor_all = lax.all_gather(factor_sums, "dp", axis=0, tiled=True)
    factor_all, *feed_owned = lax.optimization_barrier((factor_all, *feed_owned))
    if size > 3:
        image_total, text_total, factor_all = lax.optimization_barrier(
            (image_total.astype(bf16), text_total.astype(bf16), factor_all)
        )
        for slot in range(4, size):
            image_total = ring_add(image_total, image_slots[slot]).astype(bf16)
            text_total = ring_add(text_total, text_slots[slot]).astype(bf16)
        image_total = ring_add(image_total, image_slots[0])
        text_total = lax.ppermute(text_total, "tensor", pairs)
    mod_owned = jnp.einsum("sd,szke->zdke", lifted_own.astype(f32), factor_all, precision=highest)
    lifted_terms = jnp.einsum(
        "szke,zdke->sd", factor_all, modulator.astype(f32), precision=highest
    )
    if size > 3:
        text_total, lifted_terms = tie(text_total, lifted_terms)
        text_total = text_total.astype(f32) + text_slots[0].astype(f32)
    share = dp_size // size
    owner = lax.axis_index("dp") // share
    terms = lifted_terms.reshape(dp_size, 1, seq_count, own_depth)
    terms = jnp.where(jnp.arange(size)[None, :, None, None] == owner, terms, 0.0)
    terms = lax.all_to_all(
        terms.reshape(dp_size * size, seq_count, own_depth), ("dp", "tensor"), 0, 0, tiled=True
    )
    terms = jnp.sum(terms.reshape(dp_size, size, seq_count, own_depth), axis=1)
    terms = lax.dynamic_slice_in_dim(terms, lax.axis_index("tensor") * share, share, 0)
    lifted_cols = jnp.moveaxis(terms, 0, 1).reshape(seq_count, share * own_depth)
    entry_grad = [image_total, text_total]
    for m in modalities:
        row_grad, normal = modulate_back(start_rows[m], factors[:, m, 1], entry_grad[m])
        grads[m] = grads[m] + row_grad
    columns = lifted_cols.shape[1]
    own_cond = lax.dynamic_slice_in_dim(cond_float, lax.axis_index("tensor") * columns, columns, 1)
    gate = jax.nn.sigmoid(own_cond)
    cond_grad = lifted_cols * (gate * (1.0 + own_cond * (1.0 - gate)))
    return (
        carried[0].astype(bf16),
        carried[1].astype(bf16),
        grads[0],
        grads[1],
        cond_grad,
        mod_owned[None],
        inner_owned.reshape(attention_in.shape).astype(f32),
        outer_owned[None].astype(f32),
        feed_owned[0][None].astype(f32),
        feed_owned[1][None].astype(f32),
    )


def solution(mesh):
    in_specs = (
        P("dp", "tensor", None),
        P("dp", "tensor", None),
        P("dp", None),
        P(None, None, "dp", None, "tensor"),
        P(None, None, "dp", None, "tensor"),
        P(None, None, ("tensor", "dp"), None),
        P(None, None, "dp", "tensor"),
        P(None, None, ("tensor", "dp"), None),
        P("dp", "tensor", None),
        P("dp", "tensor", None),
    )
    out_specs = (
        P("dp", "tensor", None),
        P("dp", "tensor", None),
        P("dp", "tensor", None),
        P("dp", "tensor", None),
        P("dp", "tensor"),
        P(None, None, "dp", None, "tensor"),
        P(None, None, "dp", None, "tensor"),
        P(None, None, ("tensor", "dp"), None),
        P(None, None, "dp", "tensor"),
        P(None, None, ("tensor", "dp"), None),
    )
    body = partial(shards, dp_size=mesh.shape["dp"], size=mesh.shape["tensor"])
    return jax.shard_map(body, mesh=mesh, in_specs=in_specs, out_specs=out_specs, check_vma=False)
```
